256 devices in a mesh: tm: 128 (over y, x, z), tok: 2 (over core).
Axes of the slice: x: 4, y: 4, z: 8, core: 2. Of those that a mesh axis runs over, the one named last changes fastest.
Arguments:
- patches: bfloat16 [128, 12, 12, 12, 512], P('tm', 'tok'), may hold values from -6 to 6
- patch_weight: bfloat16 [512, 512], replicated, may hold values from -0.25 to 0.25
- conv_taps: bfloat16 [27, 512], replicated, may hold values from -2 to 2
- gain_space: bfloat16 [512], replicated, may hold values from 0.099609375 to 1.8984375
- qkv_space: bfloat16 [512, 1536], replicated, may hold values from -0.25 to 0.25
- out_space: bfloat16 [512, 512], replicated, may hold values from -0.25 to 0.25
- gain_time: bfloat16 [512], replicated, may hold values from 0.099609375 to 1.8984375
- qkv_time: bfloat16 [512, 1536], replicated, may hold values from -0.25 to 0.25
- out_time: bfloat16 [512, 512], replicated, may hold values from -0.25 to 0.25
Outputs:
- block_out: bfloat16 [128, 12, 12, 12, 512], P('tm', 'tok')
The draws below stay inside these ranges and needn't reach their ends.
All inputs are finite; a program needn't handle non-finite values.
Results may differ from the reference program's by a relative error of at most 0.018.
Values may be sent and summed in bfloat16 or wider, within the bound.
A program may use at most 128 MiB of HBM per device.

```python
import jax
import jax.numpy as jnp
from jax import lax

D = 512
H = 8
PATCH = 512
GRID = 12
WIN = 4
FRAMES = 128


def block_scale(key, extent, cuts, low, largest):
    def one(dim, shards_of):
        draws = jax.random.uniform(jax.random.fold_in(jax.random.fold_in(key, 6), dim), (shards_of,), jnp.float32, low / len(cuts), largest / len(cuts))
        return jnp.repeat(jnp.exp(draws), extent[dim] // shards_of).reshape((-1,) + (1,) * (len(extent) - dim - 1))

    level = one(*cuts[0])
    for cut in cuts[1:]:
        level = level * one(*cut)
    return level


def noise(rng, dims, spread, reach, split=(), kind=jnp.bfloat16):
    level = block_scale(rng, dims, split, -0.22, 0.18) if split else 1.0
    values = jax.random.normal(rng, dims, jnp.float32) * spread * level
    return jnp.minimum(jnp.maximum(values, -reach), reach).astype(kind)


def setup_inputs(seed: int = 0) -> dict:
    key_of = jax.random.split(jax.random.key(seed), 10)
    return {
        "patches": noise(key_of[0], (FRAMES, GRID, GRID, GRID, PATCH), 1.0, 6.0, ((0, 128), (1, 2))),
        "patch_weight": noise(key_of[1], (PATCH, D), PATCH ** -0.5, 0.25),
        "conv_taps": noise(key_of[2], (27, D), 9 ** -0.5, 2.0),
        "gain_space": jnp.clip(1.0 + 0.18 * jax.random.normal(key_of[3], (D,), jnp.float32), 0.099609375, 1.8984375).astype(jnp.bfloat16),
        "qkv_space": noise(key_of[4], (D, 3 * D), D ** -0.5, 0.25),
        "out_space": noise(key_of[5], (D, D), D ** -0.5, 0.25),
        "gain_time": jnp.clip(1.0 + 0.18 * jax.random.normal(key_of[6], (D,), jnp.float32), 0.099609375, 1.8984375).astype(jnp.bfloat16),
        "qkv_time": noise(key_of[7], (D, 3 * D), D ** -0.5, 0.25),
        "out_time": noise(key_of[8], (D, D), D ** -0.5, 0.25),
    }


def rms_scale(values, gain):
    mean_sq = lax.optimization_barrier(jnp.mean(values * values, axis=-1, keepdims=True))
    return values * lax.rsqrt(mean_sq + 1e-06) * gain.astype(jnp.float32)

def attend(query, keys, values):
    rows, cols = query.shape
    head_size = D // H
    count = cols // head_size
    scale = head_size ** (-0.5)
    q_heads = query.reshape(rows, count, head_size).transpose(1, 0, 2)
    k_heads = keys.reshape(-1, count, head_size).transpose(1, 0, 2)
    v_heads = values.reshape(-1, count, head_size).transpose(1, 0, 2)

    def one_head(parts):
        q_one, k_one, v_one = parts
        scores = jnp.dot(q_one, k_one.T, preferred_element_type=jnp.float32) * scale
        expo = jnp.exp(scores)
        probs = expo.astype(jnp.bfloat16)
        mixed = jnp.dot(probs, v_one, preferred_element_type=jnp.float32)
        return (mixed / lax.optimization_barrier(jnp.sum(expo, axis=-1, keepdims=True))).astype(jnp.bfloat16)
    result = lax.map(one_head, (q_heads, k_heads, v_heads))
    return result.transpose(1, 0, 2).reshape(rows, cols)

def tempo(query, keys, values, valid):
    tokens, width = query.shape
    head_size = width // H
    scale = head_size ** (-0.5)
    q_heads = query.reshape(tokens, H, head_size).astype(jnp.float32)
    k_heads = keys.reshape(-1, tokens, H, head_size).astype(jnp.float32)
    v_heads = values.reshape(-1, tokens, H, head_size).astype(jnp.float32)
    scores = jnp.einsum('nhd,wnhd->nhw', q_heads, k_heads) * scale
    expo = jnp.where(valid, jnp.exp(scores), 0.0)
    probs = expo.astype(jnp.bfloat16).astype(jnp.float32)
    mixed = jnp.einsum('nhw,wnhd->nhd', probs, v_heads)
    mixed = mixed / lax.optimization_barrier(jnp.sum(expo, axis=-1))[..., None]
    return mixed.astype(jnp.bfloat16).reshape(tokens, width)

def reference(patches, patch_weight, conv_taps, gain_space, qkv_space, out_space, gain_time, qkv_time, out_time):
    tokens = GRID * GRID * GRID

    def frame_step(carry, inputs):
        k_window, v_window = carry
        frame, index = inputs
        embed = jnp.dot(frame.reshape(tokens, PATCH), patch_weight, preferred_element_type=jnp.float32).astype(jnp.bfloat16)
        cube = embed.reshape(GRID, GRID, GRID, D)
        padded = jnp.pad(cube, ((1, 1), (1, 1), (1, 1), (0, 0)))
        conv = jnp.zeros((GRID, GRID, GRID, D), jnp.float32)
        for dz in range(3):
            for dy in range(3):
                for dx in range(3):
                    tap = conv_taps[9 * dz + 3 * dy + dx].astype(jnp.float32)
                    conv = conv + tap * padded[dz:dz + GRID, dy:dy + GRID, dx:dx + GRID].astype(jnp.float32)
        stream = (cube.astype(jnp.float32) + conv).astype(jnp.bfloat16).reshape(tokens, D)
        normed = rms_scale(stream.astype(jnp.float32), gain_space).astype(jnp.bfloat16)
        proj = jnp.dot(normed, qkv_space, preferred_element_type=jnp.float32).astype(jnp.bfloat16)
        spatial = attend(proj[:, :D], proj[:, D:2 * D], proj[:, 2 * D:])
        stream2 = (stream.astype(jnp.float32) + jnp.dot(spatial, out_space, preferred_element_type=jnp.float32)).astype(jnp.bfloat16)
        normed2 = rms_scale(stream2.astype(jnp.float32), gain_time).astype(jnp.bfloat16)
        proj2 = jnp.dot(normed2, qkv_time, preferred_element_type=jnp.float32).astype(jnp.bfloat16)
        query2 = proj2[:, :D]
        keys_all = jnp.concatenate([k_window, proj2[None, :, D:2 * D]], axis=0)
        values_all = jnp.concatenate([v_window, proj2[None, :, 2 * D:]], axis=0)
        valid = index - WIN + jnp.arange(WIN + 1, dtype=jnp.int32) >= 0
        temporal = tempo(query2, keys_all, values_all, valid)
        output = (stream2.astype(jnp.float32) + jnp.dot(temporal, out_time, preferred_element_type=jnp.float32)).astype(jnp.bfloat16)
        return ((keys_all[1:], values_all[1:]), output.reshape(GRID, GRID, GRID, D))
    start = (jnp.zeros((WIN, tokens, D), jnp.bfloat16), jnp.zeros((WIN, tokens, D), jnp.bfloat16))
    frame_ids = jnp.arange(FRAMES, dtype=jnp.int32)
    carry_end, outputs = lax.scan(frame_step, start, (patches, frame_ids))
    return outputs
```

```python
import jax
import jax.numpy as jnp
from jax import lax
from jax.sharding import PartitionSpec as P

D = 512
H = 8
WIN = 4


def extended(block, sides, width):
    for axis, dim in sides:
        count = lax.axis_size(axis)
        forward = [(i, i + 1) for i in range(count - 1)]
        backward = [(target, source) for source, target in forward]
        low = lax.ppermute(
            lax.slice_in_dim(block, block.shape[dim] - width, None, axis=dim), axis, forward
        )
        high = lax.ppermute(lax.slice_in_dim(block, 0, width, axis=dim), axis, backward)
        block = jnp.concatenate([low, block, high], axis=dim)
    return block


def from_behind(value, axis, steps):
    count = lax.axis_size(axis)
    leading, last = (max(0, -steps), min(count, count - steps))
    return lax.ppermute(value, axis, [(source, source + steps) for source in range(leading, last)])


def rms_scale(values, gain):
    mean_sq = jnp.mean(values * values, axis=-1, keepdims=True)
    return values * lax.rsqrt(mean_sq + 1e-06) * gain.astype(jnp.float32)


def split_heads(block, count, head_size):
    return block.reshape(block.shape[0], count, head_size).transpose(1, 0, 2)


def attend(query, keys, values):
    rows, cols = query.shape
    head_size = D // H
    count = cols // head_size
    scale = head_size ** (-0.5)

    def one_head(parts):
        q_one, k_one, v_one = parts
        scores = jnp.dot(q_one, k_one.T, preferred_element_type=jnp.float32) * scale
        expo = jnp.exp(scores)
        mixed = jnp.dot(expo.astype(jnp.bfloat16), v_one, preferred_element_type=jnp.float32)
        return (mixed / jnp.sum(expo, axis=-1, keepdims=True)).astype(jnp.bfloat16)

    parts = (
        split_heads(query, count, head_size),
        split_heads(keys, count, head_size),
        split_heads(values, count, head_size),
    )
    result = lax.map(one_head, parts)
    return result.transpose(1, 0, 2).reshape(rows, cols)


def tempo(query, keys, values, valid):
    tokens, width = query.shape
    head_size = width // H
    scale = head_size ** (-0.5)
    q_heads = query.reshape(tokens, H, head_size)
    k_heads = keys.reshape(-1, tokens, H, head_size)
    v_heads = values.reshape(-1, tokens, H, head_size)
    scores = (
        jnp.einsum("nhd,wnhd->nhw", q_heads, k_heads, preferred_element_type=jnp.float32) * scale
    )
    expo = jnp.where(valid, jnp.exp(scores), 0.0)
    mixed = jnp.einsum(
        "nhw,wnhd->nhd", expo.astype(jnp.bfloat16), v_heads, preferred_element_type=jnp.float32
    )
    mixed = mixed / jnp.sum(expo, axis=-1)[..., None]
    return mixed.astype(jnp.bfloat16).reshape(tokens, width)


def local(
    patches,
    patch_weight,
    conv_taps,
    gain_space,
    qkv_space,
    out_space,
    gain_time,
    qkv_time,
    out_time,
):
    frames, zdev, grid, _, patch = patches.shape
    width = patch_weight.shape[1]
    tokens = zdev * grid * grid
    embed = jnp.dot(
        patches.reshape(-1, patch), patch_weight, preferred_element_type=jnp.float32
    ).astype(jnp.bfloat16)
    embed = embed.reshape(frames, zdev, grid, grid, width)
    padded = extended(embed, (("tok", 1),), 1)
    padded = jnp.pad(padded, ((0, 0), (0, 0), (1, 1), (1, 1), (0, 0)))
    conv = jnp.zeros((frames, zdev, grid, grid, width), jnp.float32)
    for dz in range(3):
        for dy in range(3):
            for dx in range(3):
                tap = conv_taps[9 * dz + 3 * dy + dx].astype(jnp.float32)
                conv = conv + tap * padded[
                    :, dz : dz + zdev, dy : dy + grid, dx : dx + grid
                ].astype(jnp.float32)
    stream = (embed.astype(jnp.float32) + conv).astype(jnp.bfloat16).reshape(frames, tokens, width)
    normed = rms_scale(stream.astype(jnp.float32), gain_space).astype(jnp.bfloat16)
    proj = jnp.dot(normed.reshape(-1, width), qkv_space, preferred_element_type=jnp.float32).astype(
        jnp.bfloat16
    )
    proj = proj.reshape(frames, tokens, 3 * width)
    query = proj[:, :, :width]
    keys = proj[:, :, width : 2 * width]
    values = proj[:, :, 2 * width :]
    q_part = lax.all_to_all(query, "tok", split_axis=2, concat_axis=1, tiled=True)
    k_part = lax.all_to_all(keys, "tok", split_axis=2, concat_axis=1, tiled=True)
    v_part = lax.all_to_all(values, "tok", split_axis=2, concat_axis=1, tiled=True)
    mixed = jax.vmap(attend)(q_part, k_part, v_part)
    spatial = lax.all_to_all(mixed, "tok", split_axis=1, concat_axis=2, tiled=True)
    attn_proj = jnp.dot(
        spatial.reshape(-1, width), out_space, preferred_element_type=jnp.float32
    ).reshape(frames, tokens, width)
    stream2 = (stream.astype(jnp.float32) + attn_proj).astype(jnp.bfloat16)
    normed2 = rms_scale(stream2.astype(jnp.float32), gain_time).astype(jnp.bfloat16)
    proj2 = jnp.dot(
        normed2.reshape(-1, width), qkv_time, preferred_element_type=jnp.float32
    ).astype(jnp.bfloat16)
    proj2 = proj2.reshape(frames, tokens, 3 * width)
    query2 = proj2[:, :, :width]
    hops = (WIN + frames - 1) // frames
    history = [normed2]
    moving = normed2
    for hop in range(hops):
        moving = from_behind(moving, "tm", 1)
        history.insert(0, moving)
    joined_in = jnp.concatenate(history[:-1], axis=1)
    joined_kv = jnp.dot(
        joined_in.reshape(-1, width), qkv_time[:, width:], preferred_element_type=jnp.float32
    ).astype(jnp.bfloat16)
    joined_kv = joined_kv.reshape(-1, tokens, 2 * width)
    own_kv = proj2[:, :, width:]
    joined_kv = jnp.concatenate([joined_kv, own_kv], axis=0)
    joined = jnp.stack([joined_kv[:, :, :width], joined_kv[:, :, width:]])
    joined = joined.reshape(2, -1, tokens, width)
    first = lax.axis_index("tm") * frames
    offsets = jnp.arange(WIN + 1, dtype=jnp.int32)
    valid = first + 0 - WIN + offsets >= 0
    results = [tempo(query2[0], joined[0], joined[1], valid)]
    temporal = jnp.stack(results)
    time_proj = jnp.dot(
        temporal.reshape(-1, width), out_time, preferred_element_type=jnp.float32
    ).reshape(frames, tokens, width)
    output = (stream2.astype(jnp.float32) + time_proj).astype(jnp.bfloat16)
    return output.reshape(frames, zdev, grid, grid, width)


def solution(mesh):
    placed = (P("tm", "tok", None, None, None), P(), P(), P(), P(), P(), P(), P(), P())
    return jax.shard_map(
        local,
        mesh=mesh,
        in_specs=placed,
        out_specs=P("tm", "tok", None, None, None),
        check_vma=False,
    )
```

```python
import jax
import jax.numpy as jnp
from jax import lax
from jax.sharding import PartitionSpec as P
from jax.experimental import pallas as pl
from jax.experimental.pallas import tpu as pltpu
import functools

D = 512
H = 8
WIN = 4


def extended(block, sides, width):
    for axis, dim in sides:
        count = lax.axis_size(axis)
        forward = [(i, i + 1) for i in range(count - 1)]
        backward = [(target, source) for source, target in forward]
        low = lax.ppermute(
            lax.slice_in_dim(block, block.shape[dim] - width, None, axis=dim), axis, forward
        )
        high = lax.ppermute(lax.slice_in_dim(block, 0, width, axis=dim), axis, backward)
        block = jnp.concatenate([low, block, high], axis=dim)
    return block


def from_behind(value, axis, steps):
    count = lax.axis_size(axis)
    leading, last = (max(0, -steps), min(count, count - steps))
    return lax.ppermute(value, axis, [(source, source + steps) for source in range(leading, last)])


def rms_scale(values, gain):
    mean_sq = jnp.mean(values * values, axis=-1, keepdims=True)
    return values * lax.rsqrt(mean_sq + 1e-06) * gain.astype(jnp.float32)


def split_heads(block, count, head_size):
    return block.reshape(block.shape[0], count, head_size).transpose(1, 0, 2)


def attend(query, keys, values):
    rows, cols = query.shape
    head_size = D // H
    count = cols // head_size
    scale = head_size ** (-0.5)

    def one_head(parts):
        q_one, k_one, v_one = parts
        scores = jnp.dot(q_one, k_one.T, preferred_element_type=jnp.float32) * scale
        expo = jnp.exp(scores)
        mixed = jnp.dot(expo.astype(jnp.bfloat16), v_one, preferred_element_type=jnp.float32)
        return (mixed / jnp.sum(expo, axis=-1, keepdims=True)).astype(jnp.bfloat16)

    parts = (
        split_heads(query, count, head_size),
        split_heads(keys, count, head_size),
        split_heads(values, count, head_size),
    )
    result = lax.map(one_head, parts)
    return result.transpose(1, 0, 2).reshape(rows, cols)


def pair_attention_kernel(q_ref, k_ref, v_ref, o_ref):
    head_size = D // H
    scale = head_size ** (-0.5)
    q = q_ref[...]
    k = k_ref[...]
    v = v_ref[...]
    lane = lax.broadcasted_iota(jnp.int32, (1, q.shape[1]), 1)
    first = lane < head_size
    outs = []
    for mask in (first, jnp.logical_not(first)):
        q_one = jnp.where(mask, q, jnp.zeros_like(q))
        scores = lax.dot_general(
            q_one, k, (((1,), (1,)), ((), ())), preferred_element_type=jnp.float32
        ) * scale
        expo = jnp.exp(scores)
        total = jnp.sum(expo, axis=-1, keepdims=True)
        mixed = jnp.dot(expo.astype(jnp.bfloat16), v, preferred_element_type=jnp.float32)
        outs.append(mixed / total)
    o_ref[...] = jnp.where(first, outs[0], outs[1]).astype(o_ref.dtype)


def spatial_attention(query, keys, values, block_rows=288):
    rows, width = query.shape
    count = keys.shape[0]
    lanes = 2 * (D // H)
    grid = (width // lanes, rows // block_rows)
    return pl.pallas_call(
        pair_attention_kernel,
        out_shape=jax.ShapeDtypeStruct((rows, width), jnp.bfloat16),
        grid=grid,
        in_specs=[
            pl.BlockSpec((block_rows, lanes), lambda h, r: (r, h)),
            pl.BlockSpec((count, lanes), lambda h, r: (0, h)),
            pl.BlockSpec((count, lanes), lambda h, r: (0, h)),
        ],
        out_specs=pl.BlockSpec((block_rows, lanes), lambda h, r: (r, h)),
    )(query, keys, values)


def tempo(query, keys, values, valid):
    tokens, width = query.shape
    head_size = width // H
    scale = head_size ** (-0.5)
    q_heads = query.reshape(tokens, H, head_size)
    k_heads = keys.reshape(-1, tokens, H, head_size)
    v_heads = values.reshape(-1, tokens, H, head_size)
    scores = (
        jnp.einsum("nhd,wnhd->nhw", q_heads, k_heads, preferred_element_type=jnp.float32) * scale
    )
    expo = jnp.where(valid, jnp.exp(scores), 0.0)
    mixed = jnp.einsum(
        "nhw,wnhd->nhd", expo.astype(jnp.bfloat16), v_heads, preferred_element_type=jnp.float32
    )
    mixed = mixed / jnp.sum(expo, axis=-1)[..., None]
    return mixed.astype(jnp.bfloat16).reshape(tokens, width)


def local(
    patches,
    patch_weight,
    conv_taps,
    gain_space,
    qkv_space,
    out_space,
    gain_time,
    qkv_time,
    out_time,
):
    frames, zdev, grid, _, patch = patches.shape
    width = patch_weight.shape[1]
    tokens = zdev * grid * grid
    embed = jnp.dot(
        patches.reshape(-1, patch), patch_weight, preferred_element_type=jnp.float32
    ).astype(jnp.bfloat16)
    embed = embed.reshape(frames, zdev, grid, grid, width)
    padded = extended(embed, (("tok", 1),), 1)
    padded = jnp.pad(padded, ((0, 0), (0, 0), (1, 1), (1, 1), (0, 0)))
    conv = jnp.zeros((frames, zdev, grid, grid, width), jnp.float32)
    for dz in range(3):
        for dy in range(3):
            for dx in range(3):
                tap = conv_taps[9 * dz + 3 * dy + dx].astype(jnp.float32)
                conv = conv + tap * padded[
                    :, dz : dz + zdev, dy : dy + grid, dx : dx + grid
                ].astype(jnp.float32)
    stream = (embed.astype(jnp.float32) + conv).astype(jnp.bfloat16).reshape(frames, tokens, width)
    normed = rms_scale(stream.astype(jnp.float32), gain_space).astype(jnp.bfloat16)
    proj = jnp.dot(normed.reshape(-1, width), qkv_space, preferred_element_type=jnp.float32).astype(
        jnp.bfloat16
    )
    proj = proj.reshape(frames, tokens, 3 * width)
    query = proj[0, :, :width]
    own_kv = proj[0, :, width:]
    count = lax.axis_size("tok")
    other_kv = lax.ppermute(own_kv, "tok", [(i, (i + 1) % count) for i in range(count)])
    all_kv = jnp.concatenate([own_kv, other_kv], axis=0)
    spatial = spatial_attention(query, all_kv[:, :width], all_kv[:, width:])
    attn_proj = jnp.dot(
        spatial.reshape(-1, width), out_space, preferred_element_type=jnp.float32
    ).reshape(frames, tokens, width)
    stream2 = (stream.astype(jnp.float32) + attn_proj).astype(jnp.bfloat16)
    normed2 = rms_scale(stream2.astype(jnp.float32), gain_time).astype(jnp.bfloat16)
    proj2 = jnp.dot(
        normed2.reshape(-1, width), qkv_time, preferred_element_type=jnp.float32
    ).astype(jnp.bfloat16)
    proj2 = proj2.reshape(frames, tokens, 3 * width)
    query2 = proj2[:, :, :width]
    hops = (WIN + frames - 1) // frames
    history = [normed2]
    moving = normed2
    for hop in range(hops):
        moving = from_behind(moving, "tm", 1)
        history.insert(0, moving)
    joined_in = jnp.concatenate(history[:-1], axis=1)
    joined_kv = jnp.dot(
        joined_in.reshape(-1, width), qkv_time[:, width:], preferred_element_type=jnp.float32
    ).astype(jnp.bfloat16)
    joined_kv = joined_kv.reshape(-1, tokens, 2 * width)
    own_kv = proj2[:, :, width:]
    joined_kv = jnp.concatenate([joined_kv, own_kv], axis=0)
    joined = jnp.stack([joined_kv[:, :, :width], joined_kv[:, :, width:]])
    joined = joined.reshape(2, -1, tokens, width)
    first = lax.axis_index("tm") * frames
    offsets = jnp.arange(WIN + 1, dtype=jnp.int32)
    valid = first + 0 - WIN + offsets >= 0
    results = [tempo(query2[0], joined[0], joined[1], valid)]
    temporal = jnp.stack(results)
    time_proj = jnp.dot(
        temporal.reshape(-1, width), out_time, preferred_element_type=jnp.float32
    ).reshape(frames, tokens, width)
    output = (stream2.astype(jnp.float32) + time_proj).astype(jnp.bfloat16)
    return output.reshape(frames, zdev, grid, grid, width)


def solution(mesh):
    placed = (P("tm", "tok", None, None, None), P(), P(), P(), P(), P(), P(), P(), P())
    return jax.shard_map(
        local,
        mesh=mesh,
        in_specs=placed,
        out_specs=P("tm", "tok", None, None, None),
        check_vma=False,
    )
```

```python
import jax
import jax.numpy as jnp
from jax import lax
from jax.sharding import PartitionSpec as P
from jax.experimental import pallas as pl
from jax.experimental.pallas import tpu as pltpu
import functools

D = 512
H = 8
WIN = 4


def extended(block, sides, width):
    for axis, dim in sides:
        count = lax.axis_size(axis)
        forward = [(i, i + 1) for i in range(count - 1)]
        backward = [(target, source) for source, target in forward]
        low = lax.ppermute(
            lax.slice_in_dim(block, block.shape[dim] - width, None, axis=dim), axis, forward
        )
        high = lax.ppermute(lax.slice_in_dim(block, 0, width, axis=dim), axis, backward)
        block = jnp.concatenate([low, block, high], axis=dim)
    return block


def from_behind(value, axis, steps):
    count = lax.axis_size(axis)
    leading, last = (max(0, -steps), min(count, count - steps))
    return lax.ppermute(value, axis, [(source, source + steps) for source in range(leading, last)])


def rms_scale(values, gain):
    mean_sq = jnp.mean(values * values, axis=-1, keepdims=True)
    return values * lax.rsqrt(mean_sq + 1e-06) * gain.astype(jnp.float32)


def split_heads(block, count, head_size):
    return block.reshape(block.shape[0], count, head_size).transpose(1, 0, 2)


def attend(query, keys, values):
    rows, cols = query.shape
    head_size = D // H
    count = cols // head_size
    scale = head_size ** (-0.5)

    def one_head(parts):
        q_one, k_one, v_one = parts
        scores = jnp.dot(q_one, k_one.T, preferred_element_type=jnp.float32) * scale
        expo = jnp.exp(scores)
        mixed = jnp.dot(expo.astype(jnp.bfloat16), v_one, preferred_element_type=jnp.float32)
        return (mixed / jnp.sum(expo, axis=-1, keepdims=True)).astype(jnp.bfloat16)

    parts = (
        split_heads(query, count, head_size),
        split_heads(keys, count, head_size),
        split_heads(values, count, head_size),
    )
    result = lax.map(one_head, parts)
    return result.transpose(1, 0, 2).reshape(rows, cols)


def pair_attention_kernel(q_ref, k_ref, v_ref, o_ref):
    head_size = D // H
    scale = head_size ** (-0.5)
    q = q_ref[...]
    k = k_ref[...]
    v = v_ref[...]
    lane = lax.broadcasted_iota(jnp.int32, (1, q.shape[1]), 1)
    first = lane < head_size
    outs = []
    for mask in (first, jnp.logical_not(first)):
        q_one = jnp.where(mask, q, jnp.zeros_like(q))
        scores = lax.dot_general(
            q_one, k, (((1,), (1,)), ((), ())), preferred_element_type=jnp.float32
        ) * scale
        expo = jnp.exp(scores)
        total = jnp.sum(expo, axis=-1, keepdims=True)
        mixed = jnp.dot(expo.astype(jnp.bfloat16), v, preferred_element_type=jnp.float32)
        outs.append(mixed / total)
    o_ref[...] = jnp.where(first, outs[0], outs[1]).astype(o_ref.dtype)


def spatial_attention(query, keys, values, block_rows=288):
    rows, width = query.shape
    count = keys.shape[0]
    lanes = 2 * (D // H)
    grid = (width // lanes, rows // block_rows)
    return pl.pallas_call(
        pair_attention_kernel,
        out_shape=jax.ShapeDtypeStruct((rows, width), jnp.bfloat16),
        grid=grid,
        in_specs=[
            pl.BlockSpec((block_rows, lanes), lambda h, r: (r, h)),
            pl.BlockSpec((count, lanes), lambda h, r: (0, h)),
            pl.BlockSpec((count, lanes), lambda h, r: (0, h)),
        ],
        out_specs=pl.BlockSpec((block_rows, lanes), lambda h, r: (r, h)),
    )(query, keys, values)


def local(
    patches,
    patch_weight,
    conv_taps,
    gain_space,
    qkv_space,
    out_space,
    gain_time,
    qkv_time,
    out_time,
):
    frames, zdev, grid, _, patch = patches.shape
    width = patch_weight.shape[1]
    tokens = zdev * grid * grid
    embed = jnp.dot(
        patches.reshape(-1, patch), patch_weight, preferred_element_type=jnp.float32
    ).astype(jnp.bfloat16)
    embed = embed.reshape(frames, zdev, grid, grid, width)
    padded = extended(embed, (("tok", 1),), 1)
    padded = jnp.pad(padded, ((0, 0), (0, 0), (1, 1), (1, 1), (0, 0)))
    conv = jnp.zeros((frames, zdev, grid, grid, width), jnp.float32)
    for dz in range(3):
        for dy in range(3):
            for dx in range(3):
                tap = conv_taps[9 * dz + 3 * dy + dx].astype(jnp.float32)
                conv = conv + tap * padded[
                    :, dz : dz + zdev, dy : dy + grid, dx : dx + grid
                ].astype(jnp.float32)
    stream = (embed.astype(jnp.float32) + conv).astype(jnp.bfloat16).reshape(frames, tokens, width)
    normed = rms_scale(stream.astype(jnp.float32), gain_space).astype(jnp.bfloat16)
    proj = jnp.dot(normed.reshape(-1, width), qkv_space, preferred_element_type=jnp.float32).astype(
        jnp.bfloat16
    )
    proj = proj.reshape(frames, tokens, 3 * width)
    query = proj[0, :, :width]
    own_kv = proj[0, :, width:]
    count = lax.axis_size("tok")
    other_kv = lax.ppermute(own_kv, "tok", [(i, (i + 1) % count) for i in range(count)])
    all_kv = jnp.concatenate([own_kv, other_kv], axis=0)
    spatial = spatial_attention(query, all_kv[:, :width], all_kv[:, width:])
    attn_proj = jnp.dot(
        spatial.reshape(-1, width), out_space, preferred_element_type=jnp.float32
    ).reshape(frames, tokens, width)
    stream2 = (stream.astype(jnp.float32) + attn_proj).astype(jnp.bfloat16)
    normed2 = rms_scale(stream2.astype(jnp.float32), gain_time).astype(jnp.bfloat16)
    proj2 = jnp.dot(
        normed2.reshape(-1, width), qkv_time, preferred_element_type=jnp.float32
    ).astype(jnp.bfloat16)
    proj2 = proj2.reshape(frames, tokens, 3 * width)
    query2 = proj2[0, :, :width].astype(jnp.float32)
    kv_weight = qkv_time[:, width:]
    heads = lax.broadcasted_iota(jnp.int32, (width, width), 0) // (width // H)
    same_head = heads == lax.broadcasted_iota(jnp.int32, (width, width), 1) // (width // H)
    summer = jnp.concatenate([same_head, same_head], axis=0).astype(jnp.bfloat16)
    scale = (width // H) ** (-0.5)

    def time_term(kv, valid):
        keys2 = kv[:, :width].astype(jnp.float32)
        values2 = kv[:, width:].astype(jnp.float32)
        prod = query2 * keys2
        high = prod.astype(jnp.bfloat16)
        low = (prod - high.astype(jnp.float32)).astype(jnp.bfloat16)
        scores = jnp.dot(
            jnp.concatenate([high, low], axis=1), summer, preferred_element_type=jnp.float32
        ) * scale
        expo = jnp.where(valid, jnp.exp(scores), 0.0)
        return expo.astype(jnp.bfloat16).astype(jnp.float32) * values2, expo

    first = lax.axis_index("tm") * frames
    mixed, total = time_term(proj2[0, :, width:], True)
    moving = normed2[0]
    for back in range(1, WIN + 1):
        moving = from_behind(moving, "tm", 1)
        kv = jnp.dot(moving, kv_weight, preferred_element_type=jnp.float32).astype(jnp.bfloat16)
        part, expo = time_term(kv, first - back >= 0)
        mixed = mixed + part
        total = total + expo
    temporal = (mixed / total).astype(jnp.bfloat16)
    time_proj = jnp.dot(
        temporal.reshape(-1, width), out_time, preferred_element_type=jnp.float32
    ).reshape(frames, tokens, width)
    output = (stream2.astype(jnp.float32) + time_proj).astype(jnp.bfloat16)
    return output.reshape(frames, zdev, grid, grid, width)


def solution(mesh):
    placed = (P("tm", "tok", None, None, None), P(), P(), P(), P(), P(), P(), P(), P())
    return jax.shard_map(
        local,
        mesh=mesh,
        in_specs=placed,
        out_specs=P("tm", "tok", None, None, None),
        check_vma=False,
    )
```

```python
import jax
import jax.numpy as jnp
from jax import lax
from jax.sharding import PartitionSpec as P
from jax.experimental import pallas as pl
from jax.experimental.pallas import tpu as pltpu
import functools

D = 512
H = 8
WIN = 4


def extended(block, sides, width):
    for axis, dim in sides:
        count = lax.axis_size(axis)
        forward = [(i, i + 1) for i in range(count - 1)]
        backward = [(target, source) for source, target in forward]
        low = lax.ppermute(
            lax.slice_in_dim(block, block.shape[dim] - width, None, axis=dim), axis, forward
        )
        high = lax.ppermute(lax.slice_in_dim(block, 0, width, axis=dim), axis, backward)
        block = jnp.concatenate([low, block, high], axis=dim)
    return block


def from_behind(value, axis, steps):
    count = lax.axis_size(axis)
    leading, last = (max(0, -steps), min(count, count - steps))
    return lax.ppermute(value, axis, [(source, source + steps) for source in range(leading, last)])


def rms_scale(values, gain):
    mean_sq = jnp.mean(values * values, axis=-1, keepdims=True)
    return values * lax.rsqrt(mean_sq + 1e-06) * gain.astype(jnp.float32)


def split_heads(block, count, head_size):
    return block.reshape(block.shape[0], count, head_size).transpose(1, 0, 2)


def attend(query, keys, values):
    rows, cols = query.shape
    head_size = D // H
    count = cols // head_size
    scale = head_size ** (-0.5)

    def one_head(parts):
        q_one, k_one, v_one = parts
        scores = jnp.dot(q_one, k_one.T, preferred_element_type=jnp.float32) * scale
        expo = jnp.exp(scores)
        mixed = jnp.dot(expo.astype(jnp.bfloat16), v_one, preferred_element_type=jnp.float32)
        return (mixed / jnp.sum(expo, axis=-1, keepdims=True)).astype(jnp.bfloat16)

    parts = (
        split_heads(query, count, head_size),
        split_heads(keys, count, head_size),
        split_heads(values, count, head_size),
    )
    result = lax.map(one_head, parts)
    return result.transpose(1, 0, 2).reshape(rows, cols)


def pair_attention_kernel(q_ref, k_ref, v_ref, o_ref):
    head_size = D // H
    scale = head_size ** (-0.5)
    q = q_ref[...]
    k = k_ref[...]
    v = v_ref[...]
    lane = lax.broadcasted_iota(jnp.int32, (1, q.shape[1]), 1)
    first = lane < head_size
    outs = []
    for mask in (first, jnp.logical_not(first)):
        q_one = jnp.where(mask, q, jnp.zeros_like(q))
        scores = lax.dot_general(
            q_one, k, (((1,), (1,)), ((), ())), preferred_element_type=jnp.float32
        ) * scale
        expo = jnp.exp(scores)
        total = jnp.sum(expo, axis=-1, keepdims=True)
        mixed = jnp.dot(expo.astype(jnp.bfloat16), v, preferred_element_type=jnp.float32)
        outs.append(mixed / total)
    o_ref[...] = jnp.where(first, outs[0], outs[1]).astype(o_ref.dtype)


def spatial_attention(query, keys, values, block_rows=288):
    rows, width = query.shape
    count = keys.shape[0]
    lanes = 2 * (D // H)
    grid = (width // lanes, rows // block_rows)
    return pl.pallas_call(
        pair_attention_kernel,
        out_shape=jax.ShapeDtypeStruct((rows, width), jnp.bfloat16),
        grid=grid,
        in_specs=[
            pl.BlockSpec((block_rows, lanes), lambda h, r: (r, h)),
            pl.BlockSpec((count, lanes), lambda h, r: (0, h)),
            pl.BlockSpec((count, lanes), lambda h, r: (0, h)),
        ],
        out_specs=pl.BlockSpec((block_rows, lanes), lambda h, r: (r, h)),
    )(query, keys, values)


def block_kernel(
    chunks, proj_ref, other_ref, stream_ref, wo_ref, gain_ref, wt_ref,
    out_ref, stream2_ref, own, query2, hist, mixed, total, sum_ref, send_sem, recv_sem,
):
    me = lax.axis_index("tm")
    count = lax.axis_size("tm")
    core = lax.axis_index("tok")
    has_left = me > 0
    has_right = me < count - 1
    rows_all, width = own.shape
    rows = rows_all // chunks
    head_size = width // H
    scale = head_size ** (-0.5)
    lanes = 2 * head_size
    mesh_ids = pl.DeviceIdType.MESH

    @pl.when(jnp.logical_not(has_left))
    def _():
        hist[...] = jnp.zeros_like(hist)

    barrier = pltpu.get_barrier_semaphore()

    @pl.when(has_left)
    def _():
        pl.semaphore_signal(barrier, inc=1, device_id=(me - 1, core), device_id_type=mesh_ids)

    @pl.when(has_right)
    def _():
        pl.semaphore_signal(barrier, inc=1, device_id=(me + 1, core), device_id_type=mesh_ids)

    @pl.when(jnp.logical_and(has_left, has_right))
    def _():
        pl.semaphore_wait(barrier, 2)

    @pl.when(jnp.logical_xor(has_left, has_right))
    def _():
        pl.semaphore_wait(barrier, 1)

    def span_of(piece):
        return pl.ds(pl.multiple_of(piece * rows, 8), rows)

    def copy_of(hop, piece):
        span = span_of(piece)
        source = own.at[span] if hop == 0 else hist.at[hop - 1, span]
        return pltpu.make_async_remote_copy(
            src_ref=source,
            dst_ref=hist.at[hop, span],
            send_sem=send_sem.at[hop, piece],
            recv_sem=recv_sem.at[hop, piece],
            device_id=(me + 1, core),
            device_id_type=mesh_ids,
        )

    lane = lax.broadcasted_iota(jnp.int32, (1, lanes), 1)
    first_half = lane < head_size
    heads = lax.broadcasted_iota(jnp.int32, (width, width), 0) // head_size
    same_head = heads == lax.broadcasted_iota(jnp.int32, (width, width), 1) // head_size
    sum_ref[...] = same_head.astype(jnp.bfloat16)

    def space_step(piece, carry):
        span = span_of(piece)
        pieces = []
        for pair in range(width // lanes):
            cols = slice(pair * lanes, (pair + 1) * lanes)
            q = proj_ref[span, cols]
            key_cols = slice(width + pair * lanes, width + (pair + 1) * lanes)
            value_cols = slice(2 * width + pair * lanes, 2 * width + (pair + 1) * lanes)
            sources = (
                (proj_ref[:, key_cols], proj_ref[:, value_cols]),
                (other_ref[:, cols], other_ref[:, key_cols]),
            )
            outs = []
            for mask in (first_half, jnp.logical_not(first_half)):
                q_one = jnp.where(mask, q, jnp.zeros_like(q))
                rowsum = None
                mixed_one = None
                for k, v in sources:
                    scores = lax.dot_general(
                        q_one, k, (((1,), (1,)), ((), ())), preferred_element_type=jnp.float32
                    ) * scale
                    expo = jnp.exp(scores)
                    part_sum = jnp.sum(expo, axis=-1, keepdims=True)
                    part = jnp.dot(
                        expo.astype(jnp.bfloat16), v, preferred_element_type=jnp.float32
                    )
                    rowsum = part_sum if rowsum is None else rowsum + part_sum
                    mixed_one = part if mixed_one is None else mixed_one + part
                outs.append(mixed_one / rowsum)
            pieces.append(jnp.where(first_half, outs[0], outs[1]).astype(jnp.bfloat16))
        spatial = jnp.concatenate(pieces, axis=1)
        stream2 = (
            stream_ref[span, :].astype(jnp.float32)
            + jnp.dot(spatial, wo_ref[...], preferred_element_type=jnp.float32)
        ).astype(jnp.bfloat16)
        stream2_ref[span, :] = stream2
        values = stream2.astype(jnp.float32)
        mean_sq = jnp.mean(values * values, axis=-1, keepdims=True)
        normed2 = (values * lax.rsqrt(mean_sq + 1e-06) * gain_ref[...]).astype(jnp.bfloat16)
        own[span, :] = normed2
        query2[span, :] = jnp.dot(
            normed2, wt_ref[:, :width], preferred_element_type=jnp.float32
        ).astype(jnp.bfloat16)

        @pl.when(jnp.logical_and(has_right, piece >= 1))
        def _():
            copy_of(0, piece - 1).start()

        return carry

    lax.fori_loop(0, chunks, space_step, 0)

    def add_term(block, span, valid, first):
        kv = jnp.dot(block, wt_ref[:, width:], preferred_element_type=jnp.float32).astype(jnp.bfloat16)
        keys2 = kv[:, :width].astype(jnp.float32)
        values2 = kv[:, width:].astype(jnp.float32)
        prod = query2[span, :].astype(jnp.float32) * keys2
        high = prod.astype(jnp.bfloat16)
        low = (prod - high.astype(jnp.float32)).astype(jnp.bfloat16)
        summer = sum_ref[...]
        scores = (
            jnp.dot(high, summer, preferred_element_type=jnp.float32)
            + jnp.dot(low, summer, preferred_element_type=jnp.float32)
        ) * scale
        expo = jnp.where(valid, jnp.exp(scores), 0.0)
        part = expo.astype(jnp.bfloat16).astype(jnp.float32) * values2
        if first:
            mixed[span, :] = part
            total[span, :] = expo
        else:
            mixed[span, :] += part
            total[span, :] += expo

    def own_step(piece, carry):
        span = span_of(piece)
        add_term(own[span, :], span, True, True)
        return carry

    lax.fori_loop(0, chunks, own_step, 0)

    @pl.when(has_right)
    def _():
        copy_of(0, chunks - 1).start()

    for hop in range(WIN):
        def hop_step(piece, carry, hop=hop):
            span = span_of(piece)

            @pl.when(has_left)
            def _():
                copy_of(hop, piece).wait_recv()

            if hop + 1 < WIN:
                @pl.when(has_right)
                def _():
                    copy_of(hop + 1, piece).start()

            add_term(hist[hop, span, :], span, me - (hop + 1) >= 0, False)
            return carry

        lax.fori_loop(0, chunks, hop_step, 0)

    @pl.when(has_right)
    def _():
        for hop in range(WIN):
            for piece in range(chunks):
                copy_of(hop, piece).wait_send()

    out_ref[...] = (mixed[...] / total[...]).astype(out_ref.dtype)


def block_tail(proj, other, stream, out_space, gain_time, qkv_time, chunks=6):
    rows, width = stream.shape
    gain = gain_time.astype(jnp.float32).reshape(1, width)
    vmem = pl.BlockSpec(memory_space=pltpu.VMEM)
    plane = jax.ShapeDtypeStruct((rows, width), jnp.bfloat16)
    return pl.pallas_call(
        functools.partial(block_kernel, chunks),
        out_shape=(plane, plane),
        in_specs=[vmem] * 6,
        out_specs=(vmem, vmem),
        scratch_shapes=[
            pltpu.VMEM((rows, width), jnp.bfloat16),
            pltpu.VMEM((rows, width), jnp.bfloat16),
            pltpu.VMEM((WIN, rows, width), jnp.bfloat16),
            pltpu.VMEM((rows, width), jnp.float32),
            pltpu.VMEM((rows, width), jnp.float32),
            pltpu.VMEM((width, width), jnp.bfloat16),
            pltpu.SemaphoreType.DMA((WIN, chunks)),
            pltpu.SemaphoreType.DMA((WIN, chunks)),
        ],
        compiler_params=pltpu.CompilerParams(
            collective_id=0, has_side_effects=True, vmem_limit_bytes=56 * 1024 * 1024
        ),
    )(proj, other, stream, out_space, gain, qkv_time)


def local(
    patches,
    patch_weight,
    conv_taps,
    gain_space,
    qkv_space,
    out_space,
    gain_time,
    qkv_time,
    out_time,
):
    frames, zdev, grid, _, patch = patches.shape
    width = patch_weight.shape[1]
    tokens = zdev * grid * grid
    embed = jnp.dot(
        patches.reshape(-1, patch), patch_weight, preferred_element_type=jnp.float32
    ).astype(jnp.bfloat16)
    embed = embed.reshape(frames, zdev, grid, grid, width)
    padded = extended(embed, (("tok", 1),), 1)
    padded = jnp.pad(padded, ((0, 0), (0, 0), (1, 1), (1, 1), (0, 0)))
    conv = jnp.zeros((frames, zdev, grid, grid, width), jnp.float32)
    for dz in range(3):
        for dy in range(3):
            for dx in range(3):
                tap = conv_taps[9 * dz + 3 * dy + dx].astype(jnp.float32)
                conv = conv + tap * padded[
                    :, dz : dz + zdev, dy : dy + grid, dx : dx + grid
                ].astype(jnp.float32)
    stream = (embed.astype(jnp.float32) + conv).astype(jnp.bfloat16).reshape(frames, tokens, width)
    normed = rms_scale(stream.astype(jnp.float32), gain_space).astype(jnp.bfloat16)
    proj = jnp.dot(normed.reshape(-1, width), qkv_space, preferred_element_type=jnp.float32).astype(
        jnp.bfloat16
    )
    proj = proj.reshape(frames, tokens, 3 * width)
    own_kv = proj[0, :, width:]
    count = lax.axis_size("tok")
    other_kv = lax.ppermute(own_kv, "tok", [(i, (i + 1) % count) for i in range(count)])
    temporal, stream2 = block_tail(
        proj[0], other_kv, stream.reshape(-1, width), out_space, gain_time, qkv_time
    )
    time_proj = jnp.dot(
        temporal.reshape(-1, width), out_time, preferred_element_type=jnp.float32
    ).reshape(frames, tokens, width)
    output = (stream2.astype(jnp.float32) + time_proj).astype(jnp.bfloat16)
    return output.reshape(frames, zdev, grid, grid, width)


def solution(mesh):
    placed = (P("tm", "tok", None, None, None), P(), P(), P(), P(), P(), P(), P(), P())
    return jax.shard_map(
        local,
        mesh=mesh,
        in_specs=placed,
        out_specs=P("tm", "tok", None, None, None),
        check_vma=False,
    )
```

```python
import jax
import jax.numpy as jnp
from jax import lax
from jax.sharding import PartitionSpec as P
from jax.experimental import pallas as pl
from jax.experimental.pallas import tpu as pltpu
import functools

D = 512
H = 8
WIN = 4


def extended(block, sides, width):
    for axis, dim in sides:
        count = lax.axis_size(axis)
        forward = [(i, i + 1) for i in range(count - 1)]
        backward = [(target, source) for source, target in forward]
        low = lax.ppermute(
            lax.slice_in_dim(block, block.shape[dim] - width, None, axis=dim), axis, forward
        )
        high = lax.ppermute(lax.slice_in_dim(block, 0, width, axis=dim), axis, backward)
        block = jnp.concatenate([low, block, high], axis=dim)
    return block


def from_behind(value, axis, steps):
    count = lax.axis_size(axis)
    leading, last = (max(0, -steps), min(count, count - steps))
    return lax.ppermute(value, axis, [(source, source + steps) for source in range(leading, last)])


def rms_scale(values, gain):
    mean_sq = jnp.mean(values * values, axis=-1, keepdims=True)
    return values * lax.rsqrt(mean_sq + 1e-06) * gain.astype(jnp.float32)


def split_heads(block, count, head_size):
    return block.reshape(block.shape[0], count, head_size).transpose(1, 0, 2)


def attend(query, keys, values):
    rows, cols = query.shape
    head_size = D // H
    count = cols // head_size
    scale = head_size ** (-0.5)

    def one_head(parts):
        q_one, k_one, v_one = parts
        scores = jnp.dot(q_one, k_one.T, preferred_element_type=jnp.float32) * scale
        expo = jnp.exp(scores)
        mixed = jnp.dot(expo.astype(jnp.bfloat16), v_one, preferred_element_type=jnp.float32)
        return (mixed / jnp.sum(expo, axis=-1, keepdims=True)).astype(jnp.bfloat16)

    parts = (
        split_heads(query, count, head_size),
        split_heads(keys, count, head_size),
        split_heads(values, count, head_size),
    )
    result = lax.map(one_head, parts)
    return result.transpose(1, 0, 2).reshape(rows, cols)


def pair_attention_kernel(q_ref, k_ref, v_ref, o_ref):
    head_size = D // H
    scale = head_size ** (-0.5)
    q = q_ref[...]
    k = k_ref[...]
    v = v_ref[...]
    lane = lax.broadcasted_iota(jnp.int32, (1, q.shape[1]), 1)
    first = lane < head_size
    outs = []
    for mask in (first, jnp.logical_not(first)):
        q_one = jnp.where(mask, q, jnp.zeros_like(q))
        scores = lax.dot_general(
            q_one, k, (((1,), (1,)), ((), ())), preferred_element_type=jnp.float32
        ) * scale
        expo = jnp.exp(scores)
        total = jnp.sum(expo, axis=-1, keepdims=True)
        mixed = jnp.dot(expo.astype(jnp.bfloat16), v, preferred_element_type=jnp.float32)
        outs.append(mixed / total)
    o_ref[...] = jnp.where(first, outs[0], outs[1]).astype(o_ref.dtype)


def spatial_attention(query, keys, values, block_rows=288):
    rows, width = query.shape
    count = keys.shape[0]
    lanes = 2 * (D // H)
    grid = (width // lanes, rows // block_rows)
    return pl.pallas_call(
        pair_attention_kernel,
        out_shape=jax.ShapeDtypeStruct((rows, width), jnp.bfloat16),
        grid=grid,
        in_specs=[
            pl.BlockSpec((block_rows, lanes), lambda h, r: (r, h)),
            pl.BlockSpec((count, lanes), lambda h, r: (0, h)),
            pl.BlockSpec((count, lanes), lambda h, r: (0, h)),
        ],
        out_specs=pl.BlockSpec((block_rows, lanes), lambda h, r: (r, h)),
    )(query, keys, values)


def block_kernel(
    chunks, proj_ref, other_ref, stream_ref, wo_ref, gain_ref, wt_ref, wout_ref,
    out_ref, stream2_ref, own, query2, hist, mixed, total, sum_ref, send_sem, recv_sem,
):
    me = lax.axis_index("tm")
    count = lax.axis_size("tm")
    core = lax.axis_index("tok")
    has_left = me > 0
    has_right = me < count - 1
    rows_all, width = own.shape
    rows = rows_all // chunks
    head_size = width // H
    scale = head_size ** (-0.5)
    lanes = 2 * head_size
    mesh_ids = pl.DeviceIdType.MESH

    @pl.when(jnp.logical_not(has_left))
    def _():
        hist[...] = jnp.zeros_like(hist)

    barrier = pltpu.get_barrier_semaphore()

    @pl.when(has_left)
    def _():
        pl.semaphore_signal(barrier, inc=1, device_id=(me - 1, core), device_id_type=mesh_ids)

    @pl.when(has_right)
    def _():
        pl.semaphore_signal(barrier, inc=1, device_id=(me + 1, core), device_id_type=mesh_ids)

    @pl.when(jnp.logical_and(has_left, has_right))
    def _():
        pl.semaphore_wait(barrier, 2)

    @pl.when(jnp.logical_xor(has_left, has_right))
    def _():
        pl.semaphore_wait(barrier, 1)

    def span_of(piece):
        return pl.ds(pl.multiple_of(piece * rows, 8), rows)

    def copy_of(hop, piece):
        span = span_of(piece)
        source = own.at[span] if hop == 0 else hist.at[hop - 1, span]
        return pltpu.make_async_remote_copy(
            src_ref=source,
            dst_ref=hist.at[hop, span],
            send_sem=send_sem.at[hop, piece],
            recv_sem=recv_sem.at[hop, piece],
            device_id=(me + 1, core),
            device_id_type=mesh_ids,
        )

    lane = lax.broadcasted_iota(jnp.int32, (1, lanes), 1)
    first_half = lane < head_size
    heads = lax.broadcasted_iota(jnp.int32, (width, width), 0) // head_size
    same_head = heads == lax.broadcasted_iota(jnp.int32, (width, width), 1) // head_size
    sum_ref[...] = same_head.astype(jnp.bfloat16)

    def space_step(piece, carry):
        span = span_of(piece)
        pieces = []
        for pair in range(width // lanes):
            cols = slice(pair * lanes, (pair + 1) * lanes)
            q = proj_ref[span, cols]
            key_cols = slice(width + pair * lanes, width + (pair + 1) * lanes)
            value_cols = slice(2 * width + pair * lanes, 2 * width + (pair + 1) * lanes)
            sources = (
                (proj_ref[:, key_cols], proj_ref[:, value_cols]),
                (other_ref[:, cols], other_ref[:, key_cols]),
            )
            outs = []
            for mask in (first_half, jnp.logical_not(first_half)):
                q_one = jnp.where(mask, q, jnp.zeros_like(q))
                rowsum = None
                mixed_one = None
                for k, v in sources:
                    scores = lax.dot_general(
                        q_one, k, (((1,), (1,)), ((), ())), preferred_element_type=jnp.float32
                    ) * scale
                    expo = jnp.exp(scores)
                    part_sum = jnp.sum(expo, axis=-1, keepdims=True)
                    part = jnp.dot(
                        expo.astype(jnp.bfloat16), v, preferred_element_type=jnp.float32
                    )
                    rowsum = part_sum if rowsum is None else rowsum + part_sum
                    mixed_one = part if mixed_one is None else mixed_one + part
                outs.append(mixed_one / rowsum)
            pieces.append(jnp.where(first_half, outs[0], outs[1]).astype(jnp.bfloat16))
        spatial = jnp.concatenate(pieces, axis=1)
        stream2 = (
            stream_ref[span, :].astype(jnp.float32)
            + jnp.dot(spatial, wo_ref[...], preferred_element_type=jnp.float32)
        ).astype(jnp.bfloat16)
        stream2_ref[span, :] = stream2
        values = stream2.astype(jnp.float32)
        mean_sq = jnp.mean(values * values, axis=-1, keepdims=True)
        normed2 = (values * lax.rsqrt(mean_sq + 1e-06) * gain_ref[...]).astype(jnp.bfloat16)
        own[span, :] = normed2
        query2[span, :] = jnp.dot(
            normed2, wt_ref[:, :width], preferred_element_type=jnp.float32
        ).astype(jnp.bfloat16)

        @pl.when(jnp.logical_and(has_right, piece >= 1))
        def _():
            copy_of(0, piece - 1).start()

        return carry

    lax.fori_loop(0, chunks, space_step, 0)

    def add_term(block, span, valid, first):
        kv = jnp.dot(block, wt_ref[:, width:], preferred_element_type=jnp.float32).astype(jnp.bfloat16)
        keys2 = kv[:, :width].astype(jnp.float32)
        values2 = kv[:, width:].astype(jnp.float32)
        prod = query2[span, :].astype(jnp.float32) * keys2
        high = prod.astype(jnp.bfloat16)
        low = (prod - high.astype(jnp.float32)).astype(jnp.bfloat16)
        summer = sum_ref[...]
        scores = (
            jnp.dot(high, summer, preferred_element_type=jnp.float32)
            + jnp.dot(low, summer, preferred_element_type=jnp.float32)
        ) * scale
        expo = jnp.where(valid, jnp.exp(scores), 0.0)
        part = expo.astype(jnp.bfloat16).astype(jnp.float32) * values2
        if first:
            mixed[span, :] = part
            total[span, :] = expo
        else:
            mixed[span, :] += part
            total[span, :] += expo

    def own_step(piece, carry):
        span = span_of(piece)
        add_term(own[span, :], span, True, True)
        return carry

    lax.fori_loop(0, chunks, own_step, 0)

    @pl.when(has_right)
    def _():
        copy_of(0, chunks - 1).start()

    for hop in range(WIN):
        def hop_step(piece, carry, hop=hop):
            span = span_of(piece)

            @pl.when(has_left)
            def _():
                copy_of(hop, piece).wait_recv()

            if hop + 1 < WIN:
                @pl.when(has_right)
                def _():
                    copy_of(hop + 1, piece).start()

            add_term(hist[hop, span, :], span, me - (hop + 1) >= 0, False)
            if hop + 1 == WIN:
                temporal = (mixed[span, :] / total[span, :]).astype(jnp.bfloat16)
                out_ref[span, :] = (
                    stream2_ref[span, :].astype(jnp.float32)
                    + jnp.dot(temporal, wout_ref[...], preferred_element_type=jnp.float32)
                ).astype(out_ref.dtype)
            return carry

        lax.fori_loop(0, chunks, hop_step, 0)

    @pl.when(has_right)
    def _():
        for hop in range(WIN):
            for piece in range(chunks):
                copy_of(hop, piece).wait_send()


def block_tail(proj, other, stream, out_space, gain_time, qkv_time, out_time, chunks=9):
    rows, width = stream.shape
    gain = gain_time.astype(jnp.float32).reshape(1, width)
    vmem = pl.BlockSpec(memory_space=pltpu.VMEM)
    plane = jax.ShapeDtypeStruct((rows, width), jnp.bfloat16)
    return pl.pallas_call(
        functools.partial(block_kernel, chunks),
        out_shape=plane,
        in_specs=[vmem] * 7,
        out_specs=vmem,
        scratch_shapes=[
            pltpu.VMEM((rows, width), jnp.bfloat16),
            pltpu.VMEM((rows, width), jnp.bfloat16),
            pltpu.VMEM((rows, width), jnp.bfloat16),
            pltpu.VMEM((WIN, rows, width), jnp.bfloat16),
            pltpu.VMEM((rows, width), jnp.float32),
            pltpu.VMEM((rows, width), jnp.float32),
            pltpu.VMEM((width, width), jnp.bfloat16),
            pltpu.SemaphoreType.DMA((WIN, chunks)),
            pltpu.SemaphoreType.DMA((WIN, chunks)),
        ],
        compiler_params=pltpu.CompilerParams(
            collective_id=0, has_side_effects=True, vmem_limit_bytes=56 * 1024 * 1024
        ),
    )(proj, other, stream, out_space, gain, qkv_time, out_time)


def local(
    patches,
    patch_weight,
    conv_taps,
    gain_space,
    qkv_space,
    out_space,
    gain_time,
    qkv_time,
    out_time,
):
    frames, zdev, grid, _, patch = patches.shape
    width = patch_weight.shape[1]
    tokens = zdev * grid * grid
    embed = jnp.dot(
        patches.reshape(-1, patch), patch_weight, preferred_element_type=jnp.float32
    ).astype(jnp.bfloat16)
    embed = embed.reshape(frames, zdev, grid, grid, width)
    padded = extended(embed, (("tok", 1),), 1)
    padded = jnp.pad(padded, ((0, 0), (0, 0), (1, 1), (1, 1), (0, 0)))
    conv = jnp.zeros((frames, zdev, grid, grid, width), jnp.float32)
    for dz in range(3):
        for dy in range(3):
            for dx in range(3):
                tap = conv_taps[9 * dz + 3 * dy + dx].astype(jnp.float32)
                conv = conv + tap * padded[
                    :, dz : dz + zdev, dy : dy + grid, dx : dx + grid
                ].astype(jnp.float32)
    stream = (embed.astype(jnp.float32) + conv).astype(jnp.bfloat16).reshape(frames, tokens, width)
    normed = rms_scale(stream.astype(jnp.float32), gain_space).astype(jnp.bfloat16)
    proj = jnp.dot(normed.reshape(-1, width), qkv_space, preferred_element_type=jnp.float32).astype(
        jnp.bfloat16
    )
    proj = proj.reshape(frames, tokens, 3 * width)
    own_kv = proj[0, :, width:]
    count = lax.axis_size("tok")
    other_kv = lax.ppermute(own_kv, "tok", [(i, (i + 1) % count) for i in range(count)])
    output = block_tail(
        proj[0], other_kv, stream.reshape(-1, width), out_space, gain_time, qkv_time, out_time
    )
    return output.reshape(frames, zdev, grid, grid, width)


def solution(mesh):
    placed = (P("tm", "tok", None, None, None), P(), P(), P(), P(), P(), P(), P(), P())
    return jax.shard_map(
        local,
        mesh=mesh,
        in_specs=placed,
        out_specs=P("tm", "tok", None, None, None),
        check_vma=False,
    )
```

```python
import jax
import jax.numpy as jnp
from jax import lax
from jax.sharding import PartitionSpec as P
from jax.experimental import pallas as pl
from jax.experimental.pallas import tpu as pltpu
import functools

D = 512
H = 8
WIN = 4


def extended(block, sides, width):
    for axis, dim in sides:
        count = lax.axis_size(axis)
        forward = [(i, i + 1) for i in range(count - 1)]
        backward = [(target, source) for source, target in forward]
        low = lax.ppermute(
            lax.slice_in_dim(block, block.shape[dim] - width, None, axis=dim), axis, forward
        )
        high = lax.ppermute(lax.slice_in_dim(block, 0, width, axis=dim), axis, backward)
        block = jnp.concatenate([low, block, high], axis=dim)
    return block


def from_behind(value, axis, steps):
    count = lax.axis_size(axis)
    leading, last = (max(0, -steps), min(count, count - steps))
    return lax.ppermute(value, axis, [(source, source + steps) for source in range(leading, last)])


def rms_scale(values, gain):
    mean_sq = jnp.mean(values * values, axis=-1, keepdims=True)
    return values * lax.rsqrt(mean_sq + 1e-06) * gain.astype(jnp.float32)


def split_heads(block, count, head_size):
    return block.reshape(block.shape[0], count, head_size).transpose(1, 0, 2)


def attend(query, keys, values):
    rows, cols = query.shape
    head_size = D // H
    count = cols // head_size
    scale = head_size ** (-0.5)

    def one_head(parts):
        q_one, k_one, v_one = parts
        scores = jnp.dot(q_one, k_one.T, preferred_element_type=jnp.float32) * scale
        expo = jnp.exp(scores)
        mixed = jnp.dot(expo.astype(jnp.bfloat16), v_one, preferred_element_type=jnp.float32)
        return (mixed / jnp.sum(expo, axis=-1, keepdims=True)).astype(jnp.bfloat16)

    parts = (
        split_heads(query, count, head_size),
        split_heads(keys, count, head_size),
        split_heads(values, count, head_size),
    )
    result = lax.map(one_head, parts)
    return result.transpose(1, 0, 2).reshape(rows, cols)


def block_kernel(
    chunks, group, proj_ref, other_ref, stream_ref, wo_ref, gain_ref, wt_ref,
    out_ref, stream2_ref, own, query2, hist, mixed, total, sum_ref, send_first, recv_first, send_sem, recv_sem,
):
    me = lax.axis_index("tm")
    count = lax.axis_size("tm")
    core = lax.axis_index("tok")
    has_left = me > 0
    has_right = me < count - 1
    rows_all, width = own.shape
    rows = rows_all // chunks
    head_size = width // H
    scale = head_size ** (-0.5)
    lanes = 2 * head_size
    mesh_ids = pl.DeviceIdType.MESH

    @pl.when(jnp.logical_not(has_left))
    def _():
        hist[...] = jnp.zeros_like(hist)

    barrier = pltpu.get_barrier_semaphore()

    @pl.when(has_left)
    def _():
        pl.semaphore_signal(barrier, inc=1, device_id=(me - 1, core), device_id_type=mesh_ids)

    @pl.when(has_right)
    def _():
        pl.semaphore_signal(barrier, inc=1, device_id=(me + 1, core), device_id_type=mesh_ids)

    @pl.when(jnp.logical_and(has_left, has_right))
    def _():
        pl.semaphore_wait(barrier, 2)

    @pl.when(jnp.logical_xor(has_left, has_right))
    def _():
        pl.semaphore_wait(barrier, 1)

    def span_of(piece):
        return pl.ds(pl.multiple_of(piece * rows, 8), rows)

    def copy_of(hop, piece):
        if hop == 0:
            span = span_of(piece)
            source = own.at[span]
            sems = (send_first.at[piece], recv_first.at[piece])
        else:
            span = pl.ds(pl.multiple_of(piece * rows * group, 8), rows * group)
            source = hist.at[hop - 1, span]
            sems = (send_sem.at[hop - 1, piece], recv_sem.at[hop - 1, piece])
        return pltpu.make_async_remote_copy(
            src_ref=source,
            dst_ref=hist.at[hop, span],
            send_sem=sems[0],
            recv_sem=sems[1],
            device_id=(me + 1, core),
            device_id_type=mesh_ids,
        )

    lane = lax.broadcasted_iota(jnp.int32, (1, lanes), 1)
    first_half = lane < head_size
    heads = lax.broadcasted_iota(jnp.int32, (width, width), 0) // head_size
    same_head = heads == lax.broadcasted_iota(jnp.int32, (width, width), 1) // head_size
    sum_ref[...] = same_head.astype(jnp.bfloat16)

    def space_step(piece, carry):
        span = span_of(piece)
        pieces = []
        for pair in range(width // lanes):
            cols = slice(pair * lanes, (pair + 1) * lanes)
            q = proj_ref[span, cols]
            key_cols = slice(width + pair * lanes, width + (pair + 1) * lanes)
            value_cols = slice(2 * width + pair * lanes, 2 * width + (pair + 1) * lanes)
            sources = (
                (proj_ref[:, key_cols], proj_ref[:, value_cols]),
                (other_ref[:, cols], other_ref[:, key_cols]),
            )
            outs = []
            for mask in (first_half, jnp.logical_not(first_half)):
                q_one = jnp.where(mask, q, jnp.zeros_like(q))
                rowsum = None
                mixed_one = None
                for k, v in sources:
                    scores = lax.dot_general(
                        q_one, k, (((1,), (1,)), ((), ())), preferred_element_type=jnp.float32
                    ) * scale
                    expo = jnp.exp(scores)
                    part_sum = jnp.sum(expo, axis=-1, keepdims=True)
                    part = jnp.dot(
                        expo.astype(jnp.bfloat16), v, preferred_element_type=jnp.float32
                    )
                    rowsum = part_sum if rowsum is None else rowsum + part_sum
                    mixed_one = part if mixed_one is None else mixed_one + part
                outs.append(mixed_one / rowsum)
            pieces.append(jnp.where(first_half, outs[0], outs[1]).astype(jnp.bfloat16))
        spatial = jnp.concatenate(pieces, axis=1)
        stream2 = (
            stream_ref[span, :].astype(jnp.float32)
            + jnp.dot(spatial, wo_ref[...], preferred_element_type=jnp.float32)
        ).astype(jnp.bfloat16)
        stream2_ref[span, :] = stream2
        values = stream2.astype(jnp.float32)
        mean_sq = jnp.mean(values * values, axis=-1, keepdims=True)
        normed2 = (values * lax.rsqrt(mean_sq + 1e-06) * gain_ref[...]).astype(jnp.bfloat16)
        own[span, :] = normed2
        query2[span, :] = jnp.dot(
            normed2, wt_ref[:, :width], preferred_element_type=jnp.float32
        ).astype(jnp.bfloat16)

        @pl.when(jnp.logical_and(has_right, piece >= 1))
        def _():
            copy_of(0, piece - 1).start()

        return carry

    lax.fori_loop(0, chunks, space_step, 0)

    def add_term(block, span, valid, first):
        kv = jnp.dot(block, wt_ref[:, width:], preferred_element_type=jnp.float32).astype(jnp.bfloat16)
        keys2 = kv[:, :width].astype(jnp.float32)
        values2 = kv[:, width:].astype(jnp.float32)
        prod = query2[span, :].astype(jnp.float32) * keys2
        high = prod.astype(jnp.bfloat16)
        low = (prod - high.astype(jnp.float32)).astype(jnp.bfloat16)
        summer = sum_ref[...]
        scores = (
            jnp.dot(high, summer, preferred_element_type=jnp.float32)
            + jnp.dot(low, summer, preferred_element_type=jnp.float32)
        ) * scale
        expo = jnp.where(valid, jnp.exp(scores), 0.0)
        part = expo.astype(jnp.bfloat16).astype(jnp.float32) * values2
        if first:
            mixed[span, :] = part
            total[span, :] = expo
        else:
            mixed[span, :] += part
            total[span, :] += expo

    def own_step(piece, carry):
        span = span_of(piece)
        add_term(own[span, :], span, True, True)
        return carry

    lax.fori_loop(0, chunks, own_step, 0)

    @pl.when(has_right)
    def _():
        copy_of(0, chunks - 1).start()

    def first_step(piece, carry):
        span = span_of(piece)

        @pl.when(has_left)
        def _():
            copy_of(0, piece).wait_recv()

        @pl.when(jnp.logical_and(has_right, piece % group == group - 1))
        def _():
            copy_of(1, piece // group).start()

        add_term(hist[0, span, :], span, me - 1 >= 0, False)
        return carry

    lax.fori_loop(0, chunks, first_step, 0)

    for hop in range(1, WIN):
        def hop_step(piece, carry, hop=hop):
            @pl.when(has_left)
            def _():
                copy_of(hop, piece).wait_recv()

            if hop + 1 < WIN:
                @pl.when(has_right)
                def _():
                    copy_of(hop + 1, piece).start()

            for part in range(group):
                span = span_of(piece * group + part)
                add_term(hist[hop, span, :], span, me - (hop + 1) >= 0, False)
            return carry

        lax.fori_loop(0, chunks // group, hop_step, 0)

    @pl.when(has_right)
    def _():
        for piece in range(chunks):
            copy_of(0, piece).wait_send()
        for hop in range(1, WIN):
            for piece in range(chunks // group):
                copy_of(hop, piece).wait_send()

    out_ref[...] = (mixed[...] / total[...]).astype(out_ref.dtype)


def block_tail(proj, other, stream, out_space, gain_time, qkv_time, chunks=6, group=3):
    rows, width = stream.shape
    gain = gain_time.astype(jnp.float32).reshape(1, width)
    vmem = pl.BlockSpec(memory_space=pltpu.VMEM)
    plane = jax.ShapeDtypeStruct((rows, width), jnp.bfloat16)
    return pl.pallas_call(
        functools.partial(block_kernel, chunks, group),
        out_shape=(plane, plane),
        in_specs=[vmem] * 6,
        out_specs=(vmem, vmem),
        scratch_shapes=[
            pltpu.VMEM((rows, width), jnp.bfloat16),
            pltpu.VMEM((rows, width), jnp.bfloat16),
            pltpu.VMEM((WIN, rows, width), jnp.bfloat16),
            pltpu.VMEM((rows, width), jnp.float32),
            pltpu.VMEM((rows, width), jnp.float32),
            pltpu.VMEM((width, width), jnp.bfloat16),
            pltpu.SemaphoreType.DMA((chunks,)),
            pltpu.SemaphoreType.DMA((chunks,)),
            pltpu.SemaphoreType.DMA((WIN - 1, chunks // group)),
            pltpu.SemaphoreType.DMA((WIN - 1, chunks // group)),
        ],
        compiler_params=pltpu.CompilerParams(
            collective_id=0, has_side_effects=True, vmem_limit_bytes=56 * 1024 * 1024
        ),
    )(proj, other, stream, out_space, gain, qkv_time)


def local(
    patches,
    patch_weight,
    conv_taps,
    gain_space,
    qkv_space,
    out_space,
    gain_time,
    qkv_time,
    out_time,
):
    frames, zdev, grid, _, patch = patches.shape
    width = patch_weight.shape[1]
    tokens = zdev * grid * grid
    embed = jnp.dot(
        patches.reshape(-1, patch), patch_weight, preferred_element_type=jnp.float32
    ).astype(jnp.bfloat16)
    embed = embed.reshape(frames, zdev, grid, grid, width)
    padded = extended(embed, (("tok", 1),), 1)
    padded = jnp.pad(padded, ((0, 0), (0, 0), (1, 1), (1, 1), (0, 0)))
    conv = jnp.zeros((frames, zdev, grid, grid, width), jnp.float32)
    for dz in range(3):
        for dy in range(3):
            for dx in range(3):
                tap = conv_taps[9 * dz + 3 * dy + dx].astype(jnp.float32)
                conv = conv + tap * padded[
                    :, dz : dz + zdev, dy : dy + grid, dx : dx + grid
                ].astype(jnp.float32)
    stream = (embed.astype(jnp.float32) + conv).astype(jnp.bfloat16).reshape(frames, tokens, width)
    normed = rms_scale(stream.astype(jnp.float32), gain_space).astype(jnp.bfloat16)
    proj = jnp.dot(normed.reshape(-1, width), qkv_space, preferred_element_type=jnp.float32).astype(
        jnp.bfloat16
    )
    proj = proj.reshape(frames, tokens, 3 * width)
    own_kv = proj[0, :, width:]
    count = lax.axis_size("tok")
    other_kv = lax.ppermute(own_kv, "tok", [(i, (i + 1) % count) for i in range(count)])
    temporal, stream2 = block_tail(
        proj[0], other_kv, stream.reshape(-1, width), out_space, gain_time, qkv_time
    )
    time_proj = jnp.dot(
        temporal.reshape(-1, width), out_time, preferred_element_type=jnp.float32
    ).reshape(frames, tokens, width)
    output = (stream2.astype(jnp.float32) + time_proj).astype(jnp.bfloat16)
    return output.reshape(frames, zdev, grid, grid, width)


def solution(mesh):
    placed = (P("tm", "tok", None, None, None), P(), P(), P(), P(), P(), P(), P(), P())
    return jax.shard_map(
        local,
        mesh=mesh,
        in_specs=placed,
        out_specs=P("tm", "tok", None, None, None),
        check_vma=False,
    )
```

```python
import jax
import jax.numpy as jnp
from jax import lax
from jax.sharding import PartitionSpec as P
from jax.experimental import pallas as pl
from jax.experimental.pallas import tpu as pltpu
import functools

D = 512
H = 8
WIN = 4


def extended(block, sides, width):
    for axis, dim in sides:
        count = lax.axis_size(axis)
        forward = [(i, i + 1) for i in range(count - 1)]
        backward = [(target, source) for source, target in forward]
        low = lax.ppermute(
            lax.slice_in_dim(block, block.shape[dim] - width, None, axis=dim), axis, forward
        )
        high = lax.ppermute(lax.slice_in_dim(block, 0, width, axis=dim), axis, backward)
        block = jnp.concatenate([low, block, high], axis=dim)
    return block


def from_behind(value, axis, steps):
    count = lax.axis_size(axis)
    leading, last = (max(0, -steps), min(count, count - steps))
    return lax.ppermute(value, axis, [(source, source + steps) for source in range(leading, last)])


def rms_scale(values, gain):
    mean_sq = jnp.mean(values * values, axis=-1, keepdims=True)
    return values * lax.rsqrt(mean_sq + 1e-06) * gain.astype(jnp.float32)


def split_heads(block, count, head_size):
    return block.reshape(block.shape[0], count, head_size).transpose(1, 0, 2)


def attend(query, keys, values):
    rows, cols = query.shape
    head_size = D // H
    count = cols // head_size
    scale = head_size ** (-0.5)

    def one_head(parts):
        q_one, k_one, v_one = parts
        scores = jnp.dot(q_one, k_one.T, preferred_element_type=jnp.float32) * scale
        expo = jnp.exp(scores)
        mixed = jnp.dot(expo.astype(jnp.bfloat16), v_one, preferred_element_type=jnp.float32)
        return (mixed / jnp.sum(expo, axis=-1, keepdims=True)).astype(jnp.bfloat16)

    parts = (
        split_heads(query, count, head_size),
        split_heads(keys, count, head_size),
        split_heads(values, count, head_size),
    )
    result = lax.map(one_head, parts)
    return result.transpose(1, 0, 2).reshape(rows, cols)


def block_kernel(
    chunks, proj_ref, other_ref, stream_ref, wo_ref, gain_ref, wt_ref,
    out_ref, stream2_ref, own, query2, hist, mixed, total, sum_ref, send_sem, recv_sem,
):
    me = lax.axis_index("tm")
    count = lax.axis_size("tm")
    core = lax.axis_index("tok")
    has_left = me > 0
    has_right = me < count - 1
    rows_all, width = own.shape
    rows = rows_all // chunks
    head_size = width // H
    scale = head_size ** (-0.5)
    lanes = 2 * head_size
    mesh_ids = pl.DeviceIdType.MESH

    @pl.when(jnp.logical_not(has_left))
    def _():
        hist[...] = jnp.zeros_like(hist)

    barrier = pltpu.get_barrier_semaphore()

    @pl.when(has_left)
    def _():
        pl.semaphore_signal(barrier, inc=1, device_id=(me - 1, core), device_id_type=mesh_ids)

    @pl.when(has_right)
    def _():
        pl.semaphore_signal(barrier, inc=1, device_id=(me + 1, core), device_id_type=mesh_ids)

    @pl.when(jnp.logical_and(has_left, has_right))
    def _():
        pl.semaphore_wait(barrier, 2)

    @pl.when(jnp.logical_xor(has_left, has_right))
    def _():
        pl.semaphore_wait(barrier, 1)

    def span_of(piece):
        return pl.ds(pl.multiple_of(piece * rows, 8), rows)

    def copy_of(hop, piece):
        span = span_of(piece)
        source = own.at[span] if hop == 0 else hist.at[hop - 1, span]
        return pltpu.make_async_remote_copy(
            src_ref=source,
            dst_ref=hist.at[hop, span],
            send_sem=send_sem.at[hop, piece],
            recv_sem=recv_sem.at[hop, piece],
            device_id=(me + 1, core),
            device_id_type=mesh_ids,
        )

    lane = lax.broadcasted_iota(jnp.int32, (1, lanes), 1)
    first_half = lane < head_size
    heads = lax.broadcasted_iota(jnp.int32, (width, width), 0) // head_size
    same_head = heads == lax.broadcasted_iota(jnp.int32, (width, width), 1) // head_size
    sum_ref[...] = same_head.astype(jnp.bfloat16)

    def add_term(block, span, valid, first):
        kv = jnp.dot(block, wt_ref[:, width:], preferred_element_type=jnp.float32).astype(jnp.bfloat16)
        keys2 = kv[:, :width].astype(jnp.float32)
        values2 = kv[:, width:].astype(jnp.float32)
        prod = query2[span, :].astype(jnp.float32) * keys2
        high = prod.astype(jnp.bfloat16)
        low = (prod - high.astype(jnp.float32)).astype(jnp.bfloat16)
        summer = sum_ref[...]
        scores = (
            jnp.dot(high, summer, preferred_element_type=jnp.float32)
            + jnp.dot(low, summer, preferred_element_type=jnp.float32)
        ) * scale
        expo = jnp.where(valid, jnp.exp(scores), 0.0)
        part = expo.astype(jnp.bfloat16).astype(jnp.float32) * values2
        if first:
            mixed[span, :] = part
            total[span, :] = expo
        else:
            mixed[span, :] += part
            total[span, :] += expo

    def space_step(piece, carry):
        span = span_of(piece)
        pieces = []
        for pair in range(width // lanes):
            cols = slice(pair * lanes, (pair + 1) * lanes)
            q = proj_ref[span, cols]
            key_cols = slice(width + pair * lanes, width + (pair + 1) * lanes)
            value_cols = slice(2 * width + pair * lanes, 2 * width + (pair + 1) * lanes)
            sources = (
                (proj_ref[:, key_cols], proj_ref[:, value_cols]),
                (other_ref[:, cols], other_ref[:, key_cols]),
            )
            outs = []
            for mask in (first_half, jnp.logical_not(first_half)):
                q_one = jnp.where(mask, q, jnp.zeros_like(q))
                rowsum = None
                mixed_one = None
                for k, v in sources:
                    scores = lax.dot_general(
                        q_one, k, (((1,), (1,)), ((), ())), preferred_element_type=jnp.float32
                    ) * scale
                    expo = jnp.exp(scores)
                    part_sum = jnp.sum(expo, axis=-1, keepdims=True)
                    part = jnp.dot(
                        expo.astype(jnp.bfloat16), v, preferred_element_type=jnp.float32
                    )
                    rowsum = part_sum if rowsum is None else rowsum + part_sum
                    mixed_one = part if mixed_one is None else mixed_one + part
                outs.append(mixed_one / rowsum)
            pieces.append(jnp.where(first_half, outs[0], outs[1]).astype(jnp.bfloat16))
        spatial = jnp.concatenate(pieces, axis=1)
        stream2 = (
            stream_ref[span, :].astype(jnp.float32)
            + jnp.dot(spatial, wo_ref[...], preferred_element_type=jnp.float32)
        ).astype(jnp.bfloat16)
        stream2_ref[span, :] = stream2
        values = stream2.astype(jnp.float32)
        mean_sq = jnp.mean(values * values, axis=-1, keepdims=True)
        normed2 = (values * lax.rsqrt(mean_sq + 1e-06) * gain_ref[...]).astype(jnp.bfloat16)
        own[span, :] = normed2
        query2[span, :] = jnp.dot(
            normed2, wt_ref[:, :width], preferred_element_type=jnp.float32
        ).astype(jnp.bfloat16)

        add_term(own[span, :], span, True, True)

        @pl.when(has_right)
        def _():
            copy_of(0, piece).start()

        return carry

    lax.fori_loop(0, chunks, space_step, 0)

    for hop in range(WIN):
        def hop_step(piece, carry, hop=hop):
            span = span_of(piece)

            @pl.when(has_left)
            def _():
                copy_of(hop, piece).wait_recv()

            if hop + 1 < WIN:
                @pl.when(has_right)
                def _():
                    copy_of(hop + 1, piece).start()

            add_term(hist[hop, span, :], span, me - (hop + 1) >= 0, False)
            return carry

        lax.fori_loop(0, chunks, hop_step, 0)

    @pl.when(has_right)
    def _():
        for hop in range(WIN):
            for piece in range(chunks):
                copy_of(hop, piece).wait_send()

    out_ref[...] = (mixed[...] / total[...]).astype(out_ref.dtype)


def block_tail(proj, other, stream, out_space, gain_time, qkv_time, chunks=6):
    rows, width = stream.shape
    gain = gain_time.astype(jnp.float32).reshape(1, width)
    vmem = pl.BlockSpec(memory_space=pltpu.VMEM)
    plane = jax.ShapeDtypeStruct((rows, width), jnp.bfloat16)
    return pl.pallas_call(
        functools.partial(block_kernel, chunks),
        out_shape=(plane, plane),
        in_specs=[vmem] * 6,
        out_specs=(vmem, vmem),
        scratch_shapes=[
            pltpu.VMEM((rows, width), jnp.bfloat16),
            pltpu.VMEM((rows, width), jnp.bfloat16),
            pltpu.VMEM((WIN, rows, width), jnp.bfloat16),
            pltpu.VMEM((rows, width), jnp.float32),
            pltpu.VMEM((rows, width), jnp.float32),
            pltpu.VMEM((width, width), jnp.bfloat16),
            pltpu.SemaphoreType.DMA((WIN, chunks)),
            pltpu.SemaphoreType.DMA((WIN, chunks)),
        ],
        compiler_params=pltpu.CompilerParams(
            collective_id=0, has_side_effects=True, vmem_limit_bytes=56 * 1024 * 1024
        ),
    )(proj, other, stream, out_space, gain, qkv_time)


def local(
    patches,
    patch_weight,
    conv_taps,
    gain_space,
    qkv_space,
    out_space,
    gain_time,
    qkv_time,
    out_time,
):
    frames, zdev, grid, _, patch = patches.shape
    width = patch_weight.shape[1]
    tokens = zdev * grid * grid
    embed = jnp.dot(
        patches.reshape(-1, patch), patch_weight, preferred_element_type=jnp.float32
    ).astype(jnp.bfloat16)
    embed = embed.reshape(frames, zdev, grid, grid, width)
    padded = extended(embed, (("tok", 1),), 1)
    padded = jnp.pad(padded, ((0, 0), (0, 0), (1, 1), (1, 1), (0, 0)))
    conv = jnp.zeros((frames, zdev, grid, grid, width), jnp.float32)
    for dz in range(3):
        for dy in range(3):
            for dx in range(3):
                tap = conv_taps[9 * dz + 3 * dy + dx].astype(jnp.float32)
                conv = conv + tap * padded[
                    :, dz : dz + zdev, dy : dy + grid, dx : dx + grid
                ].astype(jnp.float32)
    stream = (embed.astype(jnp.float32) + conv).astype(jnp.bfloat16).reshape(frames, tokens, width)
    normed = rms_scale(stream.astype(jnp.float32), gain_space).astype(jnp.bfloat16)
    proj = jnp.dot(normed.reshape(-1, width), qkv_space, preferred_element_type=jnp.float32).astype(
        jnp.bfloat16
    )
    proj = proj.reshape(frames, tokens, 3 * width)
    own_kv = proj[0, :, width:]
    count = lax.axis_size("tok")
    other_kv = lax.ppermute(own_kv, "tok", [(i, (i + 1) % count) for i in range(count)])
    temporal, stream2 = block_tail(
        proj[0], other_kv, stream.reshape(-1, width), out_space, gain_time, qkv_time
    )
    time_proj = jnp.dot(
        temporal.reshape(-1, width), out_time, preferred_element_type=jnp.float32
    ).reshape(frames, tokens, width)
    output = (stream2.astype(jnp.float32) + time_proj).astype(jnp.bfloat16)
    return output.reshape(frames, zdev, grid, grid, width)


def solution(mesh):
    placed = (P("tm", "tok", None, None, None), P(), P(), P(), P(), P(), P(), P(), P())
    return jax.shard_map(
        local,
        mesh=mesh,
        in_specs=placed,
        out_specs=P("tm", "tok", None, None, None),
        check_vma=False,
    )
```

```python
import jax
import jax.numpy as jnp
from jax import lax
from jax.sharding import PartitionSpec as P
from jax.experimental import pallas as pl
from jax.experimental.pallas import tpu as pltpu
import functools

D = 512
H = 8
WIN = 4


def extended(block, sides, width):
    for axis, dim in sides:
        count = lax.axis_size(axis)
        forward = [(i, i + 1) for i in range(count - 1)]
        backward = [(target, source) for source, target in forward]
        low = lax.ppermute(
            lax.slice_in_dim(block, block.shape[dim] - width, None, axis=dim), axis, forward
        )
        high = lax.ppermute(lax.slice_in_dim(block, 0, width, axis=dim), axis, backward)
        block = jnp.concatenate([low, block, high], axis=dim)
    return block


def from_behind(value, axis, steps):
    count = lax.axis_size(axis)
    leading, last = (max(0, -steps), min(count, count - steps))
    return lax.ppermute(value, axis, [(source, source + steps) for source in range(leading, last)])


def rms_scale(values, gain):
    mean_sq = jnp.mean(values * values, axis=-1, keepdims=True)
    return values * lax.rsqrt(mean_sq + 1e-06) * gain.astype(jnp.float32)


def split_heads(block, count, head_size):
    return block.reshape(block.shape[0], count, head_size).transpose(1, 0, 2)


def attend(query, keys, values):
    rows, cols = query.shape
    head_size = D // H
    count = cols // head_size
    scale = head_size ** (-0.5)

    def one_head(parts):
        q_one, k_one, v_one = parts
        scores = jnp.dot(q_one, k_one.T, preferred_element_type=jnp.float32) * scale
        expo = jnp.exp(scores)
        mixed = jnp.dot(expo.astype(jnp.bfloat16), v_one, preferred_element_type=jnp.float32)
        return (mixed / jnp.sum(expo, axis=-1, keepdims=True)).astype(jnp.bfloat16)

    parts = (
        split_heads(query, count, head_size),
        split_heads(keys, count, head_size),
        split_heads(values, count, head_size),
    )
    result = lax.map(one_head, parts)
    return result.transpose(1, 0, 2).reshape(rows, cols)


def conv_kernel(e_ref, t_ref, o_ref):
    planes, rows, lanes_x, width = o_ref.shape

    def plane(z, carry):
        parts = []
        for dx in range(3):
            acc = None
            for dz in range(3):
                for dy in range(3):
                    tap = t_ref[pl.ds(9 * dz + 3 * dy + dx, 1), :]
                    term = e_ref[z + dz, dy:dy + rows] * tap
                    acc = term if acc is None else acc + term
            parts.append(acc)
        conv = (
            pltpu.roll(parts[0], 1, 1) + parts[1] + pltpu.roll(parts[2], lanes_x - 1, 1)
        )
        o_ref[z] = (e_ref[z + 1, 1:1 + rows] + conv).astype(o_ref.dtype)
        return carry

    lax.fori_loop(0, planes, plane, 0)


def depthwise(ext, taps):
    depth, grid, _, width = ext.shape
    planes = depth - 2
    padded = jnp.pad(ext.astype(jnp.float32), ((0, 0), (1, 1), (1, 3), (0, 0)))
    vmem = pl.BlockSpec(memory_space=pltpu.VMEM)
    out = pl.pallas_call(
        conv_kernel,
        out_shape=jax.ShapeDtypeStruct((planes, grid, grid + 4, width), jnp.bfloat16),
        in_specs=[vmem, vmem],
        out_specs=vmem,
        compiler_params=pltpu.CompilerParams(vmem_limit_bytes=32 * 1024 * 1024),
    )(padded, taps.astype(jnp.float32))
    return out[:, :, 1:1 + grid]


def block_kernel(
    chunks, proj_ref, other_ref, stream_ref, wo_ref, gain_ref, wt_ref,
    out_ref, stream2_ref, own, query2, hist, mixed, total, sum_ref, send_sem, recv_sem,
):
    me = lax.axis_index("tm")
    count = lax.axis_size("tm")
    core = lax.axis_index("tok")
    has_left = me > 0
    has_right = me < count - 1
    rows_all, width = own.shape
    rows = rows_all // chunks
    head_size = width // H
    scale = head_size ** (-0.5)
    lanes = 2 * head_size
    mesh_ids = pl.DeviceIdType.MESH

    @pl.when(jnp.logical_not(has_left))
    def _():
        hist[...] = jnp.zeros_like(hist)

    barrier = pltpu.get_barrier_semaphore()

    @pl.when(has_left)
    def _():
        pl.semaphore_signal(barrier, inc=1, device_id=(me - 1, core), device_id_type=mesh_ids)

    @pl.when(has_right)
    def _():
        pl.semaphore_signal(barrier, inc=1, device_id=(me + 1, core), device_id_type=mesh_ids)

    @pl.when(jnp.logical_and(has_left, has_right))
    def _():
        pl.semaphore_wait(barrier, 2)

    @pl.when(jnp.logical_xor(has_left, has_right))
    def _():
        pl.semaphore_wait(barrier, 1)

    def span_of(piece):
        return pl.ds(pl.multiple_of(piece * rows, 8), rows)

    def copy_of(hop, piece):
        span = span_of(piece)
        source = own.at[span] if hop == 0 else hist.at[hop - 1, span]
        return pltpu.make_async_remote_copy(
            src_ref=source,
            dst_ref=hist.at[hop, span],
            send_sem=send_sem.at[hop, piece],
            recv_sem=recv_sem.at[hop, piece],
            device_id=(me + 1, core),
            device_id_type=mesh_ids,
        )

    lane = lax.broadcasted_iota(jnp.int32, (1, lanes), 1)
    first_half = lane < head_size
    heads = lax.broadcasted_iota(jnp.int32, (width, width), 0) // head_size
    same_head = heads == lax.broadcasted_iota(jnp.int32, (width, width), 1) // head_size
    sum_ref[...] = same_head.astype(jnp.bfloat16)

    def add_term(block, span, valid, first):
        kv = jnp.dot(block, wt_ref[:, width:], preferred_element_type=jnp.float32).astype(jnp.bfloat16)
        keys2 = kv[:, :width].astype(jnp.float32)
        values2 = kv[:, width:].astype(jnp.float32)
        prod = query2[span, :].astype(jnp.float32) * keys2
        high = prod.astype(jnp.bfloat16)
        low = (prod - high.astype(jnp.float32)).astype(jnp.bfloat16)
        summer = sum_ref[...]
        scores = (
            jnp.dot(high, summer, preferred_element_type=jnp.float32)
            + jnp.dot(low, summer, preferred_element_type=jnp.float32)
        ) * scale
        expo = jnp.where(valid, jnp.exp(scores), 0.0)
        part = expo.astype(jnp.bfloat16).astype(jnp.float32) * values2
        if first:
            mixed[span, :] = part
            total[span, :] = expo
        else:
            mixed[span, :] += part
            total[span, :] += expo

    def space_step(piece, carry):
        span = span_of(piece)
        pieces = []
        for pair in range(width // lanes):
            cols = slice(pair * lanes, (pair + 1) * lanes)
            q = proj_ref[span, cols]
            key_cols = slice(width + pair * lanes, width + (pair + 1) * lanes)
            value_cols = slice(2 * width + pair * lanes, 2 * width + (pair + 1) * lanes)
            sources = (
                (proj_ref[:, key_cols], proj_ref[:, value_cols]),
                (other_ref[:, cols], other_ref[:, key_cols]),
            )
            outs = []
            for mask in (first_half, jnp.logical_not(first_half)):
                q_one = jnp.where(mask, q, jnp.zeros_like(q))
                rowsum = None
                mixed_one = None
                for k, v in sources:
                    scores = lax.dot_general(
                        q_one, k, (((1,), (1,)), ((), ())), preferred_element_type=jnp.float32
                    ) * scale
                    expo = jnp.exp(scores)
                    part_sum = jnp.sum(expo, axis=-1, keepdims=True)
                    part = jnp.dot(
                        expo.astype(jnp.bfloat16), v, preferred_element_type=jnp.float32
                    )
                    rowsum = part_sum if rowsum is None else rowsum + part_sum
                    mixed_one = part if mixed_one is None else mixed_one + part
                outs.append(mixed_one / rowsum)
            pieces.append(jnp.where(first_half, outs[0], outs[1]).astype(jnp.bfloat16))
        spatial = jnp.concatenate(pieces, axis=1)
        stream2 = (
            stream_ref[span, :].astype(jnp.float32)
            + jnp.dot(spatial, wo_ref[...], preferred_element_type=jnp.float32)
        ).astype(jnp.bfloat16)
        stream2_ref[span, :] = stream2
        values = stream2.astype(jnp.float32)
        mean_sq = jnp.mean(values * values, axis=-1, keepdims=True)
        normed2 = (values * lax.rsqrt(mean_sq + 1e-06) * gain_ref[...]).astype(jnp.bfloat16)
        own[span, :] = normed2
        query2[span, :] = jnp.dot(
            normed2, wt_ref[:, :width], preferred_element_type=jnp.float32
        ).astype(jnp.bfloat16)

        add_term(own[span, :], span, True, True)

        @pl.when(has_right)
        def _():
            copy_of(0, piece).start()

        return carry

    lax.fori_loop(0, chunks, space_step, 0)

    for hop in range(WIN):
        def hop_step(piece, carry, hop=hop):
            span = span_of(piece)

            @pl.when(has_left)
            def _():
                copy_of(hop, piece).wait_recv()

            if hop + 1 < WIN:
                @pl.when(has_right)
                def _():
                    copy_of(hop + 1, piece).start()

            add_term(hist[hop, span, :], span, me - (hop + 1) >= 0, False)
            return carry

        lax.fori_loop(0, chunks, hop_step, 0)

    @pl.when(has_right)
    def _():
        for hop in range(WIN):
            for piece in range(chunks):
                copy_of(hop, piece).wait_send()

    out_ref[...] = (mixed[...] / total[...]).astype(out_ref.dtype)


def block_tail(proj, other, stream, out_space, gain_time, qkv_time, chunks=6):
    rows, width = stream.shape
    gain = gain_time.astype(jnp.float32).reshape(1, width)
    vmem = pl.BlockSpec(memory_space=pltpu.VMEM)
    plane = jax.ShapeDtypeStruct((rows, width), jnp.bfloat16)
    return pl.pallas_call(
        functools.partial(block_kernel, chunks),
        out_shape=(plane, plane),
        in_specs=[vmem] * 6,
        out_specs=(vmem, vmem),
        scratch_shapes=[
            pltpu.VMEM((rows, width), jnp.bfloat16),
            pltpu.VMEM((rows, width), jnp.bfloat16),
            pltpu.VMEM((WIN, rows, width), jnp.bfloat16),
            pltpu.VMEM((rows, width), jnp.float32),
            pltpu.VMEM((rows, width), jnp.float32),
            pltpu.VMEM((width, width), jnp.bfloat16),
            pltpu.SemaphoreType.DMA((WIN, chunks)),
            pltpu.SemaphoreType.DMA((WIN, chunks)),
        ],
        compiler_params=pltpu.CompilerParams(
            collective_id=0, has_side_effects=True, vmem_limit_bytes=56 * 1024 * 1024
        ),
    )(proj, other, stream, out_space, gain, qkv_time)


def local(
    patches,
    patch_weight,
    conv_taps,
    gain_space,
    qkv_space,
    out_space,
    gain_time,
    qkv_time,
    out_time,
):
    frames, zdev, grid, _, patch = patches.shape
    width = patch_weight.shape[1]
    tokens = zdev * grid * grid
    embed = jnp.dot(
        patches.reshape(-1, patch), patch_weight, preferred_element_type=jnp.float32
    ).astype(jnp.bfloat16)
    embed = embed.reshape(frames, zdev, grid, grid, width)
    padded = extended(embed, (("tok", 1),), 1)
    stream = depthwise(padded[0], conv_taps).reshape(frames, tokens, width)
    normed = rms_scale(stream.astype(jnp.float32), gain_space).astype(jnp.bfloat16)
    proj = jnp.dot(normed.reshape(-1, width), qkv_space, preferred_element_type=jnp.float32).astype(
        jnp.bfloat16
    )
    proj = proj.reshape(frames, tokens, 3 * width)
    own_kv = proj[0, :, width:]
    count = lax.axis_size("tok")
    other_kv = lax.ppermute(own_kv, "tok", [(i, (i + 1) % count) for i in range(count)])
    temporal, stream2 = block_tail(
        proj[0], other_kv, stream.reshape(-1, width), out_space, gain_time, qkv_time
    )
    time_proj = jnp.dot(
        temporal.reshape(-1, width), out_time, preferred_element_type=jnp.float32
    ).reshape(frames, tokens, width)
    output = (stream2.astype(jnp.float32) + time_proj).astype(jnp.bfloat16)
    return output.reshape(frames, zdev, grid, grid, width)


def solution(mesh):
    placed = (P("tm", "tok", None, None, None), P(), P(), P(), P(), P(), P(), P(), P())
    return jax.shard_map(
        local,
        mesh=mesh,
        in_specs=placed,
        out_specs=P("tm", "tok", None, None, None),
        check_vma=False,
    )
```

```python
import jax
import jax.numpy as jnp
from jax import lax
from jax.sharding import PartitionSpec as P
from jax.experimental import pallas as pl
from jax.experimental.pallas import tpu as pltpu
import functools

D = 512
H = 8
WIN = 4


def extended(block, sides, width):
    for axis, dim in sides:
        count = lax.axis_size(axis)
        forward = [(i, i + 1) for i in range(count - 1)]
        backward = [(target, source) for source, target in forward]
        low = lax.ppermute(
            lax.slice_in_dim(block, block.shape[dim] - width, None, axis=dim), axis, forward
        )
        high = lax.ppermute(lax.slice_in_dim(block, 0, width, axis=dim), axis, backward)
        block = jnp.concatenate([low, block, high], axis=dim)
    return block


def from_behind(value, axis, steps):
    count = lax.axis_size(axis)
    leading, last = (max(0, -steps), min(count, count - steps))
    return lax.ppermute(value, axis, [(source, source + steps) for source in range(leading, last)])


def rms_scale(values, gain):
    mean_sq = jnp.mean(values * values, axis=-1, keepdims=True)
    return values * lax.rsqrt(mean_sq + 1e-06) * gain.astype(jnp.float32)


def split_heads(block, count, head_size):
    return block.reshape(block.shape[0], count, head_size).transpose(1, 0, 2)


def attend(query, keys, values):
    rows, cols = query.shape
    head_size = D // H
    count = cols // head_size
    scale = head_size ** (-0.5)

    def one_head(parts):
        q_one, k_one, v_one = parts
        scores = jnp.dot(q_one, k_one.T, preferred_element_type=jnp.float32) * scale
        expo = jnp.exp(scores)
        mixed = jnp.dot(expo.astype(jnp.bfloat16), v_one, preferred_element_type=jnp.float32)
        return (mixed / jnp.sum(expo, axis=-1, keepdims=True)).astype(jnp.bfloat16)

    parts = (
        split_heads(query, count, head_size),
        split_heads(keys, count, head_size),
        split_heads(values, count, head_size),
    )
    result = lax.map(one_head, parts)
    return result.transpose(1, 0, 2).reshape(rows, cols)


def conv_kernel(e_ref, t_ref, o_ref):
    planes, rows, lanes_x, width = o_ref.shape

    def plane(z, carry):
        parts = []
        for dx in range(3):
            acc = None
            for dz in range(3):
                for dy in range(3):
                    tap = t_ref[pl.ds(9 * dz + 3 * dy + dx, 1), :]
                    term = e_ref[z + dz, dy:dy + rows] * tap
                    acc = term if acc is None else acc + term
            parts.append(acc)
        conv = (
            pltpu.roll(parts[0], 1, 1) + parts[1] + pltpu.roll(parts[2], lanes_x - 1, 1)
        )
        o_ref[z] = (e_ref[z + 1, 1:1 + rows] + conv).astype(o_ref.dtype)
        return carry

    lax.fori_loop(0, planes, plane, 0)


def depthwise(ext, taps):
    depth, grid, _, width = ext.shape
    planes = depth - 2
    padded = jnp.pad(ext.astype(jnp.float32), ((0, 0), (1, 1), (1, 3), (0, 0)))
    vmem = pl.BlockSpec(memory_space=pltpu.VMEM)
    out = pl.pallas_call(
        conv_kernel,
        out_shape=jax.ShapeDtypeStruct((planes, grid, grid + 4, width), jnp.bfloat16),
        in_specs=[vmem, vmem],
        out_specs=vmem,
        compiler_params=pltpu.CompilerParams(vmem_limit_bytes=32 * 1024 * 1024),
    )(padded, taps.astype(jnp.float32))
    return out[:, :, 1:1 + grid]


def block_kernel(
    chunks, q_ref, kv_ref, other_ref, stream_ref, wo_ref, gain_ref, wt_ref,
    out_ref, stream2_ref, own, query2, hist, mixed, total, sum_ref, send_sem, recv_sem,
):
    me = lax.axis_index("tm")
    count = lax.axis_size("tm")
    core = lax.axis_index("tok")
    has_left = me > 0
    has_right = me < count - 1
    rows_all, width = own.shape
    rows = rows_all // chunks
    head_size = width // H
    scale = head_size ** (-0.5)
    lanes = 2 * head_size
    mesh_ids = pl.DeviceIdType.MESH

    @pl.when(jnp.logical_not(has_left))
    def _():
        hist[...] = jnp.zeros_like(hist)

    barrier = pltpu.get_barrier_semaphore()

    @pl.when(has_left)
    def _():
        pl.semaphore_signal(barrier, inc=1, device_id=(me - 1, core), device_id_type=mesh_ids)

    @pl.when(has_right)
    def _():
        pl.semaphore_signal(barrier, inc=1, device_id=(me + 1, core), device_id_type=mesh_ids)

    @pl.when(jnp.logical_and(has_left, has_right))
    def _():
        pl.semaphore_wait(barrier, 2)

    @pl.when(jnp.logical_xor(has_left, has_right))
    def _():
        pl.semaphore_wait(barrier, 1)

    def span_of(piece):
        return pl.ds(pl.multiple_of(piece * rows, 8), rows)

    def copy_of(hop, piece):
        span = span_of(piece)
        source = own.at[span] if hop == 0 else hist.at[hop - 1, span]
        return pltpu.make_async_remote_copy(
            src_ref=source,
            dst_ref=hist.at[hop, span],
            send_sem=send_sem.at[hop, piece],
            recv_sem=recv_sem.at[hop, piece],
            device_id=(me + 1, core),
            device_id_type=mesh_ids,
        )

    lane = lax.broadcasted_iota(jnp.int32, (1, lanes), 1)
    first_half = lane < head_size
    heads = lax.broadcasted_iota(jnp.int32, (width, width), 0) // head_size
    same_head = heads == lax.broadcasted_iota(jnp.int32, (width, width), 1) // head_size
    sum_ref[...] = same_head.astype(jnp.bfloat16)

    def add_term(block, span, valid, first):
        kv = jnp.dot(block, wt_ref[:, width:], preferred_element_type=jnp.float32).astype(jnp.bfloat16)
        keys2 = kv[:, :width].astype(jnp.float32)
        values2 = kv[:, width:].astype(jnp.float32)
        prod = query2[span, :].astype(jnp.float32) * keys2
        high = prod.astype(jnp.bfloat16)
        low = (prod - high.astype(jnp.float32)).astype(jnp.bfloat16)
        summer = sum_ref[...]
        scores = (
            jnp.dot(high, summer, preferred_element_type=jnp.float32)
            + jnp.dot(low, summer, preferred_element_type=jnp.float32)
        ) * scale
        expo = jnp.where(valid, jnp.exp(scores), 0.0)
        part = expo.astype(jnp.bfloat16).astype(jnp.float32) * values2
        if first:
            mixed[span, :] = part
            total[span, :] = expo
        else:
            mixed[span, :] += part
            total[span, :] += expo

    def space_step(piece, carry):
        span = span_of(piece)
        pieces = []
        for pair in range(width // lanes):
            cols = slice(pair * lanes, (pair + 1) * lanes)
            q = q_ref[span, cols]
            key_cols = slice(width + pair * lanes, width + (pair + 1) * lanes)
            sources = (
                (kv_ref[:, cols], kv_ref[:, key_cols]),
                (other_ref[:, cols], other_ref[:, key_cols]),
            )
            outs = []
            for mask in (first_half, jnp.logical_not(first_half)):
                q_one = jnp.where(mask, q, jnp.zeros_like(q))
                rowsum = None
                mixed_one = None
                for k, v in sources:
                    scores = lax.dot_general(
                        q_one, k, (((1,), (1,)), ((), ())), preferred_element_type=jnp.float32
                    ) * scale
                    expo = jnp.exp(scores)
                    part_sum = jnp.sum(expo, axis=-1, keepdims=True)
                    part = jnp.dot(
                        expo.astype(jnp.bfloat16), v, preferred_element_type=jnp.float32
                    )
                    rowsum = part_sum if rowsum is None else rowsum + part_sum
                    mixed_one = part if mixed_one is None else mixed_one + part
                outs.append(mixed_one / rowsum)
            pieces.append(jnp.where(first_half, outs[0], outs[1]).astype(jnp.bfloat16))
        spatial = jnp.concatenate(pieces, axis=1)
        stream2 = (
            stream_ref[span, :].astype(jnp.float32)
            + jnp.dot(spatial, wo_ref[...], preferred_element_type=jnp.float32)
        ).astype(jnp.bfloat16)
        stream2_ref[span, :] = stream2
        values = stream2.astype(jnp.float32)
        mean_sq = jnp.mean(values * values, axis=-1, keepdims=True)
        normed2 = (values * lax.rsqrt(mean_sq + 1e-06) * gain_ref[...]).astype(jnp.bfloat16)
        own[span, :] = normed2
        query2[span, :] = jnp.dot(
            normed2, wt_ref[:, :width], preferred_element_type=jnp.float32
        ).astype(jnp.bfloat16)

        add_term(own[span, :], span, True, True)

        @pl.when(has_right)
        def _():
            copy_of(0, piece).start()

        return carry

    lax.fori_loop(0, chunks, space_step, 0)

    for hop in range(WIN):
        def hop_step(piece, carry, hop=hop):
            span = span_of(piece)

            @pl.when(has_left)
            def _():
                copy_of(hop, piece).wait_recv()

            if hop + 1 < WIN:
                @pl.when(has_right)
                def _():
                    copy_of(hop + 1, piece).start()

            add_term(hist[hop, span, :], span, me - (hop + 1) >= 0, False)
            return carry

        lax.fori_loop(0, chunks, hop_step, 0)

    @pl.when(has_right)
    def _():
        for hop in range(WIN):
            for piece in range(chunks):
                copy_of(hop, piece).wait_send()

    out_ref[...] = (mixed[...] / total[...]).astype(out_ref.dtype)


def block_tail(query, keys_values, other, stream, out_space, gain_time, qkv_time, chunks=6):
    rows, width = stream.shape
    gain = gain_time.astype(jnp.float32).reshape(1, width)
    vmem = pl.BlockSpec(memory_space=pltpu.VMEM)
    plane = jax.ShapeDtypeStruct((rows, width), jnp.bfloat16)
    return pl.pallas_call(
        functools.partial(block_kernel, chunks),
        out_shape=(plane, plane),
        in_specs=[vmem] * 7,
        out_specs=(vmem, vmem),
        scratch_shapes=[
            pltpu.VMEM((rows, width), jnp.bfloat16),
            pltpu.VMEM((rows, width), jnp.bfloat16),
            pltpu.VMEM((WIN, rows, width), jnp.bfloat16),
            pltpu.VMEM((rows, width), jnp.float32),
            pltpu.VMEM((rows, width), jnp.float32),
            pltpu.VMEM((width, width), jnp.bfloat16),
            pltpu.SemaphoreType.DMA((WIN, chunks)),
            pltpu.SemaphoreType.DMA((WIN, chunks)),
        ],
        compiler_params=pltpu.CompilerParams(
            collective_id=0, has_side_effects=True, vmem_limit_bytes=56 * 1024 * 1024
        ),
    )(query, keys_values, other, stream, out_space, gain, qkv_time)


def local(
    patches,
    patch_weight,
    conv_taps,
    gain_space,
    qkv_space,
    out_space,
    gain_time,
    qkv_time,
    out_time,
):
    frames, zdev, grid, _, patch = patches.shape
    width = patch_weight.shape[1]
    tokens = zdev * grid * grid
    embed = jnp.dot(patches, patch_weight, preferred_element_type=jnp.float32).astype(
        jnp.bfloat16
    )
    padded = extended(embed, (("tok", 1),), 1)
    stream = depthwise(padded[0], conv_taps).reshape(frames, tokens, width)
    normed = rms_scale(stream.astype(jnp.float32), gain_space).astype(jnp.bfloat16)
    flat = normed.reshape(-1, width)
    own_kv = jnp.dot(flat, qkv_space[:, width:], preferred_element_type=jnp.float32).astype(
        jnp.bfloat16
    )
    count = lax.axis_size("tok")
    other_kv = lax.ppermute(own_kv, "tok", [(i, (i + 1) % count) for i in range(count)])
    query = jnp.dot(flat, qkv_space[:, :width], preferred_element_type=jnp.float32).astype(
        jnp.bfloat16
    )
    temporal, stream2 = block_tail(
        query, own_kv, other_kv, stream.reshape(-1, width), out_space, gain_time, qkv_time
    )
    time_proj = jnp.dot(
        temporal.reshape(-1, width), out_time, preferred_element_type=jnp.float32
    ).reshape(frames, tokens, width)
    output = (stream2.astype(jnp.float32) + time_proj).astype(jnp.bfloat16)
    return output.reshape(frames, zdev, grid, grid, width)


def solution(mesh):
    placed = (P("tm", "tok", None, None, None), P(), P(), P(), P(), P(), P(), P(), P())
    return jax.shard_map(
        local,
        mesh=mesh,
        in_specs=placed,
        out_specs=P("tm", "tok", None, None, None),
        check_vma=False,
    )
```

```python
import jax
import jax.numpy as jnp
from jax import lax
from jax.sharding import PartitionSpec as P
from jax.experimental import pallas as pl
from jax.experimental.pallas import tpu as pltpu
import functools

D = 512
H = 8
WIN = 4


def extended(block, sides, width):
    for axis, dim in sides:
        count = lax.axis_size(axis)
        forward = [(i, i + 1) for i in range(count - 1)]
        backward = [(target, source) for source, target in forward]
        low = lax.ppermute(
            lax.slice_in_dim(block, block.shape[dim] - width, None, axis=dim), axis, forward
        )
        high = lax.ppermute(lax.slice_in_dim(block, 0, width, axis=dim), axis, backward)
        block = jnp.concatenate([low, block, high], axis=dim)
    return block


def from_behind(value, axis, steps):
    count = lax.axis_size(axis)
    leading, last = (max(0, -steps), min(count, count - steps))
    return lax.ppermute(value, axis, [(source, source + steps) for source in range(leading, last)])


def rms_scale(values, gain):
    mean_sq = jnp.mean(values * values, axis=-1, keepdims=True)
    return values * lax.rsqrt(mean_sq + 1e-06) * gain.astype(jnp.float32)


def split_heads(block, count, head_size):
    return block.reshape(block.shape[0], count, head_size).transpose(1, 0, 2)


def attend(query, keys, values):
    rows, cols = query.shape
    head_size = D // H
    count = cols // head_size
    scale = head_size ** (-0.5)

    def one_head(parts):
        q_one, k_one, v_one = parts
        scores = jnp.dot(q_one, k_one.T, preferred_element_type=jnp.float32) * scale
        expo = jnp.exp(scores)
        mixed = jnp.dot(expo.astype(jnp.bfloat16), v_one, preferred_element_type=jnp.float32)
        return (mixed / jnp.sum(expo, axis=-1, keepdims=True)).astype(jnp.bfloat16)

    parts = (
        split_heads(query, count, head_size),
        split_heads(keys, count, head_size),
        split_heads(values, count, head_size),
    )
    result = lax.map(one_head, parts)
    return result.transpose(1, 0, 2).reshape(rows, cols)


def conv_kernel(e_ref, t_ref, o_ref):
    planes, rows, lanes_x, width = o_ref.shape

    def plane(z, carry):
        parts = []
        for dx in range(3):
            acc = None
            for dz in range(3):
                for dy in range(3):
                    tap = t_ref[pl.ds(9 * dz + 3 * dy + dx, 1), :]
                    term = e_ref[z + dz, dy:dy + rows] * tap
                    acc = term if acc is None else acc + term
            parts.append(acc)
        conv = (
            pltpu.roll(parts[0], 1, 1) + parts[1] + pltpu.roll(parts[2], lanes_x - 1, 1)
        )
        o_ref[z] = (e_ref[z + 1, 1:1 + rows] + conv).astype(o_ref.dtype)
        return carry

    lax.fori_loop(0, planes, plane, 0)


def depthwise(ext, taps):
    depth, grid, _, width = ext.shape
    planes = depth - 2
    padded = jnp.pad(ext.astype(jnp.float32), ((0, 0), (1, 1), (1, 3), (0, 0)))
    vmem = pl.BlockSpec(memory_space=pltpu.VMEM)
    out = pl.pallas_call(
        conv_kernel,
        out_shape=jax.ShapeDtypeStruct((planes, grid, grid + 4, width), jnp.bfloat16),
        in_specs=[vmem, vmem],
        out_specs=vmem,
        compiler_params=pltpu.CompilerParams(vmem_limit_bytes=32 * 1024 * 1024),
    )(padded, taps.astype(jnp.float32))
    return out[:, :, 1:1 + grid]


def block_kernel(
    chunks, ws_ref, gain_s_ref, kv_ref, other_ref, stream_ref, wo_ref, gain_ref, wt_ref,
    out_ref, stream2_ref, own, query2, hist, mixed, total, sum_ref, send_sem, recv_sem,
):
    me = lax.axis_index("tm")
    count = lax.axis_size("tm")
    core = lax.axis_index("tok")
    has_left = me > 0
    has_right = me < count - 1
    rows_all, width = own.shape
    rows = rows_all // chunks
    head_size = width // H
    scale = head_size ** (-0.5)
    lanes = 2 * head_size
    mesh_ids = pl.DeviceIdType.MESH

    @pl.when(jnp.logical_not(has_left))
    def _():
        hist[...] = jnp.zeros_like(hist)

    barrier = pltpu.get_barrier_semaphore()

    @pl.when(has_left)
    def _():
        pl.semaphore_signal(barrier, inc=1, device_id=(me - 1, core), device_id_type=mesh_ids)

    @pl.when(has_right)
    def _():
        pl.semaphore_signal(barrier, inc=1, device_id=(me + 1, core), device_id_type=mesh_ids)

    @pl.when(jnp.logical_and(has_left, has_right))
    def _():
        pl.semaphore_wait(barrier, 2)

    @pl.when(jnp.logical_xor(has_left, has_right))
    def _():
        pl.semaphore_wait(barrier, 1)

    def span_of(piece):
        return pl.ds(pl.multiple_of(piece * rows, 8), rows)

    def copy_of(hop, piece):
        span = span_of(piece)
        source = own.at[span] if hop == 0 else hist.at[hop - 1, span]
        return pltpu.make_async_remote_copy(
            src_ref=source,
            dst_ref=hist.at[hop, span],
            send_sem=send_sem.at[hop, piece],
            recv_sem=recv_sem.at[hop, piece],
            device_id=(me + 1, core),
            device_id_type=mesh_ids,
        )

    lane = lax.broadcasted_iota(jnp.int32, (1, lanes), 1)
    first_half = lane < head_size
    heads = lax.broadcasted_iota(jnp.int32, (width, width), 0) // head_size
    same_head = heads == lax.broadcasted_iota(jnp.int32, (width, width), 1) // head_size
    sum_ref[...] = same_head.astype(jnp.bfloat16)

    def add_term(block, span, valid, first):
        kv = jnp.dot(block, wt_ref[:, width:], preferred_element_type=jnp.float32).astype(jnp.bfloat16)
        keys2 = kv[:, :width].astype(jnp.float32)
        values2 = kv[:, width:].astype(jnp.float32)
        prod = query2[span, :].astype(jnp.float32) * keys2
        high = prod.astype(jnp.bfloat16)
        low = (prod - high.astype(jnp.float32)).astype(jnp.bfloat16)
        summer = sum_ref[...]
        scores = (
            jnp.dot(high, summer, preferred_element_type=jnp.float32)
            + jnp.dot(low, summer, preferred_element_type=jnp.float32)
        ) * scale
        expo = jnp.where(valid, jnp.exp(scores), 0.0)
        part = expo.astype(jnp.bfloat16).astype(jnp.float32) * values2
        if first:
            mixed[span, :] = part
            total[span, :] = expo
        else:
            mixed[span, :] += part
            total[span, :] += expo

    def space_step(piece, carry):
        span = span_of(piece)
        pieces = []
        current = stream_ref[span, :].astype(jnp.float32)
        mean_cur = jnp.mean(current * current, axis=-1, keepdims=True)
        normed = (current * lax.rsqrt(mean_cur + 1e-06) * gain_s_ref[...]).astype(jnp.bfloat16)
        query_s = jnp.dot(normed, ws_ref[...], preferred_element_type=jnp.float32).astype(
            jnp.bfloat16
        )
        for pair in range(width // lanes):
            cols = slice(pair * lanes, (pair + 1) * lanes)
            q = query_s[:, cols]
            key_cols = slice(width + pair * lanes, width + (pair + 1) * lanes)
            sources = (
                (kv_ref[:, cols], kv_ref[:, key_cols]),
                (other_ref[:, cols], other_ref[:, key_cols]),
            )
            outs = []
            for mask in (first_half, jnp.logical_not(first_half)):
                q_one = jnp.where(mask, q, jnp.zeros_like(q))
                rowsum = None
                mixed_one = None
                for k, v in sources:
                    scores = lax.dot_general(
                        q_one, k, (((1,), (1,)), ((), ())), preferred_element_type=jnp.float32
                    ) * scale
                    expo = jnp.exp(scores)
                    part_sum = jnp.sum(expo, axis=-1, keepdims=True)
                    part = jnp.dot(
                        expo.astype(jnp.bfloat16), v, preferred_element_type=jnp.float32
                    )
                    rowsum = part_sum if rowsum is None else rowsum + part_sum
                    mixed_one = part if mixed_one is None else mixed_one + part
                outs.append(mixed_one / rowsum)
            pieces.append(jnp.where(first_half, outs[0], outs[1]).astype(jnp.bfloat16))
        spatial = jnp.concatenate(pieces, axis=1)
        stream2 = (
            stream_ref[span, :].astype(jnp.float32)
            + jnp.dot(spatial, wo_ref[...], preferred_element_type=jnp.float32)
        ).astype(jnp.bfloat16)
        stream2_ref[span, :] = stream2
        values = stream2.astype(jnp.float32)
        mean_sq = jnp.mean(values * values, axis=-1, keepdims=True)
        normed2 = (values * lax.rsqrt(mean_sq + 1e-06) * gain_ref[...]).astype(jnp.bfloat16)
        own[span, :] = normed2
        query2[span, :] = jnp.dot(
            normed2, wt_ref[:, :width], preferred_element_type=jnp.float32
        ).astype(jnp.bfloat16)

        add_term(own[span, :], span, True, True)

        @pl.when(has_right)
        def _():
            copy_of(0, piece).start()

        return carry

    lax.fori_loop(0, chunks, space_step, 0)

    for hop in range(WIN):
        def hop_step(piece, carry, hop=hop):
            span = span_of(piece)

            @pl.when(has_left)
            def _():
                copy_of(hop, piece).wait_recv()

            if hop + 1 < WIN:
                @pl.when(has_right)
                def _():
                    copy_of(hop + 1, piece).start()

            add_term(hist[hop, span, :], span, me - (hop + 1) >= 0, False)
            return carry

        lax.fori_loop(0, chunks, hop_step, 0)

    @pl.when(has_right)
    def _():
        for hop in range(WIN):
            for piece in range(chunks):
                copy_of(hop, piece).wait_send()

    out_ref[...] = (mixed[...] / total[...]).astype(out_ref.dtype)


def block_tail(q_weight, gain_space, keys_values, other, stream, out_space, gain_time, qkv_time, chunks=6):
    rows, width = stream.shape
    gain = gain_time.astype(jnp.float32).reshape(1, width)
    gain_s = gain_space.astype(jnp.float32).reshape(1, width)
    vmem = pl.BlockSpec(memory_space=pltpu.VMEM)
    plane = jax.ShapeDtypeStruct((rows, width), jnp.bfloat16)
    return pl.pallas_call(
        functools.partial(block_kernel, chunks),
        out_shape=(plane, plane),
        in_specs=[vmem] * 8,
        out_specs=(vmem, vmem),
        scratch_shapes=[
            pltpu.VMEM((rows, width), jnp.bfloat16),
            pltpu.VMEM((rows, width), jnp.bfloat16),
            pltpu.VMEM((WIN, rows, width), jnp.bfloat16),
            pltpu.VMEM((rows, width), jnp.float32),
            pltpu.VMEM((rows, width), jnp.float32),
            pltpu.VMEM((width, width), jnp.bfloat16),
            pltpu.SemaphoreType.DMA((WIN, chunks)),
            pltpu.SemaphoreType.DMA((WIN, chunks)),
        ],
        compiler_params=pltpu.CompilerParams(
            collective_id=0, has_side_effects=True, vmem_limit_bytes=56 * 1024 * 1024
        ),
    )(q_weight, gain_s, keys_values, other, stream, out_space, gain, qkv_time)


def local(
    patches,
    patch_weight,
    conv_taps,
    gain_space,
    qkv_space,
    out_space,
    gain_time,
    qkv_time,
    out_time,
):
    frames, zdev, grid, _, patch = patches.shape
    width = patch_weight.shape[1]
    tokens = zdev * grid * grid
    ends = extended(patches, (("tok", 1),), 1)
    embed = jnp.dot(patches, patch_weight, preferred_element_type=jnp.float32).astype(
        jnp.bfloat16
    )
    low = jnp.dot(ends[:, :1], patch_weight, preferred_element_type=jnp.float32)
    high = jnp.dot(ends[:, -1:], patch_weight, preferred_element_type=jnp.float32)
    padded = jnp.concatenate(
        [low.astype(jnp.bfloat16), embed, high.astype(jnp.bfloat16)], axis=1
    )
    stream = depthwise(padded[0], conv_taps).reshape(frames, tokens, width)
    normed = rms_scale(stream.astype(jnp.float32), gain_space).astype(jnp.bfloat16)
    flat = normed.reshape(-1, width)
    own_kv = jnp.dot(flat, qkv_space[:, width:], preferred_element_type=jnp.float32).astype(
        jnp.bfloat16
    )
    count = lax.axis_size("tok")
    other_kv = lax.ppermute(own_kv, "tok", [(i, (i + 1) % count) for i in range(count)])
    temporal, stream2 = block_tail(
        qkv_space[:, :width], gain_space, own_kv, other_kv, stream.reshape(-1, width),
        out_space, gain_time, qkv_time,
    )
    time_proj = jnp.dot(
        temporal.reshape(-1, width), out_time, preferred_element_type=jnp.float32
    ).reshape(frames, tokens, width)
    output = (stream2.astype(jnp.float32) + time_proj).astype(jnp.bfloat16)
    return output.reshape(frames, zdev, grid, grid, width)


def solution(mesh):
    placed = (P("tm", "tok", None, None, None), P(), P(), P(), P(), P(), P(), P(), P())
    return jax.shard_map(
        local,
        mesh=mesh,
        in_specs=placed,
        out_specs=P("tm", "tok", None, None, None),
        check_vma=False,
    )
```

```python
import jax
import jax.numpy as jnp
from jax import lax
from jax.sharding import PartitionSpec as P
from jax.experimental import pallas as pl
from jax.experimental.pallas import tpu as pltpu
import functools

D = 512
H = 8
WIN = 4


def extended(block, sides, width):
    for axis, dim in sides:
        count = lax.axis_size(axis)
        forward = [(i, i + 1) for i in range(count - 1)]
        backward = [(target, source) for source, target in forward]
        low = lax.ppermute(
            lax.slice_in_dim(block, block.shape[dim] - width, None, axis=dim), axis, forward
        )
        high = lax.ppermute(lax.slice_in_dim(block, 0, width, axis=dim), axis, backward)
        block = jnp.concatenate([low, block, high], axis=dim)
    return block


def from_behind(value, axis, steps):
    count = lax.axis_size(axis)
    leading, last = (max(0, -steps), min(count, count - steps))
    return lax.ppermute(value, axis, [(source, source + steps) for source in range(leading, last)])


def rms_scale(values, gain):
    mean_sq = jnp.mean(values * values, axis=-1, keepdims=True)
    return values * lax.rsqrt(mean_sq + 1e-06) * gain.astype(jnp.float32)


def split_heads(block, count, head_size):
    return block.reshape(block.shape[0], count, head_size).transpose(1, 0, 2)


def attend(query, keys, values):
    rows, cols = query.shape
    head_size = D // H
    count = cols // head_size
    scale = head_size ** (-0.5)

    def one_head(parts):
        q_one, k_one, v_one = parts
        scores = jnp.dot(q_one, k_one.T, preferred_element_type=jnp.float32) * scale
        expo = jnp.exp(scores)
        mixed = jnp.dot(expo.astype(jnp.bfloat16), v_one, preferred_element_type=jnp.float32)
        return (mixed / jnp.sum(expo, axis=-1, keepdims=True)).astype(jnp.bfloat16)

    parts = (
        split_heads(query, count, head_size),
        split_heads(keys, count, head_size),
        split_heads(values, count, head_size),
    )
    result = lax.map(one_head, parts)
    return result.transpose(1, 0, 2).reshape(rows, cols)


def conv_kernel(e_ref, t_ref, o_ref):
    planes, rows, lanes_x, width = o_ref.shape

    def plane(z, carry):
        parts = []
        for dx in range(3):
            acc = None
            for dz in range(3):
                for dy in range(3):
                    tap = t_ref[pl.ds(9 * dz + 3 * dy + dx, 1), :]
                    term = e_ref[z + dz, dy:dy + rows] * tap
                    acc = term if acc is None else acc + term
            parts.append(acc)
        conv = (
            pltpu.roll(parts[0], 1, 1) + parts[1] + pltpu.roll(parts[2], lanes_x - 1, 1)
        )
        o_ref[z] = (e_ref[z + 1, 1:1 + rows] + conv).astype(o_ref.dtype)
        return carry

    lax.fori_loop(0, planes, plane, 0)


def depthwise(ext, taps):
    depth, grid, _, width = ext.shape
    planes = depth - 2
    padded = jnp.pad(ext.astype(jnp.float32), ((0, 0), (1, 1), (1, 3), (0, 0)))
    vmem = pl.BlockSpec(memory_space=pltpu.VMEM)
    out = pl.pallas_call(
        conv_kernel,
        out_shape=jax.ShapeDtypeStruct((planes, grid, grid + 4, width), jnp.bfloat16),
        in_specs=[vmem, vmem],
        out_specs=vmem,
        compiler_params=pltpu.CompilerParams(vmem_limit_bytes=32 * 1024 * 1024),
    )(padded, taps.astype(jnp.float32))
    return out[:, :, 1:1 + grid]


def block_kernel(
    chunks, q_ref, kv_ref, other_ref, stream_ref, wo_ref, gain_ref, wt_ref,
    out_ref, stream2_ref, own, query2, hist, mixed, total, sum_ref, send_sem, recv_sem,
):
    me = lax.axis_index("tm")
    count = lax.axis_size("tm")
    core = lax.axis_index("tok")
    has_left = me > 0
    has_right = me < count - 1
    rows_all, width = own.shape
    rows = rows_all // chunks
    head_size = width // H
    scale = head_size ** (-0.5)
    lanes = 2 * head_size
    mesh_ids = pl.DeviceIdType.MESH

    @pl.when(jnp.logical_not(has_left))
    def _():
        hist[...] = jnp.zeros_like(hist)

    barrier = pltpu.get_barrier_semaphore()

    @pl.when(has_left)
    def _():
        pl.semaphore_signal(barrier, inc=1, device_id=(me - 1, core), device_id_type=mesh_ids)

    @pl.when(has_right)
    def _():
        pl.semaphore_signal(barrier, inc=1, device_id=(me + 1, core), device_id_type=mesh_ids)

    @pl.when(jnp.logical_and(has_left, has_right))
    def _():
        pl.semaphore_wait(barrier, 2)

    @pl.when(jnp.logical_xor(has_left, has_right))
    def _():
        pl.semaphore_wait(barrier, 1)

    def span_of(piece):
        return pl.ds(pl.multiple_of(piece * rows, 8), rows)

    def copy_of(hop, piece):
        span = span_of(piece)
        source = own.at[span] if hop == 0 else hist.at[hop - 1, span]
        return pltpu.make_async_remote_copy(
            src_ref=source,
            dst_ref=hist.at[hop, span],
            send_sem=send_sem.at[hop, piece],
            recv_sem=recv_sem.at[hop, piece],
            device_id=(me + 1, core),
            device_id_type=mesh_ids,
        )

    lane = lax.broadcasted_iota(jnp.int32, (1, lanes), 1)
    first_half = lane < head_size
    heads = lax.broadcasted_iota(jnp.int32, (width, width), 0) // head_size
    same_head = heads == lax.broadcasted_iota(jnp.int32, (width, width), 1) // head_size
    sum_ref[...] = same_head.astype(jnp.bfloat16)

    def add_term(block, span, valid, first):
        kv = jnp.dot(block, wt_ref[:, width:], preferred_element_type=jnp.float32).astype(jnp.bfloat16)
        keys2 = kv[:, :width].astype(jnp.float32)
        values2 = kv[:, width:].astype(jnp.float32)
        prod = query2[span, :].astype(jnp.float32) * keys2
        high = prod.astype(jnp.bfloat16)
        low = (prod - high.astype(jnp.float32)).astype(jnp.bfloat16)
        summer = sum_ref[...]
        scores = (
            jnp.dot(high, summer, preferred_element_type=jnp.float32)
            + jnp.dot(low, summer, preferred_element_type=jnp.float32)
        ) * scale
        expo = jnp.where(valid, jnp.exp(scores), 0.0)
        part = expo.astype(jnp.bfloat16).astype(jnp.float32) * values2
        if first:
            mixed[span, :] = part
            total[span, :] = expo
        else:
            mixed[span, :] += part
            total[span, :] += expo

    def space_step(piece, carry):
        span = span_of(piece)
        pieces = []
        for pair in range(width // lanes):
            cols = slice(pair * lanes, (pair + 1) * lanes)
            q = q_ref[span, cols]
            key_cols = slice(width + pair * lanes, width + (pair + 1) * lanes)
            sources = (
                (kv_ref[:, cols], kv_ref[:, key_cols]),
                (other_ref[:, cols], other_ref[:, key_cols]),
            )
            outs = []
            for mask in (first_half, jnp.logical_not(first_half)):
                q_one = jnp.where(mask, q, jnp.zeros_like(q))
                rowsum = None
                mixed_one = None
                for k, v in sources:
                    scores = lax.dot_general(
                        q_one, k, (((1,), (1,)), ((), ())), preferred_element_type=jnp.float32
                    ) * scale
                    expo = jnp.exp(scores)
                    part_sum = jnp.sum(expo, axis=-1, keepdims=True)
                    part = jnp.dot(
                        expo.astype(jnp.bfloat16), v, preferred_element_type=jnp.float32
                    )
                    rowsum = part_sum if rowsum is None else rowsum + part_sum
                    mixed_one = part if mixed_one is None else mixed_one + part
                outs.append(mixed_one / rowsum)
            pieces.append(jnp.where(first_half, outs[0], outs[1]).astype(jnp.bfloat16))
        spatial = jnp.concatenate(pieces, axis=1)
        stream2 = (
            stream_ref[span, :].astype(jnp.float32)
            + jnp.dot(spatial, wo_ref[...], preferred_element_type=jnp.float32)
        ).astype(jnp.bfloat16)
        stream2_ref[span, :] = stream2
        values = stream2.astype(jnp.float32)
        mean_sq = jnp.mean(values * values, axis=-1, keepdims=True)
        normed2 = (values * lax.rsqrt(mean_sq + 1e-06) * gain_ref[...]).astype(jnp.bfloat16)
        own[span, :] = normed2
        query2[span, :] = jnp.dot(
            normed2, wt_ref[:, :width], preferred_element_type=jnp.float32
        ).astype(jnp.bfloat16)

        add_term(own[span, :], span, True, True)

        @pl.when(has_right)
        def _():
            copy_of(0, piece).start()

        return carry

    lax.fori_loop(0, chunks, space_step, 0)

    for hop in range(WIN):
        def hop_step(piece, carry, hop=hop):
            span = span_of(piece)

            @pl.when(has_left)
            def _():
                copy_of(hop, piece).wait_recv()

            if hop + 1 < WIN:
                @pl.when(has_right)
                def _():
                    copy_of(hop + 1, piece).start()

            add_term(hist[hop, span, :], span, me - (hop + 1) >= 0, False)
            return carry

        lax.fori_loop(0, chunks, hop_step, 0)

    @pl.when(has_right)
    def _():
        for hop in range(WIN):
            for piece in range(chunks):
                copy_of(hop, piece).wait_send()

    out_ref[...] = (mixed[...] / total[...]).astype(out_ref.dtype)


def block_tail(query, keys_values, other, stream, out_space, gain_time, qkv_time, chunks=6):
    rows, width = stream.shape
    gain = gain_time.astype(jnp.float32).reshape(1, width)
    vmem = pl.BlockSpec(memory_space=pltpu.VMEM)
    plane = jax.ShapeDtypeStruct((rows, width), jnp.bfloat16)
    return pl.pallas_call(
        functools.partial(block_kernel, chunks),
        out_shape=(plane, plane),
        in_specs=[vmem] * 7,
        out_specs=(vmem, vmem),
        scratch_shapes=[
            pltpu.VMEM((rows, width), jnp.bfloat16),
            pltpu.VMEM((rows, width), jnp.bfloat16),
            pltpu.VMEM((WIN, rows, width), jnp.bfloat16),
            pltpu.VMEM((rows, width), jnp.float32),
            pltpu.VMEM((rows, width), jnp.float32),
            pltpu.VMEM((width, width), jnp.bfloat16),
            pltpu.SemaphoreType.DMA((WIN, chunks)),
            pltpu.SemaphoreType.DMA((WIN, chunks)),
        ],
        compiler_params=pltpu.CompilerParams(
            collective_id=0, has_side_effects=True, vmem_limit_bytes=56 * 1024 * 1024
        ),
    )(query, keys_values, other, stream, out_space, gain, qkv_time)


def local(
    patches,
    patch_weight,
    conv_taps,
    gain_space,
    qkv_space,
    out_space,
    gain_time,
    qkv_time,
    out_time,
):
    frames, zdev, grid, _, patch = patches.shape
    width = patch_weight.shape[1]
    tokens = zdev * grid * grid
    embed = jnp.dot(patches, patch_weight, preferred_element_type=jnp.float32).astype(
        jnp.bfloat16
    )
    padded = extended(embed, (("tok", 1),), 1)
    stream = depthwise(padded[0], conv_taps).reshape(frames, tokens, width)
    normed = rms_scale(stream.astype(jnp.float32), gain_space).astype(jnp.bfloat16)
    flat = lax.optimization_barrier(normed.reshape(-1, width))
    own_kv = jnp.dot(flat, qkv_space[:, width:], preferred_element_type=jnp.float32).astype(
        jnp.bfloat16
    )
    count = lax.axis_size("tok")
    other_kv = lax.ppermute(own_kv, "tok", [(i, (i + 1) % count) for i in range(count)])
    query = jnp.dot(flat, qkv_space[:, :width], preferred_element_type=jnp.float32).astype(
        jnp.bfloat16
    )
    temporal, stream2 = block_tail(
        query, own_kv, other_kv, stream.reshape(-1, width), out_space, gain_time, qkv_time
    )
    time_proj = jnp.dot(
        temporal.reshape(-1, width), out_time, preferred_element_type=jnp.float32
    ).reshape(frames, tokens, width)
    output = (stream2.astype(jnp.float32) + time_proj).astype(jnp.bfloat16)
    return output.reshape(frames, zdev, grid, grid, width)


def solution(mesh):
    placed = (P("tm", "tok", None, None, None), P(), P(), P(), P(), P(), P(), P(), P())
    return jax.shard_map(
        local,
        mesh=mesh,
        in_specs=placed,
        out_specs=P("tm", "tok", None, None, None),
        check_vma=False,
    )
```

```python
import jax
import jax.numpy as jnp
from jax import lax
from jax.sharding import PartitionSpec as P
from jax.experimental import pallas as pl
from jax.experimental.pallas import tpu as pltpu
import functools

D = 512
H = 8
WIN = 4


def extended(block, sides, width):
    for axis, dim in sides:
        count = lax.axis_size(axis)
        forward = [(i, i + 1) for i in range(count - 1)]
        backward = [(target, source) for source, target in forward]
        low = lax.ppermute(
            lax.slice_in_dim(block, block.shape[dim] - width, None, axis=dim), axis, forward
        )
        high = lax.ppermute(lax.slice_in_dim(block, 0, width, axis=dim), axis, backward)
        block = jnp.concatenate([low, block, high], axis=dim)
    return block


def from_behind(value, axis, steps):
    count = lax.axis_size(axis)
    leading, last = (max(0, -steps), min(count, count - steps))
    return lax.ppermute(value, axis, [(source, source + steps) for source in range(leading, last)])


def rms_scale(values, gain):
    mean_sq = jnp.mean(values * values, axis=-1, keepdims=True)
    return values * lax.rsqrt(mean_sq + 1e-06) * gain.astype(jnp.float32)


def split_heads(block, count, head_size):
    return block.reshape(block.shape[0], count, head_size).transpose(1, 0, 2)


def attend(query, keys, values):
    rows, cols = query.shape
    head_size = D // H
    count = cols // head_size
    scale = head_size ** (-0.5)

    def one_head(parts):
        q_one, k_one, v_one = parts
        scores = jnp.dot(q_one, k_one.T, preferred_element_type=jnp.float32) * scale
        expo = jnp.exp(scores)
        mixed = jnp.dot(expo.astype(jnp.bfloat16), v_one, preferred_element_type=jnp.float32)
        return (mixed / jnp.sum(expo, axis=-1, keepdims=True)).astype(jnp.bfloat16)

    parts = (
        split_heads(query, count, head_size),
        split_heads(keys, count, head_size),
        split_heads(values, count, head_size),
    )
    result = lax.map(one_head, parts)
    return result.transpose(1, 0, 2).reshape(rows, cols)


def conv_kernel(e_ref, t_ref, o_ref):
    planes, rows, lanes_x, width = o_ref.shape

    def plane(z, carry):
        parts = []
        for dx in range(3):
            acc = None
            for dz in range(3):
                for dy in range(3):
                    tap = t_ref[pl.ds(9 * dz + 3 * dy + dx, 1), :]
                    term = e_ref[z + dz, dy:dy + rows] * tap
                    acc = term if acc is None else acc + term
            parts.append(acc)
        conv = (
            pltpu.roll(parts[0], 1, 1) + parts[1] + pltpu.roll(parts[2], lanes_x - 1, 1)
        )
        o_ref[z] = (e_ref[z + 1, 1:1 + rows] + conv).astype(o_ref.dtype)
        return carry

    lax.fori_loop(0, planes, plane, 0)


def depthwise(ext, taps):
    depth, grid, _, width = ext.shape
    planes = depth - 2
    padded = jnp.pad(ext.astype(jnp.float32), ((0, 0), (1, 1), (1, 3), (0, 0)))
    vmem = pl.BlockSpec(memory_space=pltpu.VMEM)
    out = pl.pallas_call(
        conv_kernel,
        out_shape=jax.ShapeDtypeStruct((planes, grid, grid + 4, width), jnp.bfloat16),
        in_specs=[vmem, vmem],
        out_specs=vmem,
        compiler_params=pltpu.CompilerParams(vmem_limit_bytes=32 * 1024 * 1024),
    )(padded, taps.astype(jnp.float32))
    return out[:, :, 1:1 + grid]


def block_kernel(
    chunks, q_ref, kv_ref, other_ref, stream_ref, wo_ref, gain_ref, wt_ref,
    out_ref, stream2_ref, own, query2, hist, mixed, total, sum_ref, send_sem, recv_sem,
):
    me = lax.axis_index("tm")
    count = lax.axis_size("tm")
    core = lax.axis_index("tok")
    has_left = me > 0
    has_right = me < count - 1
    rows_all, width = own.shape
    rows = rows_all // chunks
    head_size = width // H
    scale = head_size ** (-0.5)
    lanes = 2 * head_size
    mesh_ids = pl.DeviceIdType.MESH

    @pl.when(jnp.logical_not(has_left))
    def _():
        hist[...] = jnp.zeros_like(hist)

    barrier = pltpu.get_barrier_semaphore()

    @pl.when(has_left)
    def _():
        pl.semaphore_signal(barrier, inc=1, device_id=(me - 1, core), device_id_type=mesh_ids)

    @pl.when(has_right)
    def _():
        pl.semaphore_signal(barrier, inc=1, device_id=(me + 1, core), device_id_type=mesh_ids)

    @pl.when(jnp.logical_and(has_left, has_right))
    def _():
        pl.semaphore_wait(barrier, 2)

    @pl.when(jnp.logical_xor(has_left, has_right))
    def _():
        pl.semaphore_wait(barrier, 1)

    def span_of(piece):
        return pl.ds(pl.multiple_of(piece * rows, 8), rows)

    def copy_of(hop, piece):
        span = span_of(piece)
        source = own.at[span] if hop == 0 else hist.at[hop - 1, span]
        return pltpu.make_async_remote_copy(
            src_ref=source,
            dst_ref=hist.at[hop, span],
            send_sem=send_sem.at[hop, piece],
            recv_sem=recv_sem.at[hop, piece],
            device_id=(me + 1, core),
            device_id_type=mesh_ids,
        )

    lane = lax.broadcasted_iota(jnp.int32, (1, lanes), 1)
    first_half = lane < head_size
    heads = lax.broadcasted_iota(jnp.int32, (width, width), 0) // head_size
    same_head = heads == lax.broadcasted_iota(jnp.int32, (width, width), 1) // head_size
    sum_ref[...] = same_head.astype(jnp.bfloat16)

    def add_term(block, span, valid, first):
        kv = jnp.dot(block, wt_ref[:, width:], preferred_element_type=jnp.float32).astype(jnp.bfloat16)
        keys2 = kv[:, :width].astype(jnp.float32)
        values2 = kv[:, width:].astype(jnp.float32)
        prod = query2[span, :].astype(jnp.float32) * keys2
        high = prod.astype(jnp.bfloat16)
        low = (prod - high.astype(jnp.float32)).astype(jnp.bfloat16)
        summer = sum_ref[...]
        scores = (
            jnp.dot(high, summer, preferred_element_type=jnp.float32)
            + jnp.dot(low, summer, preferred_element_type=jnp.float32)
        ) * scale
        expo = jnp.where(valid, jnp.exp(scores), 0.0)
        part = expo.astype(jnp.bfloat16).astype(jnp.float32) * values2
        if first:
            mixed[span, :] = part
            total[span, :] = expo
        else:
            mixed[span, :] += part
            total[span, :] += expo

    def space_step(piece, carry):
        span = span_of(piece)
        pieces = []
        for pair in range(width // lanes):
            cols = slice(pair * lanes, (pair + 1) * lanes)
            q = q_ref[span, cols]
            key_cols = slice(width + pair * lanes, width + (pair + 1) * lanes)
            sources = (
                (kv_ref[:, cols], kv_ref[:, key_cols]),
                (other_ref[:, cols], other_ref[:, key_cols]),
            )
            outs = []
            for mask in (first_half, jnp.logical_not(first_half)):
                q_one = jnp.where(mask, q, jnp.zeros_like(q))
                rowsum = None
                mixed_one = None
                for k, v in sources:
                    scores = lax.dot_general(
                        q_one, k, (((1,), (1,)), ((), ())), preferred_element_type=jnp.float32
                    ) * scale
                    expo = jnp.exp(scores)
                    part_sum = jnp.sum(expo, axis=-1, keepdims=True)
                    part = jnp.dot(
                        expo.astype(jnp.bfloat16), v, preferred_element_type=jnp.float32
                    )
                    rowsum = part_sum if rowsum is None else rowsum + part_sum
                    mixed_one = part if mixed_one is None else mixed_one + part
                outs.append(mixed_one / rowsum)
            pieces.append(jnp.where(first_half, outs[0], outs[1]).astype(jnp.bfloat16))
        spatial = jnp.concatenate(pieces, axis=1)
        stream2 = (
            stream_ref[span, :].astype(jnp.float32)
            + jnp.dot(spatial, wo_ref[...], preferred_element_type=jnp.float32)
        ).astype(jnp.bfloat16)
        stream2_ref[span, :] = stream2
        values = stream2.astype(jnp.float32)
        mean_sq = jnp.mean(values * values, axis=-1, keepdims=True)
        normed2 = (values * lax.rsqrt(mean_sq + 1e-06) * gain_ref[...]).astype(jnp.bfloat16)
        own[span, :] = normed2
        query2[span, :] = jnp.dot(
            normed2, wt_ref[:, :width], preferred_element_type=jnp.float32
        ).astype(jnp.bfloat16)

        add_term(own[span, :], span, True, True)

        @pl.when(has_right)
        def _():
            copy_of(0, piece).start()

        return carry

    lax.fori_loop(0, chunks, space_step, 0)

    for hop in range(WIN):
        def hop_step(piece, carry, hop=hop):
            span = span_of(piece)

            @pl.when(has_left)
            def _():
                copy_of(hop, piece).wait_recv()

            if hop + 1 < WIN:
                @pl.when(has_right)
                def _():
                    copy_of(hop + 1, piece).start()

            add_term(hist[hop, span, :], span, me - (hop + 1) >= 0, False)
            return carry

        lax.fori_loop(0, chunks, hop_step, 0)

    @pl.when(has_right)
    def _():
        for hop in range(WIN):
            for piece in range(chunks):
                copy_of(hop, piece).wait_send()

    out_ref[...] = (mixed[...] / total[...]).astype(out_ref.dtype)


def block_tail(query, keys_values, other, stream, out_space, gain_time, qkv_time, chunks=6):
    rows, width = stream.shape
    gain = gain_time.astype(jnp.float32).reshape(1, width)
    vmem = pl.BlockSpec(memory_space=pltpu.VMEM)
    plane = jax.ShapeDtypeStruct((rows, width), jnp.bfloat16)
    return pl.pallas_call(
        functools.partial(block_kernel, chunks),
        out_shape=(plane, plane),
        in_specs=[vmem] * 7,
        out_specs=(vmem, vmem),
        scratch_shapes=[
            pltpu.VMEM((rows, width), jnp.bfloat16),
            pltpu.VMEM((rows, width), jnp.bfloat16),
            pltpu.VMEM((WIN, rows, width), jnp.bfloat16),
            pltpu.VMEM((rows, width), jnp.float32),
            pltpu.VMEM((rows, width), jnp.float32),
            pltpu.VMEM((width, width), jnp.bfloat16),
            pltpu.SemaphoreType.DMA((WIN, chunks)),
            pltpu.SemaphoreType.DMA((WIN, chunks)),
        ],
        compiler_params=pltpu.CompilerParams(
            collective_id=0, has_side_effects=True, vmem_limit_bytes=56 * 1024 * 1024
        ),
    )(query, keys_values, other, stream, out_space, gain, qkv_time)


def local(
    patches,
    patch_weight,
    conv_taps,
    gain_space,
    qkv_space,
    out_space,
    gain_time,
    qkv_time,
    out_time,
):
    frames, zdev, grid, _, patch = patches.shape
    width = patch_weight.shape[1]
    tokens = zdev * grid * grid
    embed = jnp.dot(patches, patch_weight, preferred_element_type=jnp.float32).astype(
        jnp.bfloat16
    )
    if lax.axis_size("tok") == 2:
        side = lax.axis_index("tok")
        edge = lax.dynamic_slice_in_dim(embed, jnp.where(side == 0, zdev - 1, 0), 1, axis=1)
        halo = lax.ppermute(edge, "tok", [(0, 1), (1, 0)])
        empty = jnp.zeros_like(halo)
        low = jnp.where(side == 1, halo, empty)
        high = jnp.where(side == 0, halo, empty)
        padded = jnp.concatenate([low, embed, high], axis=1)
    else:
        padded = extended(embed, (("tok", 1),), 1)
    stream = depthwise(padded[0], conv_taps).reshape(frames, tokens, width)
    normed = rms_scale(stream.astype(jnp.float32), gain_space).astype(jnp.bfloat16)
    flat = normed.reshape(-1, width)
    own_kv = jnp.dot(flat, qkv_space[:, width:], preferred_element_type=jnp.float32).astype(
        jnp.bfloat16
    )
    count = lax.axis_size("tok")
    other_kv = lax.ppermute(own_kv, "tok", [(i, (i + 1) % count) for i in range(count)])
    query = jnp.dot(flat, qkv_space[:, :width], preferred_element_type=jnp.float32).astype(
        jnp.bfloat16
    )
    temporal, stream2 = block_tail(
        query, own_kv, other_kv, stream.reshape(-1, width), out_space, gain_time, qkv_time
    )
    time_proj = jnp.dot(
        temporal.reshape(-1, width), out_time, preferred_element_type=jnp.float32
    ).reshape(frames, tokens, width)
    output = (stream2.astype(jnp.float32) + time_proj).astype(jnp.bfloat16)
    return output.reshape(frames, zdev, grid, grid, width)


def solution(mesh):
    placed = (P("tm", "tok", None, None, None), P(), P(), P(), P(), P(), P(), P(), P())
    return jax.shard_map(
        local,
        mesh=mesh,
        in_specs=placed,
        out_specs=P("tm", "tok", None, None, None),
        check_vma=False,
    )
```

```python
import jax
import jax.numpy as jnp
from jax import lax
from jax.sharding import PartitionSpec as P
from jax.experimental import pallas as pl
from jax.experimental.pallas import tpu as pltpu
import functools

D = 512
H = 8
WIN = 4


def extended(block, sides, width):
    for axis, dim in sides:
        count = lax.axis_size(axis)
        forward = [(i, i + 1) for i in range(count - 1)]
        backward = [(target, source) for source, target in forward]
        low = lax.ppermute(
            lax.slice_in_dim(block, block.shape[dim] - width, None, axis=dim), axis, forward
        )
        high = lax.ppermute(lax.slice_in_dim(block, 0, width, axis=dim), axis, backward)
        block = jnp.concatenate([low, block, high], axis=dim)
    return block


def from_behind(value, axis, steps):
    count = lax.axis_size(axis)
    leading, last = (max(0, -steps), min(count, count - steps))
    return lax.ppermute(value, axis, [(source, source + steps) for source in range(leading, last)])


def rms_scale(values, gain):
    mean_sq = jnp.mean(values * values, axis=-1, keepdims=True)
    return values * lax.rsqrt(mean_sq + 1e-06) * gain.astype(jnp.float32)


def split_heads(block, count, head_size):
    return block.reshape(block.shape[0], count, head_size).transpose(1, 0, 2)


def attend(query, keys, values):
    rows, cols = query.shape
    head_size = D // H
    count = cols // head_size
    scale = head_size ** (-0.5)

    def one_head(parts):
        q_one, k_one, v_one = parts
        scores = jnp.dot(q_one, k_one.T, preferred_element_type=jnp.float32) * scale
        expo = jnp.exp(scores)
        mixed = jnp.dot(expo.astype(jnp.bfloat16), v_one, preferred_element_type=jnp.float32)
        return (mixed / jnp.sum(expo, axis=-1, keepdims=True)).astype(jnp.bfloat16)

    parts = (
        split_heads(query, count, head_size),
        split_heads(keys, count, head_size),
        split_heads(values, count, head_size),
    )
    result = lax.map(one_head, parts)
    return result.transpose(1, 0, 2).reshape(rows, cols)


def conv_kernel(e_ref, t_ref, o_ref):
    planes, rows, lanes_x, width = o_ref.shape

    def plane(z, carry):
        parts = []
        for dx in range(3):
            acc = None
            for dz in range(3):
                for dy in range(3):
                    tap = t_ref[pl.ds(9 * dz + 3 * dy + dx, 1), :]
                    term = e_ref[z + dz, dy:dy + rows] * tap
                    acc = term if acc is None else acc + term
            parts.append(acc)
        conv = (
            pltpu.roll(parts[0], 1, 1) + parts[1] + pltpu.roll(parts[2], lanes_x - 1, 1)
        )
        o_ref[z] = (e_ref[z + 1, 1:1 + rows] + conv).astype(o_ref.dtype)
        return carry

    lax.fori_loop(0, planes, plane, 0)


def depthwise(ext, taps):
    depth, grid, _, width = ext.shape
    planes = depth - 2
    padded = jnp.pad(ext.astype(jnp.float32), ((0, 0), (1, 1), (1, 3), (0, 0)))
    vmem = pl.BlockSpec(memory_space=pltpu.VMEM)
    out = pl.pallas_call(
        conv_kernel,
        out_shape=jax.ShapeDtypeStruct((planes, grid, grid + 4, width), jnp.bfloat16),
        in_specs=[vmem, vmem],
        out_specs=vmem,
        compiler_params=pltpu.CompilerParams(vmem_limit_bytes=32 * 1024 * 1024),
    )(padded, taps.astype(jnp.float32))
    return out[:, :, 1:1 + grid]


def block_kernel(
    chunks, q_ref, kv_ref, other_ref, stream_ref, wo_ref, gain_ref, wt_ref, wout_ref,
    out_ref, stream2_ref, own, query2, hist, mixed, total, sum_ref, send_sem, recv_sem,
):
    me = lax.axis_index("tm")
    count = lax.axis_size("tm")
    core = lax.axis_index("tok")
    has_left = me > 0
    has_right = me < count - 1
    rows_all, width = own.shape
    rows = rows_all // chunks
    head_size = width // H
    scale = head_size ** (-0.5)
    lanes = 2 * head_size
    mesh_ids = pl.DeviceIdType.MESH

    @pl.when(jnp.logical_not(has_left))
    def _():
        hist[...] = jnp.zeros_like(hist)

    barrier = pltpu.get_barrier_semaphore()

    @pl.when(has_left)
    def _():
        pl.semaphore_signal(barrier, inc=1, device_id=(me - 1, core), device_id_type=mesh_ids)

    @pl.when(has_right)
    def _():
        pl.semaphore_signal(barrier, inc=1, device_id=(me + 1, core), device_id_type=mesh_ids)

    @pl.when(jnp.logical_and(has_left, has_right))
    def _():
        pl.semaphore_wait(barrier, 2)

    @pl.when(jnp.logical_xor(has_left, has_right))
    def _():
        pl.semaphore_wait(barrier, 1)

    def span_of(piece):
        return pl.ds(pl.multiple_of(piece * rows, 8), rows)

    def copy_of(hop, piece):
        span = span_of(piece)
        source = own.at[span] if hop == 0 else hist.at[hop - 1, span]
        return pltpu.make_async_remote_copy(
            src_ref=source,
            dst_ref=hist.at[hop, span],
            send_sem=send_sem.at[hop, piece],
            recv_sem=recv_sem.at[hop, piece],
            device_id=(me + 1, core),
            device_id_type=mesh_ids,
        )

    lane = lax.broadcasted_iota(jnp.int32, (1, lanes), 1)
    first_half = lane < head_size
    heads = lax.broadcasted_iota(jnp.int32, (width, width), 0) // head_size
    same_head = heads == lax.broadcasted_iota(jnp.int32, (width, width), 1) // head_size
    sum_ref[...] = same_head.astype(jnp.bfloat16)

    def add_term(block, span, valid, first):
        kv = jnp.dot(block, wt_ref[:, width:], preferred_element_type=jnp.float32).astype(jnp.bfloat16)
        keys2 = kv[:, :width].astype(jnp.float32)
        values2 = kv[:, width:].astype(jnp.float32)
        prod = query2[span, :].astype(jnp.float32) * keys2
        high = prod.astype(jnp.bfloat16)
        low = (prod - high.astype(jnp.float32)).astype(jnp.bfloat16)
        summer = sum_ref[...]
        scores = (
            jnp.dot(high, summer, preferred_element_type=jnp.float32)
            + jnp.dot(low, summer, preferred_element_type=jnp.float32)
        ) * scale
        expo = jnp.where(valid, jnp.exp(scores), 0.0)
        part = expo.astype(jnp.bfloat16).astype(jnp.float32) * values2
        if first:
            mixed[span, :] = part
            total[span, :] = expo
        else:
            mixed[span, :] += part
            total[span, :] += expo

    def space_step(piece, carry):
        span = span_of(piece)
        pieces = []
        for pair in range(width // lanes):
            cols = slice(pair * lanes, (pair + 1) * lanes)
            q = q_ref[span, cols]
            key_cols = slice(width + pair * lanes, width + (pair + 1) * lanes)
            sources = (
                (kv_ref[:, cols], kv_ref[:, key_cols]),
                (other_ref[:, cols], other_ref[:, key_cols]),
            )
            outs = []
            for mask in (first_half, jnp.logical_not(first_half)):
                q_one = jnp.where(mask, q, jnp.zeros_like(q))
                rowsum = None
                mixed_one = None
                for k, v in sources:
                    scores = lax.dot_general(
                        q_one, k, (((1,), (1,)), ((), ())), preferred_element_type=jnp.float32
                    ) * scale
                    expo = jnp.exp(scores)
                    part_sum = jnp.sum(expo, axis=-1, keepdims=True)
                    part = jnp.dot(
                        expo.astype(jnp.bfloat16), v, preferred_element_type=jnp.float32
                    )
                    rowsum = part_sum if rowsum is None else rowsum + part_sum
                    mixed_one = part if mixed_one is None else mixed_one + part
                outs.append(mixed_one / rowsum)
            pieces.append(jnp.where(first_half, outs[0], outs[1]).astype(jnp.bfloat16))
        spatial = jnp.concatenate(pieces, axis=1)
        stream2 = (
            stream_ref[span, :].astype(jnp.float32)
            + jnp.dot(spatial, wo_ref[...], preferred_element_type=jnp.float32)
        ).astype(jnp.bfloat16)
        stream2_ref[span, :] = stream2
        values = stream2.astype(jnp.float32)
        mean_sq = jnp.mean(values * values, axis=-1, keepdims=True)
        normed2 = (values * lax.rsqrt(mean_sq + 1e-06) * gain_ref[...]).astype(jnp.bfloat16)
        own[span, :] = normed2
        query2[span, :] = jnp.dot(
            normed2, wt_ref[:, :width], preferred_element_type=jnp.float32
        ).astype(jnp.bfloat16)

        add_term(own[span, :], span, True, True)

        @pl.when(has_right)
        def _():
            copy_of(0, piece).start()

        return carry

    lax.fori_loop(0, chunks, space_step, 0)

    for hop in range(WIN):
        def hop_step(piece, carry, hop=hop):
            span = span_of(piece)

            @pl.when(has_left)
            def _():
                copy_of(hop, piece).wait_recv()

            if hop + 1 < WIN:
                @pl.when(has_right)
                def _():
                    copy_of(hop + 1, piece).start()

            add_term(hist[hop, span, :], span, me - (hop + 1) >= 0, False)
            if hop + 1 == WIN:
                temporal = (mixed[span, :] / total[span, :]).astype(jnp.bfloat16)
                out_ref[span, :] = (
                    stream2_ref[span, :].astype(jnp.float32)
                    + jnp.dot(temporal, wout_ref[...], preferred_element_type=jnp.float32)
                ).astype(out_ref.dtype)
            return carry

        lax.fori_loop(0, chunks, hop_step, 0)

    @pl.when(has_right)
    def _():
        for hop in range(WIN):
            for piece in range(chunks):
                copy_of(hop, piece).wait_send()


def block_tail(
    query, keys_values, other, stream, out_space, gain_time, qkv_time, out_time, chunks=6
):
    rows, width = stream.shape
    gain = gain_time.astype(jnp.float32).reshape(1, width)
    vmem = pl.BlockSpec(memory_space=pltpu.VMEM)
    plane = jax.ShapeDtypeStruct((rows, width), jnp.bfloat16)
    return pl.pallas_call(
        functools.partial(block_kernel, chunks),
        out_shape=plane,
        in_specs=[vmem] * 8,
        out_specs=vmem,
        scratch_shapes=[
            pltpu.VMEM((rows, width), jnp.bfloat16),
            pltpu.VMEM((rows, width), jnp.bfloat16),
            pltpu.VMEM((rows, width), jnp.bfloat16),
            pltpu.VMEM((WIN, rows, width), jnp.bfloat16),
            pltpu.VMEM((rows, width), jnp.float32),
            pltpu.VMEM((rows, width), jnp.float32),
            pltpu.VMEM((width, width), jnp.bfloat16),
            pltpu.SemaphoreType.DMA((WIN, chunks)),
            pltpu.SemaphoreType.DMA((WIN, chunks)),
        ],
        compiler_params=pltpu.CompilerParams(
            collective_id=0, has_side_effects=True, vmem_limit_bytes=56 * 1024 * 1024
        ),
    )(query, keys_values, other, stream, out_space, gain, qkv_time, out_time)


def local(
    patches,
    patch_weight,
    conv_taps,
    gain_space,
    qkv_space,
    out_space,
    gain_time,
    qkv_time,
    out_time,
):
    frames, zdev, grid, _, patch = patches.shape
    width = patch_weight.shape[1]
    tokens = zdev * grid * grid
    embed = jnp.dot(patches, patch_weight, preferred_element_type=jnp.float32).astype(
        jnp.bfloat16
    )
    if lax.axis_size("tok") == 2:
        side = lax.axis_index("tok")
        edge = lax.dynamic_slice_in_dim(embed, jnp.where(side == 0, zdev - 1, 0), 1, axis=1)
        halo = lax.ppermute(edge, "tok", [(0, 1), (1, 0)])
        empty = jnp.zeros_like(halo)
        low = jnp.where(side == 1, halo, empty)
        high = jnp.where(side == 0, halo, empty)
        padded = jnp.concatenate([low, embed, high], axis=1)
    else:
        padded = extended(embed, (("tok", 1),), 1)
    stream = depthwise(padded[0], conv_taps).reshape(frames, tokens, width)
    normed = rms_scale(stream.astype(jnp.float32), gain_space).astype(jnp.bfloat16)
    flat = normed.reshape(-1, width)
    own_kv = jnp.dot(flat, qkv_space[:, width:], preferred_element_type=jnp.float32).astype(
        jnp.bfloat16
    )
    count = lax.axis_size("tok")
    other_kv = lax.ppermute(own_kv, "tok", [(i, (i + 1) % count) for i in range(count)])
    query = jnp.dot(flat, qkv_space[:, :width], preferred_element_type=jnp.float32).astype(
        jnp.bfloat16
    )
    output = block_tail(
        query, own_kv, other_kv, stream.reshape(-1, width), out_space, gain_time, qkv_time,
        out_time,
    )
    return output.reshape(frames, zdev, grid, grid, width)


def solution(mesh):
    placed = (P("tm", "tok", None, None, None), P(), P(), P(), P(), P(), P(), P(), P())
    return jax.shard_map(
        local,
        mesh=mesh,
        in_specs=placed,
        out_specs=P("tm", "tok", None, None, None),
        check_vma=False,
    )
```

```python
import jax
import jax.numpy as jnp
from jax import lax
from jax.sharding import PartitionSpec as P
from jax.experimental import pallas as pl
from jax.experimental.pallas import tpu as pltpu
import functools

D = 512
H = 8
WIN = 4


def extended(block, sides, width):
    for axis, dim in sides:
        count = lax.axis_size(axis)
        forward = [(i, i + 1) for i in range(count - 1)]
        backward = [(target, source) for source, target in forward]
        low = lax.ppermute(
            lax.slice_in_dim(block, block.shape[dim] - width, None, axis=dim), axis, forward
        )
        high = lax.ppermute(lax.slice_in_dim(block, 0, width, axis=dim), axis, backward)
        block = jnp.concatenate([low, block, high], axis=dim)
    return block


def from_behind(value, axis, steps):
    count = lax.axis_size(axis)
    leading, last = (max(0, -steps), min(count, count - steps))
    return lax.ppermute(value, axis, [(source, source + steps) for source in range(leading, last)])


def rms_scale(values, gain):
    mean_sq = jnp.mean(values * values, axis=-1, keepdims=True)
    return values * lax.rsqrt(mean_sq + 1e-06) * gain.astype(jnp.float32)


def split_heads(block, count, head_size):
    return block.reshape(block.shape[0], count, head_size).transpose(1, 0, 2)


def attend(query, keys, values):
    rows, cols = query.shape
    head_size = D // H
    count = cols // head_size
    scale = head_size ** (-0.5)

    def one_head(parts):
        q_one, k_one, v_one = parts
        scores = jnp.dot(q_one, k_one.T, preferred_element_type=jnp.float32) * scale
        expo = jnp.exp(scores)
        mixed = jnp.dot(expo.astype(jnp.bfloat16), v_one, preferred_element_type=jnp.float32)
        return (mixed / jnp.sum(expo, axis=-1, keepdims=True)).astype(jnp.bfloat16)

    parts = (
        split_heads(query, count, head_size),
        split_heads(keys, count, head_size),
        split_heads(values, count, head_size),
    )
    result = lax.map(one_head, parts)
    return result.transpose(1, 0, 2).reshape(rows, cols)


def conv_kernel(e_ref, t_ref, o_ref):
    planes, rows, lanes_x, width = o_ref.shape

    def plane(z, carry):
        parts = []
        for dx in range(3):
            acc = None
            for dz in range(3):
                for dy in range(3):
                    tap = t_ref[pl.ds(9 * dz + 3 * dy + dx, 1), :]
                    term = e_ref[z + dz, dy:dy + rows] * tap
                    acc = term if acc is None else acc + term
            parts.append(acc)
        conv = (
            pltpu.roll(parts[0], 1, 1) + parts[1] + pltpu.roll(parts[2], lanes_x - 1, 1)
        )
        o_ref[z] = (e_ref[z + 1, 1:1 + rows] + conv).astype(o_ref.dtype)
        return carry

    lax.fori_loop(0, planes, plane, 0)


def depthwise(ext, taps):
    depth, grid, _, width = ext.shape
    planes = depth - 2
    padded = jnp.pad(ext.astype(jnp.float32), ((0, 0), (1, 1), (1, 3), (0, 0)))
    vmem = pl.BlockSpec(memory_space=pltpu.VMEM)
    out = pl.pallas_call(
        conv_kernel,
        out_shape=jax.ShapeDtypeStruct((planes, grid, grid + 4, width), jnp.bfloat16),
        in_specs=[vmem, vmem],
        out_specs=vmem,
        compiler_params=pltpu.CompilerParams(vmem_limit_bytes=32 * 1024 * 1024),
    )(padded, taps.astype(jnp.float32))
    return out[:, :, 1:1 + grid]


def block_kernel(
    chunks, ws_ref, gain_s_ref, kv_ref, other_ref, stream_ref, wo_ref, gain_ref, wt_ref, wout_ref,
    out_ref, stream2_ref, own, query2, hist, mixed, total, sum_ref, send_sem, recv_sem,
):
    me = lax.axis_index("tm")
    count = lax.axis_size("tm")
    core = lax.axis_index("tok")
    has_left = me > 0
    has_right = me < count - 1
    rows_all, width = own.shape
    rows = rows_all // chunks
    head_size = width // H
    scale = head_size ** (-0.5)
    lanes = 2 * head_size
    mesh_ids = pl.DeviceIdType.MESH

    @pl.when(jnp.logical_not(has_left))
    def _():
        hist[...] = jnp.zeros_like(hist)

    barrier = pltpu.get_barrier_semaphore()

    @pl.when(has_left)
    def _():
        pl.semaphore_signal(barrier, inc=1, device_id=(me - 1, core), device_id_type=mesh_ids)

    @pl.when(has_right)
    def _():
        pl.semaphore_signal(barrier, inc=1, device_id=(me + 1, core), device_id_type=mesh_ids)

    @pl.when(jnp.logical_and(has_left, has_right))
    def _():
        pl.semaphore_wait(barrier, 2)

    @pl.when(jnp.logical_xor(has_left, has_right))
    def _():
        pl.semaphore_wait(barrier, 1)

    def span_of(piece):
        return pl.ds(pl.multiple_of(piece * rows, 8), rows)

    def copy_of(hop, piece):
        span = span_of(piece)
        source = own.at[span] if hop == 0 else hist.at[hop - 1, span]
        return pltpu.make_async_remote_copy(
            src_ref=source,
            dst_ref=hist.at[hop, span],
            send_sem=send_sem.at[hop, piece],
            recv_sem=recv_sem.at[hop, piece],
            device_id=(me + 1, core),
            device_id_type=mesh_ids,
        )

    lane = lax.broadcasted_iota(jnp.int32, (1, lanes), 1)
    first_half = lane < head_size
    heads = lax.broadcasted_iota(jnp.int32, (width, width), 0) // head_size
    same_head = heads == lax.broadcasted_iota(jnp.int32, (width, width), 1) // head_size
    sum_ref[...] = same_head.astype(jnp.bfloat16)

    def add_term(block, span, valid, first):
        kv = jnp.dot(block, wt_ref[:, width:], preferred_element_type=jnp.float32).astype(jnp.bfloat16)
        keys2 = kv[:, :width].astype(jnp.float32)
        values2 = kv[:, width:].astype(jnp.float32)
        prod = query2[span, :].astype(jnp.float32) * keys2
        high = prod.astype(jnp.bfloat16)
        low = (prod - high.astype(jnp.float32)).astype(jnp.bfloat16)
        summer = sum_ref[...]
        scores = (
            jnp.dot(high, summer, preferred_element_type=jnp.float32)
            + jnp.dot(low, summer, preferred_element_type=jnp.float32)
        ) * scale
        expo = jnp.where(valid, jnp.exp(scores), 0.0)
        part = expo.astype(jnp.bfloat16).astype(jnp.float32) * values2
        if first:
            mixed[span, :] = part
            total[span, :] = expo
        else:
            mixed[span, :] += part
            total[span, :] += expo

    def space_step(piece, carry):
        span = span_of(piece)
        pieces = []
        current = stream_ref[span, :].astype(jnp.float32)
        mean_cur = jnp.mean(current * current, axis=-1, keepdims=True)
        normed = (current * lax.rsqrt(mean_cur + 1e-06) * gain_s_ref[...]).astype(jnp.bfloat16)
        query_s = jnp.dot(normed, ws_ref[:, :width], preferred_element_type=jnp.float32).astype(
            jnp.bfloat16
        )
        for pair in range(width // lanes):
            cols = slice(pair * lanes, (pair + 1) * lanes)
            q = query_s[:, cols]
            key_cols = slice(width + pair * lanes, width + (pair + 1) * lanes)
            sources = (
                (kv_ref[:, cols], kv_ref[:, key_cols]),
                (other_ref[:, cols], other_ref[:, key_cols]),
            )
            outs = []
            for mask in (first_half, jnp.logical_not(first_half)):
                q_one = jnp.where(mask, q, jnp.zeros_like(q))
                rowsum = None
                mixed_one = None
                for k, v in sources:
                    scores = lax.dot_general(
                        q_one, k, (((1,), (1,)), ((), ())), preferred_element_type=jnp.float32
                    ) * scale
                    expo = jnp.exp(scores)
                    part_sum = jnp.sum(expo, axis=-1, keepdims=True)
                    part = jnp.dot(
                        expo.astype(jnp.bfloat16), v, preferred_element_type=jnp.float32
                    )
                    rowsum = part_sum if rowsum is None else rowsum + part_sum
                    mixed_one = part if mixed_one is None else mixed_one + part
                outs.append(mixed_one / rowsum)
            pieces.append(jnp.where(first_half, outs[0], outs[1]).astype(jnp.bfloat16))
        spatial = jnp.concatenate(pieces, axis=1)
        stream2 = (
            stream_ref[span, :].astype(jnp.float32)
            + jnp.dot(spatial, wo_ref[...], preferred_element_type=jnp.float32)
        ).astype(jnp.bfloat16)
        stream2_ref[span, :] = stream2
        values = stream2.astype(jnp.float32)
        mean_sq = jnp.mean(values * values, axis=-1, keepdims=True)
        normed2 = (values * lax.rsqrt(mean_sq + 1e-06) * gain_ref[...]).astype(jnp.bfloat16)
        own[span, :] = normed2
        query2[span, :] = jnp.dot(
            normed2, wt_ref[:, :width], preferred_element_type=jnp.float32
        ).astype(jnp.bfloat16)

        add_term(own[span, :], span, True, True)

        @pl.when(has_right)
        def _():
            copy_of(0, piece).start()

        return carry

    lax.fori_loop(0, chunks, space_step, 0)

    for hop in range(WIN):
        def hop_step(piece, carry, hop=hop):
            span = span_of(piece)

            @pl.when(has_left)
            def _():
                copy_of(hop, piece).wait_recv()

            if hop + 1 < WIN:
                @pl.when(has_right)
                def _():
                    copy_of(hop + 1, piece).start()

            add_term(hist[hop, span, :], span, me - (hop + 1) >= 0, False)
            if hop + 1 == WIN:
                temporal = (mixed[span, :] / total[span, :]).astype(jnp.bfloat16)
                out_ref[span, :] = (
                    stream2_ref[span, :].astype(jnp.float32)
                    + jnp.dot(temporal, wout_ref[...], preferred_element_type=jnp.float32)
                ).astype(out_ref.dtype)
            return carry

        lax.fori_loop(0, chunks, hop_step, 0)

    @pl.when(has_right)
    def _():
        for hop in range(WIN):
            for piece in range(chunks):
                copy_of(hop, piece).wait_send()


def block_tail(
    qkv_space, gain_space, keys_values, other, stream, out_space, gain_time, qkv_time, out_time,
    chunks=6,
):
    rows, width = stream.shape
    gain = gain_time.astype(jnp.float32).reshape(1, width)
    gain_s = gain_space.astype(jnp.float32).reshape(1, width)
    vmem = pl.BlockSpec(memory_space=pltpu.VMEM)
    plane = jax.ShapeDtypeStruct((rows, width), jnp.bfloat16)
    return pl.pallas_call(
        functools.partial(block_kernel, chunks),
        out_shape=plane,
        in_specs=[vmem] * 9,
        out_specs=vmem,
        scratch_shapes=[
            pltpu.VMEM((rows, width), jnp.bfloat16),
            pltpu.VMEM((rows, width), jnp.bfloat16),
            pltpu.VMEM((rows, width), jnp.bfloat16),
            pltpu.VMEM((WIN, rows, width), jnp.bfloat16),
            pltpu.VMEM((rows, width), jnp.float32),
            pltpu.VMEM((rows, width), jnp.float32),
            pltpu.VMEM((width, width), jnp.bfloat16),
            pltpu.SemaphoreType.DMA((WIN, chunks)),
            pltpu.SemaphoreType.DMA((WIN, chunks)),
        ],
        compiler_params=pltpu.CompilerParams(
            collective_id=0, has_side_effects=True, vmem_limit_bytes=56 * 1024 * 1024
        ),
    )(qkv_space, gain_s, keys_values, other, stream, out_space, gain, qkv_time, out_time)


def local(
    patches,
    patch_weight,
    conv_taps,
    gain_space,
    qkv_space,
    out_space,
    gain_time,
    qkv_time,
    out_time,
):
    frames, zdev, grid, _, patch = patches.shape
    width = patch_weight.shape[1]
    tokens = zdev * grid * grid
    embed = jnp.dot(patches, patch_weight, preferred_element_type=jnp.float32).astype(
        jnp.bfloat16
    )
    if lax.axis_size("tok") == 2:
        side = lax.axis_index("tok")
        edge = lax.dynamic_slice_in_dim(embed, jnp.where(side == 0, zdev - 1, 0), 1, axis=1)
        halo = lax.ppermute(edge, "tok", [(0, 1), (1, 0)])
        empty = jnp.zeros_like(halo)
        low = jnp.where(side == 1, halo, empty)
        high = jnp.where(side == 0, halo, empty)
        padded = jnp.concatenate([low, embed, high], axis=1)
    else:
        padded = extended(embed, (("tok", 1),), 1)
    stream = depthwise(padded[0], conv_taps).reshape(frames, tokens, width)
    normed = rms_scale(stream.astype(jnp.float32), gain_space).astype(jnp.bfloat16)
    flat = normed.reshape(-1, width)
    own_kv = jnp.dot(flat, qkv_space[:, width:], preferred_element_type=jnp.float32).astype(
        jnp.bfloat16
    )
    count = lax.axis_size("tok")
    other_kv = lax.ppermute(own_kv, "tok", [(i, (i + 1) % count) for i in range(count)])
    output = block_tail(
        qkv_space, gain_space, own_kv, other_kv, stream.reshape(-1, width), out_space,
        gain_time, qkv_time, out_time,
    )
    return output.reshape(frames, zdev, grid, grid, width)


def solution(mesh):
    placed = (P("tm", "tok", None, None, None), P(), P(), P(), P(), P(), P(), P(), P())
    return jax.shard_map(
        local,
        mesh=mesh,
        in_specs=placed,
        out_specs=P("tm", "tok", None, None, None),
        check_vma=False,
    )
```

```python
import jax
import jax.numpy as jnp
from jax import lax
from jax.sharding import PartitionSpec as P
from jax.experimental import pallas as pl
from jax.experimental.pallas import tpu as pltpu
import functools

D = 512
H = 8
WIN = 4


def extended(block, sides, width):
    for axis, dim in sides:
        count = lax.axis_size(axis)
        forward = [(i, i + 1) for i in range(count - 1)]
        backward = [(target, source) for source, target in forward]
        low = lax.ppermute(
            lax.slice_in_dim(block, block.shape[dim] - width, None, axis=dim), axis, forward
        )
        high = lax.ppermute(lax.slice_in_dim(block, 0, width, axis=dim), axis, backward)
        block = jnp.concatenate([low, block, high], axis=dim)
    return block


def from_behind(value, axis, steps):
    count = lax.axis_size(axis)
    leading, last = (max(0, -steps), min(count, count - steps))
    return lax.ppermute(value, axis, [(source, source + steps) for source in range(leading, last)])


def rms_scale(values, gain):
    mean_sq = jnp.mean(values * values, axis=-1, keepdims=True)
    return values * lax.rsqrt(mean_sq + 1e-06) * gain.astype(jnp.float32)


def split_heads(block, count, head_size):
    return block.reshape(block.shape[0], count, head_size).transpose(1, 0, 2)


def attend(query, keys, values):
    rows, cols = query.shape
    head_size = D // H
    count = cols // head_size
    scale = head_size ** (-0.5)

    def one_head(parts):
        q_one, k_one, v_one = parts
        scores = jnp.dot(q_one, k_one.T, preferred_element_type=jnp.float32) * scale
        expo = jnp.exp(scores)
        mixed = jnp.dot(expo.astype(jnp.bfloat16), v_one, preferred_element_type=jnp.float32)
        return (mixed / jnp.sum(expo, axis=-1, keepdims=True)).astype(jnp.bfloat16)

    parts = (
        split_heads(query, count, head_size),
        split_heads(keys, count, head_size),
        split_heads(values, count, head_size),
    )
    result = lax.map(one_head, parts)
    return result.transpose(1, 0, 2).reshape(rows, cols)


def conv_kernel(e_ref, t_ref, o_ref):
    planes, rows, lanes_x, width = o_ref.shape

    def plane(z, carry):
        parts = []
        for dx in range(3):
            acc = None
            for dz in range(3):
                for dy in range(3):
                    tap = t_ref[pl.ds(9 * dz + 3 * dy + dx, 1), :]
                    term = e_ref[z + dz, dy:dy + rows] * tap
                    acc = term if acc is None else acc + term
            parts.append(acc)
        conv = (
            pltpu.roll(parts[0], 1, 1) + parts[1] + pltpu.roll(parts[2], lanes_x - 1, 1)
        )
        o_ref[z] = (e_ref[z + 1, 1:1 + rows] + conv).astype(o_ref.dtype)
        return carry

    lax.fori_loop(0, planes, plane, 0)


def depthwise(ext, taps):
    depth, grid, _, width = ext.shape
    planes = depth - 2
    padded = jnp.pad(ext.astype(jnp.float32), ((0, 0), (1, 1), (1, 3), (0, 0)))
    vmem = pl.BlockSpec(memory_space=pltpu.VMEM)
    out = pl.pallas_call(
        conv_kernel,
        out_shape=jax.ShapeDtypeStruct((planes, grid, grid + 4, width), jnp.bfloat16),
        in_specs=[vmem, vmem],
        out_specs=vmem,
        compiler_params=pltpu.CompilerParams(vmem_limit_bytes=32 * 1024 * 1024),
    )(padded, taps.astype(jnp.float32))
    return out[:, :, 1:1 + grid]


def block_kernel(
    chunks, q_ref, kv_ref, other_ref, stream_ref, wo_ref, gain_ref, wt_ref, wout_ref,
    out_ref, stream2_ref, own, query2, hist, mixed, total, sum_ref, send_sem, recv_sem,
):
    me = lax.axis_index("tm")
    count = lax.axis_size("tm")
    core = lax.axis_index("tok")
    has_left = me > 0
    has_right = me < count - 1
    rows_all, width = own.shape
    rows = rows_all // chunks
    head_size = width // H
    scale = head_size ** (-0.5)
    lanes = 2 * head_size
    mesh_ids = pl.DeviceIdType.MESH

    @pl.when(jnp.logical_not(has_left))
    def _():
        hist[...] = jnp.zeros_like(hist)

    barrier = pltpu.get_barrier_semaphore()

    @pl.when(has_left)
    def _():
        pl.semaphore_signal(barrier, inc=1, device_id=(me - 1, core), device_id_type=mesh_ids)

    @pl.when(has_right)
    def _():
        pl.semaphore_signal(barrier, inc=1, device_id=(me + 1, core), device_id_type=mesh_ids)

    @pl.when(jnp.logical_and(has_left, has_right))
    def _():
        pl.semaphore_wait(barrier, 2)

    @pl.when(jnp.logical_xor(has_left, has_right))
    def _():
        pl.semaphore_wait(barrier, 1)

    def span_of(piece):
        return pl.ds(pl.multiple_of(piece * rows, 8), rows)

    def copy_of(hop, piece):
        span = span_of(piece)
        source = own.at[span] if hop == 0 else hist.at[hop - 1, span]
        return pltpu.make_async_remote_copy(
            src_ref=source,
            dst_ref=hist.at[hop, span],
            send_sem=send_sem.at[hop, piece],
            recv_sem=recv_sem.at[hop, piece],
            device_id=(me + 1, core),
            device_id_type=mesh_ids,
        )

    lane = lax.broadcasted_iota(jnp.int32, (1, lanes), 1)
    first_half = lane < head_size
    heads = lax.broadcasted_iota(jnp.int32, (width, width), 0) // head_size
    same_head = heads == lax.broadcasted_iota(jnp.int32, (width, width), 1) // head_size
    sum_ref[...] = same_head.astype(jnp.bfloat16)

    def add_term(block, span, valid, first):
        kv = jnp.dot(block, wt_ref[:, width:], preferred_element_type=jnp.float32).astype(jnp.bfloat16)
        keys2 = kv[:, :width].astype(jnp.float32)
        values2 = kv[:, width:].astype(jnp.float32)
        prod = query2[span, :].astype(jnp.float32) * keys2
        high = prod.astype(jnp.bfloat16)
        low = (prod - high.astype(jnp.float32)).astype(jnp.bfloat16)
        summer = sum_ref[...]
        scores = (
            jnp.dot(high, summer, preferred_element_type=jnp.float32)
            + jnp.dot(low, summer, preferred_element_type=jnp.float32)
        ) * scale
        expo = jnp.where(valid, jnp.exp(scores), 0.0)
        part = expo.astype(jnp.bfloat16).astype(jnp.float32) * values2
        if first:
            mixed[span, :] = part
            total[span, :] = expo
        else:
            mixed[span, :] += part
            total[span, :] += expo

    def space_step(piece, carry):
        span = span_of(piece)
        pieces = []
        for pair in range(width // lanes):
            cols = slice(pair * lanes, (pair + 1) * lanes)
            q = q_ref[span, cols]
            key_cols = slice(width + pair * lanes, width + (pair + 1) * lanes)
            sources = (
                (kv_ref[:, cols], kv_ref[:, key_cols]),
                (other_ref[:, cols], other_ref[:, key_cols]),
            )
            outs = []
            for mask in (first_half, jnp.logical_not(first_half)):
                q_one = jnp.where(mask, q, jnp.zeros_like(q))
                rowsum = None
                mixed_one = None
                for k, v in sources:
                    scores = lax.dot_general(
                        q_one, k, (((1,), (1,)), ((), ())), preferred_element_type=jnp.float32
                    ) * scale
                    expo = jnp.exp(scores)
                    part_sum = jnp.sum(expo, axis=-1, keepdims=True)
                    part = jnp.dot(
                        expo.astype(jnp.bfloat16), v, preferred_element_type=jnp.float32
                    )
                    rowsum = part_sum if rowsum is None else rowsum + part_sum
                    mixed_one = part if mixed_one is None else mixed_one + part
                outs.append(mixed_one / rowsum)
            pieces.append(jnp.where(first_half, outs[0], outs[1]).astype(jnp.bfloat16))
        spatial = jnp.concatenate(pieces, axis=1)
        stream2 = (
            stream_ref[span, :].astype(jnp.float32)
            + jnp.dot(spatial, wo_ref[...], preferred_element_type=jnp.float32)
        ).astype(jnp.bfloat16)
        stream2_ref[span, :] = stream2
        values = stream2.astype(jnp.float32)
        mean_sq = jnp.mean(values * values, axis=-1, keepdims=True)
        normed2 = (values * lax.rsqrt(mean_sq + 1e-06) * gain_ref[...]).astype(jnp.bfloat16)
        own[span, :] = normed2
        query2[span, :] = jnp.dot(
            normed2, wt_ref[:, :width], preferred_element_type=jnp.float32
        ).astype(jnp.bfloat16)

        add_term(own[span, :], span, True, True)

        @pl.when(has_right)
        def _():
            copy_of(0, piece).start()

        return carry

    lax.fori_loop(0, chunks, space_step, 0)

    for hop in range(WIN):
        def hop_step(piece, carry, hop=hop):
            span = span_of(piece)

            @pl.when(has_left)
            def _():
                copy_of(hop, piece).wait_recv()

            if hop + 1 < WIN:
                @pl.when(has_right)
                def _():
                    copy_of(hop + 1, piece).start()

            add_term(hist[hop, span, :], span, me - (hop + 1) >= 0, False)
            if hop + 1 == WIN:
                temporal = (mixed[span, :] / total[span, :]).astype(jnp.bfloat16)
                out_ref[span, :] = (
                    stream2_ref[span, :].astype(jnp.float32)
                    + jnp.dot(temporal, wout_ref[...], preferred_element_type=jnp.float32)
                ).astype(out_ref.dtype)
            return carry

        lax.fori_loop(0, chunks, hop_step, 0)

    @pl.when(has_right)
    def _():
        for hop in range(WIN):
            for piece in range(chunks):
                copy_of(hop, piece).wait_send()


def block_tail(
    query, keys_values, other, stream, out_space, gain_time, qkv_time, out_time, chunks=3
):
    rows, width = stream.shape
    gain = gain_time.astype(jnp.float32).reshape(1, width)
    vmem = pl.BlockSpec(memory_space=pltpu.VMEM)
    plane = jax.ShapeDtypeStruct((rows, width), jnp.bfloat16)
    return pl.pallas_call(
        functools.partial(block_kernel, chunks),
        out_shape=plane,
        in_specs=[vmem] * 8,
        out_specs=vmem,
        scratch_shapes=[
            pltpu.VMEM((rows, width), jnp.bfloat16),
            pltpu.VMEM((rows, width), jnp.bfloat16),
            pltpu.VMEM((rows, width), jnp.bfloat16),
            pltpu.VMEM((WIN, rows, width), jnp.bfloat16),
            pltpu.VMEM((rows, width), jnp.float32),
            pltpu.VMEM((rows, width), jnp.float32),
            pltpu.VMEM((width, width), jnp.bfloat16),
            pltpu.SemaphoreType.DMA((WIN, chunks)),
            pltpu.SemaphoreType.DMA((WIN, chunks)),
        ],
        compiler_params=pltpu.CompilerParams(
            collective_id=0, has_side_effects=True, vmem_limit_bytes=56 * 1024 * 1024
        ),
    )(query, keys_values, other, stream, out_space, gain, qkv_time, out_time)


def local(
    patches,
    patch_weight,
    conv_taps,
    gain_space,
    qkv_space,
    out_space,
    gain_time,
    qkv_time,
    out_time,
):
    frames, zdev, grid, _, patch = patches.shape
    width = patch_weight.shape[1]
    tokens = zdev * grid * grid
    embed = jnp.dot(patches, patch_weight, preferred_element_type=jnp.float32).astype(
        jnp.bfloat16
    )
    if lax.axis_size("tok") == 2:
        side = lax.axis_index("tok")
        edge = lax.dynamic_slice_in_dim(embed, jnp.where(side == 0, zdev - 1, 0), 1, axis=1)
        halo = lax.ppermute(edge, "tok", [(0, 1), (1, 0)])
        empty = jnp.zeros_like(halo)
        low = jnp.where(side == 1, halo, empty)
        high = jnp.where(side == 0, halo, empty)
        padded = jnp.concatenate([low, embed, high], axis=1)
    else:
        padded = extended(embed, (("tok", 1),), 1)
    stream = depthwise(padded[0], conv_taps).reshape(frames, tokens, width)
    normed = rms_scale(stream.astype(jnp.float32), gain_space).astype(jnp.bfloat16)
    flat = normed.reshape(-1, width)
    own_kv = jnp.dot(flat, qkv_space[:, width:], preferred_element_type=jnp.float32).astype(
        jnp.bfloat16
    )
    count = lax.axis_size("tok")
    other_kv = lax.ppermute(own_kv, "tok", [(i, (i + 1) % count) for i in range(count)])
    query = jnp.dot(flat, qkv_space[:, :width], preferred_element_type=jnp.float32).astype(
        jnp.bfloat16
    )
    output = block_tail(
        query, own_kv, other_kv, stream.reshape(-1, width), out_space, gain_time, qkv_time,
        out_time,
    )
    return output.reshape(frames, zdev, grid, grid, width)


def solution(mesh):
    placed = (P("tm", "tok", None, None, None), P(), P(), P(), P(), P(), P(), P(), P())
    return jax.shard_map(
        local,
        mesh=mesh,
        in_specs=placed,
        out_specs=P("tm", "tok", None, None, None),
        check_vma=False,
    )
```

```python
import jax
import jax.numpy as jnp
from jax import lax
from jax.sharding import PartitionSpec as P
from jax.experimental import pallas as pl
from jax.experimental.pallas import tpu as pltpu
import functools

D = 512
H = 8
WIN = 4


def extended(block, sides, width):
    for axis, dim in sides:
        count = lax.axis_size(axis)
        forward = [(i, i + 1) for i in range(count - 1)]
        backward = [(target, source) for source, target in forward]
        low = lax.ppermute(
            lax.slice_in_dim(block, block.shape[dim] - width, None, axis=dim), axis, forward
        )
        high = lax.ppermute(lax.slice_in_dim(block, 0, width, axis=dim), axis, backward)
        block = jnp.concatenate([low, block, high], axis=dim)
    return block


def from_behind(value, axis, steps):
    count = lax.axis_size(axis)
    leading, last = (max(0, -steps), min(count, count - steps))
    return lax.ppermute(value, axis, [(source, source + steps) for source in range(leading, last)])


def rms_scale(values, gain):
    mean_sq = jnp.mean(values * values, axis=-1, keepdims=True)
    return values * lax.rsqrt(mean_sq + 1e-06) * gain.astype(jnp.float32)


def split_heads(block, count, head_size):
    return block.reshape(block.shape[0], count, head_size).transpose(1, 0, 2)


def attend(query, keys, values):
    rows, cols = query.shape
    head_size = D // H
    count = cols // head_size
    scale = head_size ** (-0.5)

    def one_head(parts):
        q_one, k_one, v_one = parts
        scores = jnp.dot(q_one, k_one.T, preferred_element_type=jnp.float32) * scale
        expo = jnp.exp(scores)
        mixed = jnp.dot(expo.astype(jnp.bfloat16), v_one, preferred_element_type=jnp.float32)
        return (mixed / jnp.sum(expo, axis=-1, keepdims=True)).astype(jnp.bfloat16)

    parts = (
        split_heads(query, count, head_size),
        split_heads(keys, count, head_size),
        split_heads(values, count, head_size),
    )
    result = lax.map(one_head, parts)
    return result.transpose(1, 0, 2).reshape(rows, cols)


def conv_kernel(e_ref, t_ref, o_ref):
    planes, rows, lanes_x, width = o_ref.shape

    def plane(z, carry):
        parts = []
        for dx in range(3):
            acc = None
            for dz in range(3):
                for dy in range(3):
                    tap = t_ref[pl.ds(9 * dz + 3 * dy + dx, 1), :]
                    term = e_ref[z + dz, dy:dy + rows] * tap
                    acc = term if acc is None else acc + term
            parts.append(acc)
        conv = (
            pltpu.roll(parts[0], 1, 1) + parts[1] + pltpu.roll(parts[2], lanes_x - 1, 1)
        )
        o_ref[z] = (e_ref[z + 1, 1:1 + rows] + conv).astype(o_ref.dtype)
        return carry

    lax.fori_loop(0, planes, plane, 0)


def depthwise(ext, taps):
    depth, grid, _, width = ext.shape
    planes = depth - 2
    padded = jnp.pad(ext.astype(jnp.float32), ((0, 0), (1, 1), (1, 3), (0, 0)))
    vmem = pl.BlockSpec(memory_space=pltpu.VMEM)
    out = pl.pallas_call(
        conv_kernel,
        out_shape=jax.ShapeDtypeStruct((planes, grid, grid + 4, width), jnp.bfloat16),
        in_specs=[vmem, vmem],
        out_specs=vmem,
        compiler_params=pltpu.CompilerParams(vmem_limit_bytes=32 * 1024 * 1024),
    )(padded, taps.astype(jnp.float32))
    return out[:, :, 1:1 + grid]


def block_kernel(
    chunks, q_ref, kv_ref, other_ref, stream_ref, wo_ref, gain_ref, wt_ref, wout_ref,
    out_ref, stream2_ref, own, query2, hist, mixed, total, sum_ref, send_sem, recv_sem,
):
    me = lax.axis_index("tm")
    count = lax.axis_size("tm")
    core = lax.axis_index("tok")
    has_left = me > 0
    has_right = me < count - 1
    rows_all, width = own.shape
    rows = rows_all // chunks
    head_size = width // H
    scale = head_size ** (-0.5)
    lanes = 2 * head_size
    mesh_ids = pl.DeviceIdType.MESH

    @pl.when(jnp.logical_not(has_left))
    def _():
        hist[...] = jnp.zeros_like(hist)

    barrier = pltpu.get_barrier_semaphore()

    @pl.when(has_left)
    def _():
        pl.semaphore_signal(barrier, inc=1, device_id=(me - 1, core), device_id_type=mesh_ids)

    @pl.when(has_right)
    def _():
        pl.semaphore_signal(barrier, inc=1, device_id=(me + 1, core), device_id_type=mesh_ids)

    @pl.when(jnp.logical_and(has_left, has_right))
    def _():
        pl.semaphore_wait(barrier, 2)

    @pl.when(jnp.logical_xor(has_left, has_right))
    def _():
        pl.semaphore_wait(barrier, 1)

    def span_of(piece):
        return pl.ds(pl.multiple_of(piece * rows, 8), rows)

    def copy_of(hop, piece):
        span = span_of(piece)
        source = own.at[span] if hop == 0 else hist.at[hop - 1, span]
        return pltpu.make_async_remote_copy(
            src_ref=source,
            dst_ref=hist.at[hop, span],
            send_sem=send_sem.at[hop, piece],
            recv_sem=recv_sem.at[hop, piece],
            device_id=(me + 1, core),
            device_id_type=mesh_ids,
        )

    lane = lax.broadcasted_iota(jnp.int32, (1, lanes), 1)
    first_half = lane < head_size
    heads = lax.broadcasted_iota(jnp.int32, (width, width), 0) // head_size
    same_head = heads == lax.broadcasted_iota(jnp.int32, (width, width), 1) // head_size
    sum_ref[...] = same_head.astype(jnp.bfloat16)

    def add_term(block, span, valid, first):
        kv = jnp.dot(block, wt_ref[:, width:], preferred_element_type=jnp.float32).astype(jnp.bfloat16)
        keys2 = kv[:, :width].astype(jnp.float32)
        values2 = kv[:, width:].astype(jnp.float32)
        prod = query2[span, :].astype(jnp.float32) * keys2
        high = prod.astype(jnp.bfloat16)
        low = (prod - high.astype(jnp.float32)).astype(jnp.bfloat16)
        summer = sum_ref[...]
        scores = (
            jnp.dot(high, summer, preferred_element_type=jnp.float32)
            + jnp.dot(low, summer, preferred_element_type=jnp.float32)
        ) * scale
        expo = jnp.where(valid, jnp.exp(scores), 0.0)
        part = expo.astype(jnp.bfloat16).astype(jnp.float32) * values2
        if first:
            mixed[span, :] = part
            total[span, :] = expo
        else:
            mixed[span, :] += part
            total[span, :] += expo

    def space_step(piece, carry):
        span = span_of(piece)
        pieces = []
        for pair in range(width // lanes):
            cols = slice(pair * lanes, (pair + 1) * lanes)
            q = q_ref[span, cols]
            key_cols = slice(width + pair * lanes, width + (pair + 1) * lanes)
            sources = (
                (kv_ref[:, cols], kv_ref[:, key_cols]),
                (other_ref[:, cols], other_ref[:, key_cols]),
            )
            outs = []
            for mask in (first_half, jnp.logical_not(first_half)):
                q_one = jnp.where(mask, q, jnp.zeros_like(q))
                rowsum = None
                mixed_one = None
                for k, v in sources:
                    scores = lax.dot_general(
                        q_one, k, (((1,), (1,)), ((), ())), preferred_element_type=jnp.float32
                    ) * scale
                    expo = jnp.exp(scores)
                    part_sum = jnp.sum(expo, axis=-1, keepdims=True)
                    part = jnp.dot(
                        expo.astype(jnp.bfloat16), v, preferred_element_type=jnp.float32
                    )
                    rowsum = part_sum if rowsum is None else rowsum + part_sum
                    mixed_one = part if mixed_one is None else mixed_one + part
                outs.append(mixed_one / rowsum)
            pieces.append(jnp.where(first_half, outs[0], outs[1]).astype(jnp.bfloat16))
        spatial = jnp.concatenate(pieces, axis=1)
        stream2 = (
            stream_ref[span, :].astype(jnp.float32)
            + jnp.dot(spatial, wo_ref[...], preferred_element_type=jnp.float32)
        ).astype(jnp.bfloat16)
        stream2_ref[span, :] = stream2
        values = stream2.astype(jnp.float32)
        mean_sq = jnp.mean(values * values, axis=-1, keepdims=True)
        normed2 = (values * lax.rsqrt(mean_sq + 1e-06) * gain_ref[...]).astype(jnp.bfloat16)
        own[span, :] = normed2
        query2[span, :] = jnp.dot(
            normed2, wt_ref[:, :width], preferred_element_type=jnp.float32
        ).astype(jnp.bfloat16)

        add_term(own[span, :], span, True, True)

        @pl.when(has_right)
        def _():
            copy_of(0, piece).start()

        return carry

    lax.fori_loop(0, chunks, space_step, 0)

    for hop in range(WIN):
        def hop_step(piece, carry, hop=hop):
            span = span_of(piece)

            @pl.when(has_left)
            def _():
                copy_of(hop, piece).wait_recv()

            if hop + 1 < WIN:
                @pl.when(has_right)
                def _():
                    copy_of(hop + 1, piece).start()

            add_term(hist[hop, span, :], span, me - (hop + 1) >= 0, False)
            if hop + 1 == WIN:
                temporal = (mixed[span, :] / total[span, :]).astype(jnp.bfloat16)
                out_ref[span, :] = (
                    stream2_ref[span, :].astype(jnp.float32)
                    + jnp.dot(temporal, wout_ref[...], preferred_element_type=jnp.float32)
                ).astype(out_ref.dtype)
            return carry

        lax.fori_loop(0, chunks, hop_step, 0)

    @pl.when(has_right)
    def _():
        for hop in range(WIN):
            for piece in range(chunks):
                copy_of(hop, piece).wait_send()


def block_tail(
    query, keys_values, other, stream, out_space, gain_time, qkv_time, out_time, chunks=2
):
    rows, width = stream.shape
    gain = gain_time.astype(jnp.float32).reshape(1, width)
    vmem = pl.BlockSpec(memory_space=pltpu.VMEM)
    plane = jax.ShapeDtypeStruct((rows, width), jnp.bfloat16)
    return pl.pallas_call(
        functools.partial(block_kernel, chunks),
        out_shape=plane,
        in_specs=[vmem] * 8,
        out_specs=vmem,
        scratch_shapes=[
            pltpu.VMEM((rows, width), jnp.bfloat16),
            pltpu.VMEM((rows, width), jnp.bfloat16),
            pltpu.VMEM((rows, width), jnp.bfloat16),
            pltpu.VMEM((WIN, rows, width), jnp.bfloat16),
            pltpu.VMEM((rows, width), jnp.float32),
            pltpu.VMEM((rows, width), jnp.float32),
            pltpu.VMEM((width, width), jnp.bfloat16),
            pltpu.SemaphoreType.DMA((WIN, chunks)),
            pltpu.SemaphoreType.DMA((WIN, chunks)),
        ],
        compiler_params=pltpu.CompilerParams(
            collective_id=0, has_side_effects=True, vmem_limit_bytes=56 * 1024 * 1024
        ),
    )(query, keys_values, other, stream, out_space, gain, qkv_time, out_time)


def local(
    patches,
    patch_weight,
    conv_taps,
    gain_space,
    qkv_space,
    out_space,
    gain_time,
    qkv_time,
    out_time,
):
    frames, zdev, grid, _, patch = patches.shape
    width = patch_weight.shape[1]
    tokens = zdev * grid * grid
    embed = jnp.dot(patches, patch_weight, preferred_element_type=jnp.float32).astype(
        jnp.bfloat16
    )
    if lax.axis_size("tok") == 2:
        side = lax.axis_index("tok")
        edge = lax.dynamic_slice_in_dim(embed, jnp.where(side == 0, zdev - 1, 0), 1, axis=1)
        halo = lax.ppermute(edge, "tok", [(0, 1), (1, 0)])
        empty = jnp.zeros_like(halo)
        low = jnp.where(side == 1, halo, empty)
        high = jnp.where(side == 0, halo, empty)
        padded = jnp.concatenate([low, embed, high], axis=1)
    else:
        padded = extended(embed, (("tok", 1),), 1)
    stream = depthwise(padded[0], conv_taps).reshape(frames, tokens, width)
    normed = rms_scale(stream.astype(jnp.float32), gain_space).astype(jnp.bfloat16)
    flat = normed.reshape(-1, width)
    own_kv = jnp.dot(flat, qkv_space[:, width:], preferred_element_type=jnp.float32).astype(
        jnp.bfloat16
    )
    count = lax.axis_size("tok")
    other_kv = lax.ppermute(own_kv, "tok", [(i, (i + 1) % count) for i in range(count)])
    query = jnp.dot(flat, qkv_space[:, :width], preferred_element_type=jnp.float32).astype(
        jnp.bfloat16
    )
    output = block_tail(
        query, own_kv, other_kv, stream.reshape(-1, width), out_space, gain_time, qkv_time,
        out_time,
    )
    return output.reshape(frames, zdev, grid, grid, width)


def solution(mesh):
    placed = (P("tm", "tok", None, None, None), P(), P(), P(), P(), P(), P(), P(), P())
    return jax.shard_map(
        local,
        mesh=mesh,
        in_specs=placed,
        out_specs=P("tm", "tok", None, None, None),
        check_vma=False,
    )
```

```python
import jax
import jax.numpy as jnp
from jax import lax
from jax.sharding import PartitionSpec as P
from jax.experimental import pallas as pl
from jax.experimental.pallas import tpu as pltpu
import functools

D = 512
H = 8
WIN = 4


def extended(block, sides, width):
    for axis, dim in sides:
        count = lax.axis_size(axis)
        forward = [(i, i + 1) for i in range(count - 1)]
        backward = [(target, source) for source, target in forward]
        low = lax.ppermute(
            lax.slice_in_dim(block, block.shape[dim] - width, None, axis=dim), axis, forward
        )
        high = lax.ppermute(lax.slice_in_dim(block, 0, width, axis=dim), axis, backward)
        block = jnp.concatenate([low, block, high], axis=dim)
    return block


def from_behind(value, axis, steps):
    count = lax.axis_size(axis)
    leading, last = (max(0, -steps), min(count, count - steps))
    return lax.ppermute(value, axis, [(source, source + steps) for source in range(leading, last)])


def rms_scale(values, gain):
    mean_sq = jnp.mean(values * values, axis=-1, keepdims=True)
    return values * lax.rsqrt(mean_sq + 1e-06) * gain.astype(jnp.float32)


def split_heads(block, count, head_size):
    return block.reshape(block.shape[0], count, head_size).transpose(1, 0, 2)


def attend(query, keys, values):
    rows, cols = query.shape
    head_size = D // H
    count = cols // head_size
    scale = head_size ** (-0.5)

    def one_head(parts):
        q_one, k_one, v_one = parts
        scores = jnp.dot(q_one, k_one.T, preferred_element_type=jnp.float32) * scale
        expo = jnp.exp(scores)
        mixed = jnp.dot(expo.astype(jnp.bfloat16), v_one, preferred_element_type=jnp.float32)
        return (mixed / jnp.sum(expo, axis=-1, keepdims=True)).astype(jnp.bfloat16)

    parts = (
        split_heads(query, count, head_size),
        split_heads(keys, count, head_size),
        split_heads(values, count, head_size),
    )
    result = lax.map(one_head, parts)
    return result.transpose(1, 0, 2).reshape(rows, cols)


def conv_kernel(e_ref, t_ref, o_ref):
    planes, rows, lanes_x, width = o_ref.shape

    def plane(z, carry):
        parts = []
        for dx in range(3):
            acc = None
            for dz in range(3):
                for dy in range(3):
                    tap = t_ref[pl.ds(9 * dz + 3 * dy + dx, 1), :]
                    term = e_ref[z + dz, dy:dy + rows].astype(jnp.float32) * tap
                    acc = term if acc is None else acc + term
            parts.append(acc)
        conv = (
            pltpu.roll(parts[0], 1, 1) + parts[1] + pltpu.roll(parts[2], lanes_x - 1, 1)
        )
        o_ref[z] = (e_ref[z + 1, 1:1 + rows].astype(jnp.float32) + conv).astype(o_ref.dtype)
        return carry

    lax.fori_loop(0, planes, plane, 0)


def depthwise(ext, taps):
    depth, grid, _, width = ext.shape
    planes = depth - 2
    padded = jnp.pad(ext, ((0, 0), (1, 1), (1, 3), (0, 0)))
    vmem = pl.BlockSpec(memory_space=pltpu.VMEM)
    out = pl.pallas_call(
        conv_kernel,
        out_shape=jax.ShapeDtypeStruct((planes, grid, grid + 4, width), jnp.bfloat16),
        in_specs=[vmem, vmem],
        out_specs=vmem,
        compiler_params=pltpu.CompilerParams(vmem_limit_bytes=32 * 1024 * 1024),
    )(padded, taps.astype(jnp.float32))
    return out[:, :, 1:1 + grid]


def block_kernel(
    chunks, q_ref, kv_ref, other_ref, stream_ref, wo_ref, gain_ref, wt_ref, wout_ref,
    out_ref, stream2_ref, own, query2, hist, mixed, total, sum_ref, send_sem, recv_sem,
):
    me = lax.axis_index("tm")
    count = lax.axis_size("tm")
    core = lax.axis_index("tok")
    has_left = me > 0
    has_right = me < count - 1
    rows_all, width = own.shape
    rows = rows_all // chunks
    head_size = width // H
    scale = head_size ** (-0.5)
    lanes = 2 * head_size
    mesh_ids = pl.DeviceIdType.MESH

    @pl.when(jnp.logical_not(has_left))
    def _():
        hist[...] = jnp.zeros_like(hist)

    barrier = pltpu.get_barrier_semaphore()

    @pl.when(has_left)
    def _():
        pl.semaphore_signal(barrier, inc=1, device_id=(me - 1, core), device_id_type=mesh_ids)

    @pl.when(has_right)
    def _():
        pl.semaphore_signal(barrier, inc=1, device_id=(me + 1, core), device_id_type=mesh_ids)

    @pl.when(jnp.logical_and(has_left, has_right))
    def _():
        pl.semaphore_wait(barrier, 2)

    @pl.when(jnp.logical_xor(has_left, has_right))
    def _():
        pl.semaphore_wait(barrier, 1)

    def span_of(piece):
        return pl.ds(pl.multiple_of(piece * rows, 8), rows)

    def copy_of(hop, piece):
        span = span_of(piece)
        source = own.at[span] if hop == 0 else hist.at[hop - 1, span]
        return pltpu.make_async_remote_copy(
            src_ref=source,
            dst_ref=hist.at[hop, span],
            send_sem=send_sem.at[hop, piece],
            recv_sem=recv_sem.at[hop, piece],
            device_id=(me + 1, core),
            device_id_type=mesh_ids,
        )

    lane = lax.broadcasted_iota(jnp.int32, (1, lanes), 1)
    first_half = lane < head_size
    heads = lax.broadcasted_iota(jnp.int32, (width, width), 0) // head_size
    same_head = heads == lax.broadcasted_iota(jnp.int32, (width, width), 1) // head_size
    sum_ref[...] = same_head.astype(jnp.bfloat16)

    def add_term(block, span, valid, first):
        kv = jnp.dot(block, wt_ref[:, width:], preferred_element_type=jnp.float32).astype(jnp.bfloat16)
        keys2 = kv[:, :width].astype(jnp.float32)
        values2 = kv[:, width:].astype(jnp.float32)
        prod = query2[span, :].astype(jnp.float32) * keys2
        high = prod.astype(jnp.bfloat16)
        low = (prod - high.astype(jnp.float32)).astype(jnp.bfloat16)
        summer = sum_ref[...]
        scores = (
            jnp.dot(high, summer, preferred_element_type=jnp.float32)
            + jnp.dot(low, summer, preferred_element_type=jnp.float32)
        ) * scale
        expo = jnp.where(valid, jnp.exp(scores), 0.0)
        part = expo.astype(jnp.bfloat16).astype(jnp.float32) * values2
        if first:
            mixed[span, :] = part
            total[span, :] = expo
        else:
            mixed[span, :] += part
            total[span, :] += expo

    def space_step(piece, carry):
        span = span_of(piece)
        pieces = []
        for pair in range(width // lanes):
            cols = slice(pair * lanes, (pair + 1) * lanes)
            q = q_ref[span, cols]
            key_cols = slice(width + pair * lanes, width + (pair + 1) * lanes)
            sources = (
                (kv_ref[:, cols], kv_ref[:, key_cols]),
                (other_ref[:, cols], other_ref[:, key_cols]),
            )
            outs = []
            for mask in (first_half, jnp.logical_not(first_half)):
                q_one = jnp.where(mask, q, jnp.zeros_like(q))
                rowsum = None
                mixed_one = None
                for k, v in sources:
                    scores = lax.dot_general(
                        q_one, k, (((1,), (1,)), ((), ())), preferred_element_type=jnp.float32
                    ) * scale
                    expo = jnp.exp(scores)
                    part_sum = jnp.sum(expo, axis=-1, keepdims=True)
                    part = jnp.dot(
                        expo.astype(jnp.bfloat16), v, preferred_element_type=jnp.float32
                    )
                    rowsum = part_sum if rowsum is None else rowsum + part_sum
                    mixed_one = part if mixed_one is None else mixed_one + part
                outs.append(mixed_one / rowsum)
            pieces.append(jnp.where(first_half, outs[0], outs[1]).astype(jnp.bfloat16))
        spatial = jnp.concatenate(pieces, axis=1)
        stream2 = (
            stream_ref[span, :].astype(jnp.float32)
            + jnp.dot(spatial, wo_ref[...], preferred_element_type=jnp.float32)
        ).astype(jnp.bfloat16)
        stream2_ref[span, :] = stream2
        values = stream2.astype(jnp.float32)
        mean_sq = jnp.mean(values * values, axis=-1, keepdims=True)
        normed2 = (values * lax.rsqrt(mean_sq + 1e-06) * gain_ref[...]).astype(jnp.bfloat16)
        own[span, :] = normed2
        query2[span, :] = jnp.dot(
            normed2, wt_ref[:, :width], preferred_element_type=jnp.float32
        ).astype(jnp.bfloat16)

        add_term(own[span, :], span, True, True)

        @pl.when(has_right)
        def _():
            copy_of(0, piece).start()

        return carry

    lax.fori_loop(0, chunks, space_step, 0)

    for hop in range(WIN):
        def hop_step(piece, carry, hop=hop):
            span = span_of(piece)

            @pl.when(has_left)
            def _():
                copy_of(hop, piece).wait_recv()

            if hop + 1 < WIN:
                @pl.when(has_right)
                def _():
                    copy_of(hop + 1, piece).start()

            add_term(hist[hop, span, :], span, me - (hop + 1) >= 0, False)
            if hop + 1 == WIN:
                temporal = (mixed[span, :] / total[span, :]).astype(jnp.bfloat16)
                out_ref[span, :] = (
                    stream2_ref[span, :].astype(jnp.float32)
                    + jnp.dot(temporal, wout_ref[...], preferred_element_type=jnp.float32)
                ).astype(out_ref.dtype)
            return carry

        lax.fori_loop(0, chunks, hop_step, 0)

    @pl.when(has_right)
    def _():
        for hop in range(WIN):
            for piece in range(chunks):
                copy_of(hop, piece).wait_send()


def block_tail(
    query, keys_values, other, stream, out_space, gain_time, qkv_time, out_time, chunks=3
):
    rows, width = stream.shape
    gain = gain_time.astype(jnp.float32).reshape(1, width)
    vmem = pl.BlockSpec(memory_space=pltpu.VMEM)
    plane = jax.ShapeDtypeStruct((rows, width), jnp.bfloat16)
    return pl.pallas_call(
        functools.partial(block_kernel, chunks),
        out_shape=plane,
        in_specs=[vmem] * 8,
        out_specs=vmem,
        scratch_shapes=[
            pltpu.VMEM((rows, width), jnp.bfloat16),
            pltpu.VMEM((rows, width), jnp.bfloat16),
            pltpu.VMEM((rows, width), jnp.bfloat16),
            pltpu.VMEM((WIN, rows, width), jnp.bfloat16),
            pltpu.VMEM((rows, width), jnp.float32),
            pltpu.VMEM((rows, width), jnp.float32),
            pltpu.VMEM((width, width), jnp.bfloat16),
            pltpu.SemaphoreType.DMA((WIN, chunks)),
            pltpu.SemaphoreType.DMA((WIN, chunks)),
        ],
        compiler_params=pltpu.CompilerParams(
            collective_id=0, has_side_effects=True, vmem_limit_bytes=56 * 1024 * 1024
        ),
    )(query, keys_values, other, stream, out_space, gain, qkv_time, out_time)


def local(
    patches,
    patch_weight,
    conv_taps,
    gain_space,
    qkv_space,
    out_space,
    gain_time,
    qkv_time,
    out_time,
):
    frames, zdev, grid, _, patch = patches.shape
    width = patch_weight.shape[1]
    tokens = zdev * grid * grid
    embed = jnp.dot(patches, patch_weight, preferred_element_type=jnp.float32).astype(
        jnp.bfloat16
    )
    if lax.axis_size("tok") == 2:
        side = lax.axis_index("tok")
        edge = lax.dynamic_slice_in_dim(embed, jnp.where(side == 0, zdev - 1, 0), 1, axis=1)
        halo = lax.ppermute(edge, "tok", [(0, 1), (1, 0)])
        empty = jnp.zeros_like(halo)
        low = jnp.where(side == 1, halo, empty)
        high = jnp.where(side == 0, halo, empty)
        padded = jnp.concatenate([low, embed, high], axis=1)
    else:
        padded = extended(embed, (("tok", 1),), 1)
    stream = depthwise(padded[0], conv_taps).reshape(frames, tokens, width)
    normed = rms_scale(stream.astype(jnp.float32), gain_space).astype(jnp.bfloat16)
    flat = normed.reshape(-1, width)
    own_kv = jnp.dot(flat, qkv_space[:, width:], preferred_element_type=jnp.float32).astype(
        jnp.bfloat16
    )
    count = lax.axis_size("tok")
    other_kv = lax.ppermute(own_kv, "tok", [(i, (i + 1) % count) for i in range(count)])
    query = jnp.dot(flat, qkv_space[:, :width], preferred_element_type=jnp.float32).astype(
        jnp.bfloat16
    )
    output = block_tail(
        query, own_kv, other_kv, stream.reshape(-1, width), out_space, gain_time, qkv_time,
        out_time,
    )
    return output.reshape(frames, zdev, grid, grid, width)


def solution(mesh):
    placed = (P("tm", "tok", None, None, None), P(), P(), P(), P(), P(), P(), P(), P())
    return jax.shard_map(
        local,
        mesh=mesh,
        in_specs=placed,
        out_specs=P("tm", "tok", None, None, None),
        check_vma=False,
    )
```

```python
import jax
import jax.numpy as jnp
from jax import lax
from jax.sharding import PartitionSpec as P
from jax.experimental import pallas as pl
from jax.experimental.pallas import tpu as pltpu
import functools

D = 512
H = 8
WIN = 4


def extended(block, sides, width):
    for axis, dim in sides:
        count = lax.axis_size(axis)
        forward = [(i, i + 1) for i in range(count - 1)]
        backward = [(target, source) for source, target in forward]
        low = lax.ppermute(
            lax.slice_in_dim(block, block.shape[dim] - width, None, axis=dim), axis, forward
        )
        high = lax.ppermute(lax.slice_in_dim(block, 0, width, axis=dim), axis, backward)
        block = jnp.concatenate([low, block, high], axis=dim)
    return block


def from_behind(value, axis, steps):
    count = lax.axis_size(axis)
    leading, last = (max(0, -steps), min(count, count - steps))
    return lax.ppermute(value, axis, [(source, source + steps) for source in range(leading, last)])


def rms_scale(values, gain):
    mean_sq = jnp.mean(values * values, axis=-1, keepdims=True)
    return values * lax.rsqrt(mean_sq + 1e-06) * gain.astype(jnp.float32)


def split_heads(block, count, head_size):
    return block.reshape(block.shape[0], count, head_size).transpose(1, 0, 2)


def attend(query, keys, values):
    rows, cols = query.shape
    head_size = D // H
    count = cols // head_size
    scale = head_size ** (-0.5)

    def one_head(parts):
        q_one, k_one, v_one = parts
        scores = jnp.dot(q_one, k_one.T, preferred_element_type=jnp.float32) * scale
        expo = jnp.exp(scores)
        mixed = jnp.dot(expo.astype(jnp.bfloat16), v_one, preferred_element_type=jnp.float32)
        return (mixed / jnp.sum(expo, axis=-1, keepdims=True)).astype(jnp.bfloat16)

    parts = (
        split_heads(query, count, head_size),
        split_heads(keys, count, head_size),
        split_heads(values, count, head_size),
    )
    result = lax.map(one_head, parts)
    return result.transpose(1, 0, 2).reshape(rows, cols)


def conv_kernel(e_ref, t_ref, o_ref):
    planes, rows, lanes_x, width = o_ref.shape

    def plane(z, carry):
        parts = []
        for dx in range(3):
            acc = None
            for dz in range(3):
                for dy in range(3):
                    tap = t_ref[pl.ds(9 * dz + 3 * dy + dx, 1), :]
                    term = e_ref[z + dz, dy:dy + rows] * tap
                    acc = term if acc is None else acc + term
            parts.append(acc)
        conv = (
            pltpu.roll(parts[0], 1, 1) + parts[1] + pltpu.roll(parts[2], lanes_x - 1, 1)
        )
        o_ref[z] = (e_ref[z + 1, 1:1 + rows] + conv).astype(o_ref.dtype)
        return carry

    lax.fori_loop(0, planes, plane, 0)


def depthwise(ext, taps):
    depth, grid, _, width = ext.shape
    planes = depth - 2
    padded = jnp.pad(ext.astype(jnp.float32), ((0, 0), (1, 1), (1, 3), (0, 0)))
    vmem = pl.BlockSpec(memory_space=pltpu.VMEM)
    out = pl.pallas_call(
        conv_kernel,
        out_shape=jax.ShapeDtypeStruct((planes, grid, grid + 4, width), jnp.bfloat16),
        in_specs=[vmem, vmem],
        out_specs=vmem,
        compiler_params=pltpu.CompilerParams(vmem_limit_bytes=32 * 1024 * 1024),
    )(padded, taps.astype(jnp.float32))
    return out[:, :, 1:1 + grid]


def block_kernel(
    chunks, q_ref, kv_ref, other_ref, stream_ref, wo_ref, gain_ref, wt_ref, wout_ref,
    out_ref, stream2_ref, own, query2, hist, mixed, total, sum_ref, send_sem, recv_sem,
):
    me = lax.axis_index("tm")
    count = lax.axis_size("tm")
    core = lax.axis_index("tok")
    has_left = me > 0
    has_right = me < count - 1
    rows_all, width = own.shape
    rows = rows_all // chunks
    head_size = width // H
    scale = head_size ** (-0.5)
    lanes = 2 * head_size
    mesh_ids = pl.DeviceIdType.MESH

    @pl.when(jnp.logical_not(has_left))
    def _():
        hist[...] = jnp.zeros_like(hist)

    barrier = pltpu.get_barrier_semaphore()

    @pl.when(has_left)
    def _():
        pl.semaphore_signal(barrier, inc=1, device_id=(me - 1, core), device_id_type=mesh_ids)

    @pl.when(has_right)
    def _():
        pl.semaphore_signal(barrier, inc=1, device_id=(me + 1, core), device_id_type=mesh_ids)

    @pl.when(jnp.logical_and(has_left, has_right))
    def _():
        pl.semaphore_wait(barrier, 2)

    @pl.when(jnp.logical_xor(has_left, has_right))
    def _():
        pl.semaphore_wait(barrier, 1)

    def span_of(piece):
        return pl.ds(pl.multiple_of(piece * rows, 8), rows)

    def copy_of(hop, piece):
        span = span_of(piece)
        source = own.at[span] if hop == 0 else hist.at[hop - 1, span]
        return pltpu.make_async_remote_copy(
            src_ref=source,
            dst_ref=hist.at[hop, span],
            send_sem=send_sem.at[hop, piece],
            recv_sem=recv_sem.at[hop, piece],
            device_id=(me + 1, core),
            device_id_type=mesh_ids,
        )

    lane = lax.broadcasted_iota(jnp.int32, (1, lanes), 1)
    first_half = lane < head_size
    heads = lax.broadcasted_iota(jnp.int32, (width, width), 0) // head_size
    same_head = heads == lax.broadcasted_iota(jnp.int32, (width, width), 1) // head_size
    sum_ref[...] = same_head.astype(jnp.bfloat16)

    def add_term(block, span, valid, first):
        kv = jnp.dot(block, wt_ref[:, width:], preferred_element_type=jnp.float32).astype(jnp.bfloat16)
        keys2 = kv[:, :width].astype(jnp.float32)
        values2 = kv[:, width:].astype(jnp.float32)
        prod = query2[span, :].astype(jnp.float32) * keys2
        high = prod.astype(jnp.bfloat16)
        low = (prod - high.astype(jnp.float32)).astype(jnp.bfloat16)
        summer = sum_ref[...]
        scores = (
            jnp.dot(high, summer, preferred_element_type=jnp.float32)
            + jnp.dot(low, summer, preferred_element_type=jnp.float32)
        ) * scale
        expo = jnp.where(valid, jnp.exp(scores), 0.0)
        part = expo.astype(jnp.bfloat16).astype(jnp.float32) * values2
        if first:
            mixed[span, :] = part
            total[span, :] = expo
        else:
            mixed[span, :] += part
            total[span, :] += expo

    def space_step(piece, carry):
        span = span_of(piece)
        pieces = []
        for pair in range(width // lanes):
            cols = slice(pair * lanes, (pair + 1) * lanes)
            q = q_ref[span, cols]
            key_cols = slice(width + pair * lanes, width + (pair + 1) * lanes)
            sources = (
                (kv_ref[:, cols], kv_ref[:, key_cols]),
                (other_ref[:, cols], other_ref[:, key_cols]),
            )
            outs = []
            for half in range(2):
                part_lanes = slice(half * head_size, (half + 1) * head_size)
                q_one = q[:, part_lanes]
                rowsum = None
                mixed_one = None
                for k, v in sources:
                    scores = lax.dot_general(
                        q_one, k[:, part_lanes], (((1,), (1,)), ((), ())),
                        preferred_element_type=jnp.float32,
                    ) * scale
                    expo = jnp.exp(scores)
                    part_sum = jnp.sum(expo, axis=-1, keepdims=True)
                    part = jnp.dot(
                        expo.astype(jnp.bfloat16), v[:, part_lanes],
                        preferred_element_type=jnp.float32,
                    )
                    rowsum = part_sum if rowsum is None else rowsum + part_sum
                    mixed_one = part if mixed_one is None else mixed_one + part
                outs.append(mixed_one / rowsum)
            pieces.append(jnp.concatenate(outs, axis=1).astype(jnp.bfloat16))
        spatial = jnp.concatenate(pieces, axis=1)
        stream2 = (
            stream_ref[span, :].astype(jnp.float32)
            + jnp.dot(spatial, wo_ref[...], preferred_element_type=jnp.float32)
        ).astype(jnp.bfloat16)
        stream2_ref[span, :] = stream2
        values = stream2.astype(jnp.float32)
        mean_sq = jnp.mean(values * values, axis=-1, keepdims=True)
        normed2 = (values * lax.rsqrt(mean_sq + 1e-06) * gain_ref[...]).astype(jnp.bfloat16)
        own[span, :] = normed2
        query2[span, :] = jnp.dot(
            normed2, wt_ref[:, :width], preferred_element_type=jnp.float32
        ).astype(jnp.bfloat16)

        add_term(own[span, :], span, True, True)

        @pl.when(has_right)
        def _():
            copy_of(0, piece).start()

        return carry

    lax.fori_loop(0, chunks, space_step, 0)

    for hop in range(WIN):
        def hop_step(piece, carry, hop=hop):
            span = span_of(piece)

            @pl.when(has_left)
            def _():
                copy_of(hop, piece).wait_recv()

            if hop + 1 < WIN:
                @pl.when(has_right)
                def _():
                    copy_of(hop + 1, piece).start()

            add_term(hist[hop, span, :], span, me - (hop + 1) >= 0, False)
            if hop + 1 == WIN:
                temporal = (mixed[span, :] / total[span, :]).astype(jnp.bfloat16)
                out_ref[span, :] = (
                    stream2_ref[span, :].astype(jnp.float32)
                    + jnp.dot(temporal, wout_ref[...], preferred_element_type=jnp.float32)
                ).astype(out_ref.dtype)
            return carry

        lax.fori_loop(0, chunks, hop_step, 0)

    @pl.when(has_right)
    def _():
        for hop in range(WIN):
            for piece in range(chunks):
                copy_of(hop, piece).wait_send()


def block_tail(
    query, keys_values, other, stream, out_space, gain_time, qkv_time, out_time, chunks=3
):
    rows, width = stream.shape
    gain = gain_time.astype(jnp.float32).reshape(1, width)
    vmem = pl.BlockSpec(memory_space=pltpu.VMEM)
    plane = jax.ShapeDtypeStruct((rows, width), jnp.bfloat16)
    return pl.pallas_call(
        functools.partial(block_kernel, chunks),
        out_shape=plane,
        in_specs=[vmem] * 8,
        out_specs=vmem,
        scratch_shapes=[
            pltpu.VMEM((rows, width), jnp.bfloat16),
            pltpu.VMEM((rows, width), jnp.bfloat16),
            pltpu.VMEM((rows, width), jnp.bfloat16),
            pltpu.VMEM((WIN, rows, width), jnp.bfloat16),
            pltpu.VMEM((rows, width), jnp.float32),
            pltpu.VMEM((rows, width), jnp.float32),
            pltpu.VMEM((width, width), jnp.bfloat16),
            pltpu.SemaphoreType.DMA((WIN, chunks)),
            pltpu.SemaphoreType.DMA((WIN, chunks)),
        ],
        compiler_params=pltpu.CompilerParams(
            collective_id=0, has_side_effects=True, vmem_limit_bytes=56 * 1024 * 1024
        ),
    )(query, keys_values, other, stream, out_space, gain, qkv_time, out_time)


def local(
    patches,
    patch_weight,
    conv_taps,
    gain_space,
    qkv_space,
    out_space,
    gain_time,
    qkv_time,
    out_time,
):
    frames, zdev, grid, _, patch = patches.shape
    width = patch_weight.shape[1]
    tokens = zdev * grid * grid
    embed = jnp.dot(patches, patch_weight, preferred_element_type=jnp.float32).astype(
        jnp.bfloat16
    )
    if lax.axis_size("tok") == 2:
        side = lax.axis_index("tok")
        edge = lax.dynamic_slice_in_dim(embed, jnp.where(side == 0, zdev - 1, 0), 1, axis=1)
        halo = lax.ppermute(edge, "tok", [(0, 1), (1, 0)])
        empty = jnp.zeros_like(halo)
        low = jnp.where(side == 1, halo, empty)
        high = jnp.where(side == 0, halo, empty)
        padded = jnp.concatenate([low, embed, high], axis=1)
    else:
        padded = extended(embed, (("tok", 1),), 1)
    stream = depthwise(padded[0], conv_taps).reshape(frames, tokens, width)
    normed = rms_scale(stream.astype(jnp.float32), gain_space).astype(jnp.bfloat16)
    flat = normed.reshape(-1, width)
    own_kv = jnp.dot(flat, qkv_space[:, width:], preferred_element_type=jnp.float32).astype(
        jnp.bfloat16
    )
    count = lax.axis_size("tok")
    other_kv = lax.ppermute(own_kv, "tok", [(i, (i + 1) % count) for i in range(count)])
    query = jnp.dot(flat, qkv_space[:, :width], preferred_element_type=jnp.float32).astype(
        jnp.bfloat16
    )
    output = block_tail(
        query, own_kv, other_kv, stream.reshape(-1, width), out_space, gain_time, qkv_time,
        out_time,
    )
    return output.reshape(frames, zdev, grid, grid, width)


def solution(mesh):
    placed = (P("tm", "tok", None, None, None), P(), P(), P(), P(), P(), P(), P(), P())
    return jax.shard_map(
        local,
        mesh=mesh,
        in_specs=placed,
        out_specs=P("tm", "tok", None, None, None),
        check_vma=False,
    )
```

```python
import jax
import jax.numpy as jnp
from jax import lax
from jax.sharding import PartitionSpec as P
from jax.experimental import pallas as pl
from jax.experimental.pallas import tpu as pltpu
import functools

D = 512
H = 8
WIN = 4


def extended(block, sides, width):
    for axis, dim in sides:
        count = lax.axis_size(axis)
        forward = [(i, i + 1) for i in range(count - 1)]
        backward = [(target, source) for source, target in forward]
        low = lax.ppermute(
            lax.slice_in_dim(block, block.shape[dim] - width, None, axis=dim), axis, forward
        )
        high = lax.ppermute(lax.slice_in_dim(block, 0, width, axis=dim), axis, backward)
        block = jnp.concatenate([low, block, high], axis=dim)
    return block


def from_behind(value, axis, steps):
    count = lax.axis_size(axis)
    leading, last = (max(0, -steps), min(count, count - steps))
    return lax.ppermute(value, axis, [(source, source + steps) for source in range(leading, last)])


def rms_scale(values, gain):
    mean_sq = jnp.mean(values * values, axis=-1, keepdims=True)
    return values * lax.rsqrt(mean_sq + 1e-06) * gain.astype(jnp.float32)


def split_heads(block, count, head_size):
    return block.reshape(block.shape[0], count, head_size).transpose(1, 0, 2)


def attend(query, keys, values):
    rows, cols = query.shape
    head_size = D // H
    count = cols // head_size
    scale = head_size ** (-0.5)

    def one_head(parts):
        q_one, k_one, v_one = parts
        scores = jnp.dot(q_one, k_one.T, preferred_element_type=jnp.float32) * scale
        expo = jnp.exp(scores)
        mixed = jnp.dot(expo.astype(jnp.bfloat16), v_one, preferred_element_type=jnp.float32)
        return (mixed / jnp.sum(expo, axis=-1, keepdims=True)).astype(jnp.bfloat16)

    parts = (
        split_heads(query, count, head_size),
        split_heads(keys, count, head_size),
        split_heads(values, count, head_size),
    )
    result = lax.map(one_head, parts)
    return result.transpose(1, 0, 2).reshape(rows, cols)


def conv_kernel(e_ref, t_ref, o_ref):
    planes, rows, lanes_x, width = o_ref.shape

    def plane(z, carry):
        parts = []
        for dx in range(3):
            acc = None
            for dz in range(3):
                for dy in range(3):
                    tap = t_ref[pl.ds(9 * dz + 3 * dy + dx, 1), :]
                    term = e_ref[z + dz, dy:dy + rows] * tap
                    acc = term if acc is None else acc + term
            parts.append(acc)
        conv = (
            pltpu.roll(parts[0], 1, 1) + parts[1] + pltpu.roll(parts[2], lanes_x - 1, 1)
        )
        o_ref[z] = (e_ref[z + 1, 1:1 + rows] + conv).astype(o_ref.dtype)
        return carry

    lax.fori_loop(0, planes, plane, 0)


def depthwise(ext, taps):
    depth, grid, _, width = ext.shape
    planes = depth - 2
    padded = jnp.pad(ext.astype(jnp.float32), ((0, 0), (1, 1), (1, 3), (0, 0)))
    vmem = pl.BlockSpec(memory_space=pltpu.VMEM)
    out = pl.pallas_call(
        conv_kernel,
        out_shape=jax.ShapeDtypeStruct((planes, grid, grid + 4, width), jnp.bfloat16),
        in_specs=[vmem, vmem],
        out_specs=vmem,
        compiler_params=pltpu.CompilerParams(vmem_limit_bytes=32 * 1024 * 1024),
    )(padded, taps.astype(jnp.float32))
    return out[:, :, 1:1 + grid]


def block_kernel(
    chunks, q_ref, kv_ref, other_ref, stream_ref, wo_ref, gain_ref, wt_ref, wout_ref,
    out_ref, stream2_ref, own, query2, hist, mixed, total, sum_ref, send_sem, recv_sem,
):
    me = lax.axis_index("tm")
    count = lax.axis_size("tm")
    core = lax.axis_index("tok")
    has_left = me > 0
    has_right = me < count - 1
    rows_all, width = own.shape
    rows = rows_all // chunks
    head_size = width // H
    scale = head_size ** (-0.5)
    lanes = 2 * head_size
    mesh_ids = pl.DeviceIdType.MESH

    @pl.when(jnp.logical_not(has_left))
    def _():
        hist[...] = jnp.zeros_like(hist)

    barrier = pltpu.get_barrier_semaphore()

    @pl.when(has_left)
    def _():
        pl.semaphore_signal(barrier, inc=1, device_id=(me - 1, core), device_id_type=mesh_ids)

    @pl.when(has_right)
    def _():
        pl.semaphore_signal(barrier, inc=1, device_id=(me + 1, core), device_id_type=mesh_ids)

    @pl.when(jnp.logical_and(has_left, has_right))
    def _():
        pl.semaphore_wait(barrier, 2)

    @pl.when(jnp.logical_xor(has_left, has_right))
    def _():
        pl.semaphore_wait(barrier, 1)

    def span_of(piece):
        return pl.ds(pl.multiple_of(piece * rows, 8), rows)

    def copy_of(hop, piece):
        span = span_of(piece)
        source = own.at[span] if hop == 0 else hist.at[hop - 1, span]
        return pltpu.make_async_remote_copy(
            src_ref=source,
            dst_ref=hist.at[hop, span],
            send_sem=send_sem.at[hop, piece],
            recv_sem=recv_sem.at[hop, piece],
            device_id=(me + 1, core),
            device_id_type=mesh_ids,
        )

    lane = lax.broadcasted_iota(jnp.int32, (1, lanes), 1)
    first_half = lane < head_size
    heads = lax.broadcasted_iota(jnp.int32, (width, width), 0) // head_size
    same_head = heads == lax.broadcasted_iota(jnp.int32, (width, width), 1) // head_size
    sum_ref[...] = same_head.astype(jnp.bfloat16)

    def add_term(block, span, valid, first):
        kv = jnp.dot(block, wt_ref[:, width:], preferred_element_type=jnp.float32).astype(jnp.bfloat16)
        keys2 = kv[:, :width].astype(jnp.float32)
        values2 = kv[:, width:].astype(jnp.float32)
        prod = query2[span, :].astype(jnp.float32) * keys2
        high = prod.astype(jnp.bfloat16)
        low = (prod - high.astype(jnp.float32)).astype(jnp.bfloat16)
        summer = sum_ref[...]
        scores = (
            jnp.dot(high, summer, preferred_element_type=jnp.float32)
            + jnp.dot(low, summer, preferred_element_type=jnp.float32)
        ) * scale
        expo = jnp.where(valid, jnp.exp(scores), 0.0)
        part = expo.astype(jnp.bfloat16).astype(jnp.float32) * values2
        if first:
            mixed[span, :] = part
            total[span, :] = expo
        else:
            mixed[span, :] += part
            total[span, :] += expo

    def space_step(piece, carry):
        span = span_of(piece)
        pieces = []
        for pair in range(width // lanes):
            cols = slice(pair * lanes, (pair + 1) * lanes)
            q = q_ref[span, cols]
            key_cols = slice(width + pair * lanes, width + (pair + 1) * lanes)
            sources = (
                (kv_ref[:, cols], kv_ref[:, key_cols]),
                (other_ref[:, cols], other_ref[:, key_cols]),
            )
            outs = []
            for mask in (first_half, jnp.logical_not(first_half)):
                q_one = jnp.where(mask, q, jnp.zeros_like(q))
                rowsum = None
                mixed_one = None
                for k, v in sources:
                    scores = lax.dot_general(
                        q_one, k, (((1,), (1,)), ((), ())), preferred_element_type=jnp.float32
                    ) * scale
                    expo = jnp.exp(scores)
                    part_sum = jnp.sum(expo, axis=-1, keepdims=True)
                    part = jnp.dot(
                        expo.astype(jnp.bfloat16), v, preferred_element_type=jnp.float32
                    )
                    rowsum = part_sum if rowsum is None else rowsum + part_sum
                    mixed_one = part if mixed_one is None else mixed_one + part
                outs.append(mixed_one / rowsum)
            pieces.append(jnp.where(first_half, outs[0], outs[1]).astype(jnp.bfloat16))
        spatial = jnp.concatenate(pieces, axis=1)
        stream2 = (
            stream_ref[span, :].astype(jnp.float32)
            + jnp.dot(spatial, wo_ref[...], preferred_element_type=jnp.float32)
        ).astype(jnp.bfloat16)
        stream2_ref[span, :] = stream2
        values = stream2.astype(jnp.float32)
        mean_sq = jnp.mean(values * values, axis=-1, keepdims=True)
        normed2 = (values * lax.rsqrt(mean_sq + 1e-06) * gain_ref[...]).astype(jnp.bfloat16)
        own[span, :] = normed2
        query2[span, :] = jnp.dot(
            normed2, wt_ref[:, :width], preferred_element_type=jnp.float32
        ).astype(jnp.bfloat16)

        add_term(own[span, :], span, True, True)

        @pl.when(has_right)
        def _():
            copy_of(0, piece).start()

        return carry

    lax.fori_loop(0, chunks, space_step, 0)

    for hop in range(WIN):
        def hop_step(piece, carry, hop=hop):
            span = span_of(piece)

            @pl.when(has_left)
            def _():
                copy_of(hop, piece).wait_recv()

            if hop + 1 < WIN:
                @pl.when(has_right)
                def _():
                    copy_of(hop + 1, piece).start()

            add_term(hist[hop, span, :], span, me - (hop + 1) >= 0, False)
            if hop + 1 == WIN:
                temporal = (mixed[span, :] / total[span, :]).astype(jnp.bfloat16)
                out_ref[span, :] = (
                    stream2_ref[span, :].astype(jnp.float32)
                    + jnp.dot(temporal, wout_ref[...], preferred_element_type=jnp.float32)
                ).astype(out_ref.dtype)
            return carry

        lax.fori_loop(0, chunks, hop_step, 0)

    @pl.when(has_right)
    def _():
        for hop in range(WIN):
            for piece in range(chunks):
                copy_of(hop, piece).wait_send()


def block_tail(
    query, keys_values, other, stream, out_space, gain_time, qkv_time, out_time, chunks=3
):
    rows, width = stream.shape
    gain = gain_time.astype(jnp.float32).reshape(1, width)
    vmem = pl.BlockSpec(memory_space=pltpu.VMEM)
    plane = jax.ShapeDtypeStruct((rows, width), jnp.bfloat16)
    return pl.pallas_call(
        functools.partial(block_kernel, chunks),
        out_shape=plane,
        in_specs=[vmem] * 8,
        out_specs=vmem,
        scratch_shapes=[
            pltpu.VMEM((rows, width), jnp.bfloat16),
            pltpu.VMEM((rows, width), jnp.bfloat16),
            pltpu.VMEM((rows, width), jnp.bfloat16),
            pltpu.VMEM((WIN, rows, width), jnp.bfloat16),
            pltpu.VMEM((rows, width), jnp.float32),
            pltpu.VMEM((rows, width), jnp.float32),
            pltpu.VMEM((width, width), jnp.bfloat16),
            pltpu.SemaphoreType.DMA((WIN, chunks)),
            pltpu.SemaphoreType.DMA((WIN, chunks)),
        ],
        compiler_params=pltpu.CompilerParams(
            collective_id=0, has_side_effects=True, vmem_limit_bytes=56 * 1024 * 1024
        ),
    )(query, keys_values, other, stream, out_space, gain, qkv_time, out_time)


def local(
    patches,
    patch_weight,
    conv_taps,
    gain_space,
    qkv_space,
    out_space,
    gain_time,
    qkv_time,
    out_time,
):
    frames, zdev, grid, _, patch = patches.shape
    width = patch_weight.shape[1]
    tokens = zdev * grid * grid
    embed = jnp.dot(patches, patch_weight, preferred_element_type=jnp.float32).astype(
        jnp.bfloat16
    )
    if lax.axis_size("tok") == 2:
        side = lax.axis_index("tok")
        edge = lax.dynamic_slice_in_dim(embed, jnp.where(side == 0, zdev - 1, 0), 1, axis=1)
        halo = lax.ppermute(edge, "tok", [(0, 1), (1, 0)])
        empty = jnp.zeros_like(halo)
        low = jnp.where(side == 1, halo, empty)
        high = jnp.where(side == 0, halo, empty)
        padded = jnp.concatenate([low, embed, high], axis=1)
    else:
        padded = extended(embed, (("tok", 1),), 1)
    stream = depthwise(padded[0], conv_taps).reshape(frames, tokens, width)
    normed = rms_scale(stream.astype(jnp.float32), gain_space).astype(jnp.bfloat16)
    flat = lax.optimization_barrier(normed.reshape(-1, width))
    own_kv = jnp.dot(flat, qkv_space[:, width:], preferred_element_type=jnp.float32).astype(
        jnp.bfloat16
    )
    count = lax.axis_size("tok")
    other_kv = lax.ppermute(own_kv, "tok", [(i, (i + 1) % count) for i in range(count)])
    query = jnp.dot(flat, qkv_space[:, :width], preferred_element_type=jnp.float32).astype(
        jnp.bfloat16
    )
    output = block_tail(
        query, own_kv, other_kv, stream.reshape(-1, width), out_space, gain_time, qkv_time,
        out_time,
    )
    return output.reshape(frames, zdev, grid, grid, width)


def solution(mesh):
    placed = (P("tm", "tok", None, None, None), P(), P(), P(), P(), P(), P(), P(), P())
    return jax.shard_map(
        local,
        mesh=mesh,
        in_specs=placed,
        out_specs=P("tm", "tok", None, None, None),
        check_vma=False,
    )
```
